32 devices in a mesh: sa: 8 (over z, x), ha: 4 (over y, core).
Axes of the slice: x: 2, y: 2, z: 4, core: 2. Of those that a mesh axis runs over, the one named last changes fastest.
Arguments:
- media_tokens: bfloat16 [32768, 1536], P(('sa', 'ha')), may hold values from -6 to 6
- latents: float32 [1024, 1536], P(('sa', 'ha')), may hold values from -6 to 6
- frame_counts: int32 [16], P('sa'), may hold values from 1 to 8, as said below
- gain_media: float32 [1536], replicated, may hold values from 0.1 to 1.9
- gain_latent: float32 [1536], replicated, may hold values from 0.1 to 1.9
- gain_ffn: float32 [1536], replicated, may hold values from 0.1 to 1.9
- qkv_weight: bfloat16 [3, 1536, 1536], P(None, None, 'ha'), may hold values from -0.15625 to 0.15625
- out_weight: bfloat16 [1536, 1536], P('ha'), may hold values from -3.5 to 3.5
- up_weight: bfloat16 [1536, 6144], P(None, 'ha'), may hold values from -0.15625 to 0.15625
- down_weight: bfloat16 [6144, 1536], P('ha'), may hold values from -0.078125 to 0.078125
- cotangent: bfloat16 [1024, 1536], P(('sa', 'ha')), may hold values from -6 to 6
Outputs:
- output: float32 [1024, 1536], P(('sa', 'ha'))
- grad_media: float32 [32768, 1536], P(('sa', 'ha'))
- grad_latents: float32 [1024, 1536], P(('sa', 'ha'))
- grad_gain_media: float32 [1536], replicated
- grad_gain_latent: float32 [1536], replicated
- grad_gain_ffn: float32 [1536], replicated
- grad_qkv: float32 [3, 1536, 1536], P(None, None, 'ha')
- grad_out_weight: float32 [1536, 1536], P('ha')
- grad_up: float32 [1536, 6144], P(None, 'ha')
- grad_down: float32 [6144, 1536], P('ha')
- rms_residual: float32 [], replicated
- rms_attention: float32 [], replicated
- rms_ffn: float32 [], replicated
The draws below stay inside these ranges and needn't reach their ends.
Inputs may be any that keep to these rules, and one draw needn't show every extreme that they name: Frames of each video that hold data; its slots from frame_counts onward are padding; in every draw some video has all 8 frames and some has one.
All inputs are finite; a program needn't handle non-finite values.
Results may differ from the reference program's by a relative error of at most 0.013.
Values may be sent and summed in bfloat16 or wider, within the bound.
A program may use at most 256 MiB of HBM per device.

```python
import jax
import jax.numpy as jnp
from jax import lax

D = 1536
HEADS = 16
HEAD = 96
FF = 6144
LAT = 64
SLOTS = 8
PATCH = 256
VIDEOS = 16
MEDIA = 32768
LATENTS = 1024


def draw_frame_counts(key, part):
    first_key = jax.random.fold_in(key, 11)
    second_key = jax.random.fold_in(key, 12)
    counts = jax.random.randint(first_key, (VIDEOS,), 1, SLOTS + 1, dtype=jnp.int32)
    ranking = jax.random.permutation(second_key, VIDEOS)
    counts = counts.at[ranking[0]].set(SLOTS)
    counts = counts.at[ranking[1]].set(1)
    return counts


def levels(key, dims, pieces, smallest, largest):
    def one(dim, blocks):
        steps = jax.random.uniform(jax.random.fold_in(jax.random.fold_in(key, 6), dim), (blocks,), jnp.float32, smallest / len(pieces), largest / len(pieces))
        return jnp.repeat(jnp.exp(steps), dims[dim] // blocks).reshape((-1,) + (1,) * (len(dims) - dim - 1))

    level = one(*pieces[0])
    for cut in pieces[1:]:
        level = level * one(*cut)
    return level


def centred(own_key, dims, deviation, most, cuts=(), held_as=jnp.bfloat16):
    gain = levels(own_key, dims, cuts, -0.22, 0.18) if cuts else 1.0
    result = jax.random.normal(own_key, dims, jnp.float32) * deviation * gain
    return jnp.minimum(jnp.maximum(result, -most), most).astype(held_as)


def setup_inputs(seed: int = 0) -> dict:
    keys = jax.random.split(jax.random.key(seed), 12)
    return {
        "media_tokens": centred(keys[0], (MEDIA, D), 1.0, 6.0, ((0, 32),)),
        "latents": centred(keys[1], (LATENTS, D), 1.0, 6.0, ((0, 32),), jnp.float32),
        "frame_counts": draw_frame_counts(jax.random.fold_in(keys[11], 71), 0),
        "gain_media": jnp.clip(1.0 + 0.18 * jax.random.normal(keys[3], (D,), jnp.float32), 0.1, 1.9),
        "gain_latent": jnp.clip(1.0 + 0.18 * jax.random.normal(keys[4], (D,), jnp.float32), 0.1, 1.9),
        "gain_ffn": jnp.clip(1.0 + 0.18 * jax.random.normal(keys[5], (D,), jnp.float32), 0.1, 1.9),
        "qkv_weight": centred(keys[6], (3, D, D), D ** -0.5, 0.15625, ((2, 4),)),
        "out_weight": centred(keys[7], (D, D), (max(D // 512, 1)) ** -0.5, 3.5, ((0, 4),)),
        "up_weight": centred(keys[8], (D, FF), D ** -0.5, 0.15625, ((1, 4),)),
        "down_weight": centred(keys[9], (FF, D), FF ** -0.5, 0.078125, ((0, 4),)),
        "cotangent": centred(keys[10], (LATENTS, D), 1.0, 6.0, ((0, 32),)),
    }


@jax.custom_vjp
def low(v):
    return lax.optimization_barrier(v.astype(jnp.bfloat16)).astype(jnp.float32)

@jax.custom_vjp
def low_back(v):
    return v

def low_keep(v):
    return (low(v), None)

def low_pass(kept, grad):
    return (grad,)

def back_keep(v):
    return (v, None)

def back_low(kept, grad):
    return (low(grad),)
low.defvjp(low_keep, low_pass)
low_back.defvjp(back_keep, back_low)
epsilon = 1e-05
negative = -1000000000.0
highest = lax.Precision.HIGHEST

def normalize(values):
    centered = values - lax.optimization_barrier(jnp.mean(values, axis=-1, keepdims=True))
    return centered * lax.rsqrt(lax.optimization_barrier(jnp.mean(centered * centered, axis=-1, keepdims=True)) + epsilon)

def matmul(left, right):
    return jnp.dot(left, right, precision=highest, preferred_element_type=jnp.float32)

def attend(packed):
    queries, key_media, value_media, key_latent, value_latent, frames_valid = packed
    key_rows = SLOTS * PATCH + LAT
    key_all = jnp.concatenate([key_media, key_latent], axis=0).reshape(key_rows, HEADS, HEAD)
    value_all = jnp.concatenate([value_media, value_latent], axis=0).reshape(key_rows, HEADS, HEAD)
    scores = jnp.einsum('qhe,khe->hqk', queries.reshape(LAT, HEADS, HEAD), key_all, precision=highest) * HEAD ** (-0.5)
    scores = low_back(scores)
    position = jnp.arange(key_rows, dtype=jnp.int32) // PATCH
    usable = jnp.logical_or(position < frames_valid, position >= SLOTS)
    scores = jnp.where(usable[None, None, :], scores, negative)
    weights = low(jax.nn.softmax(scores, axis=-1))
    mixture = jnp.einsum('hqk,khe->qhe', weights, value_all, precision=highest)
    return mixture.reshape(LAT, D)

def forward(frame_counts, media_tokens, latents, gain_media, gain_latent, gain_ffn, qkv_weight, out_weight, up_weight, down_weight):
    media_hat = low(normalize(media_tokens) * gain_media)
    latent_hat = low(normalize(latents) * gain_latent)
    queries = low_back(low(matmul(latent_hat, qkv_weight[0])))
    key_media = low_back(low(matmul(media_hat, qkv_weight[1])))
    value_media = low_back(low(matmul(media_hat, qkv_weight[2])))
    key_latent = low_back(low(matmul(latent_hat, qkv_weight[1])))
    value_latent = low_back(low(matmul(latent_hat, qkv_weight[2])))
    video_rows = SLOTS * PATCH
    packed = (queries.reshape(VIDEOS, LAT, D), key_media.reshape(VIDEOS, video_rows, D), value_media.reshape(VIDEOS, video_rows, D), key_latent.reshape(VIDEOS, LAT, D), value_latent.reshape(VIDEOS, LAT, D), frame_counts)
    mixture = lax.map(jax.checkpoint(attend), packed).reshape(VIDEOS * LAT, D)
    attended = low_back(low(mixture))
    attn_branch = low_back(matmul(attended, out_weight))
    residual = latents + attn_branch
    mid_hat = low(normalize(residual) * gain_ffn)
    pre_act = low_back(matmul(mid_hat, up_weight))
    hidden = low(jax.nn.gelu(pre_act, approximate=False))
    ffn_branch = low_back(matmul(hidden, down_weight))
    return (residual + ffn_branch, (residual, attn_branch, ffn_branch))

def reference(media_tokens, latents, frame_counts, gain_media, gain_latent, gain_ffn, qkv_weight, out_weight, up_weight, down_weight, cotangent):

    def bound(media_wide, latent_rows, gain_one, gain_two, gain_three, qkv_wide, out_wide, up_wide, down_wide):
        return forward(frame_counts, media_wide, latent_rows, gain_one, gain_two, gain_three, qkv_wide, out_wide, up_wide, down_wide)
    output, pullback, extras = jax.vjp(bound, media_tokens.astype(jnp.float32), latents, gain_media, gain_latent, gain_ffn, qkv_weight.astype(jnp.float32), out_weight.astype(jnp.float32), up_weight.astype(jnp.float32), down_weight.astype(jnp.float32), has_aux=True)
    grads = pullback(cotangent.astype(jnp.float32))
    residual, attn_branch, ffn_branch = extras
    rms_residual = jnp.sqrt(jnp.mean(residual * residual))
    rms_attention = jnp.sqrt(jnp.mean(attn_branch * attn_branch))
    rms_ffn = jnp.sqrt(jnp.mean(ffn_branch * ffn_branch))
    return (output, grads[0], grads[1], grads[2], grads[3], grads[4], grads[5], grads[6], grads[7], grads[8], rms_residual, rms_attention, rms_ffn)
```

```python
import jax
import jax.numpy as jnp
from jax import lax
from jax.sharding import PartitionSpec as P

HEAD = 96
PATCH = 256
EPS = 1e-05
NEG = -1000000000.0
F32 = jnp.float32
BF16 = jnp.bfloat16


def normalize(values):
    centered = values - jnp.mean(values, axis=-1, keepdims=True)
    inverse = lax.rsqrt(jnp.mean(centered * centered, axis=-1, keepdims=True) + EPS)
    return centered * inverse, inverse


def norm_grad(grad, normed, inverse):
    first = jnp.mean(grad, axis=-1, keepdims=True)
    second = jnp.mean(grad * normed, axis=-1, keepdims=True)
    return inverse * (grad - first - normed * second)


def gelu_exact(values):
    return jax.nn.gelu(values, approximate=False)


def swap_core(x, group):
    return lax.ppermute(x, "ha", [(i, i ^ 1) for i in range(group)])


def dot(spec, a, b):
    return jnp.einsum(spec, a, b, preferred_element_type=F32)


def shards(
    media_tokens,
    latents,
    frame_counts,
    gain_media,
    gain_latent,
    gain_ffn,
    qkv_weight,
    out_weight,
    up_weight,
    down_weight,
    cotangent,
):
    group = lax.axis_size("ha")
    media_rows = media_tokens.shape[0]
    lat = latents.shape[0]
    width = media_tokens.shape[1]
    cols = qkv_weight.shape[2]
    heads = cols // HEAD
    place = lax.axis_index("ha")
    core = place % 2
    count = frame_counts[place // 2]
    scale = HEAD ** (-0.5)
    entry_total = float(lat * width * lax.axis_size("sa") * group)
    both = ("sa", "ha")

    media_norm, media_inv = normalize(media_tokens.astype(F32))
    latent_norm, latent_inv = normalize(latents)
    latent_hat = (latent_norm * gain_latent).astype(BF16)
    hat = jnp.concatenate([(media_norm * gain_media).astype(BF16), latent_hat], axis=0)

    w_all = lax.all_gather(qkv_weight, "ha", axis=0)
    o_all = lax.all_gather(out_weight, "ha", axis=0)
    cot_all = lax.all_gather(cotangent, both, axis=0, tiled=True)
    lat_all = lax.all_gather(latent_hat, both, axis=0, tiled=True)
    keys = dot("rd,ade->are", hat, w_all[:, 1]).astype(BF16)
    values = dot("rd,ade->are", hat, w_all[:, 2]).astype(BF16)
    q_own = dot("rd,ade->are", latent_hat, w_all[:, 0]).astype(BF16)

    def pair_rows(x):
        other = swap_core(x, group)
        return jnp.where(
            core == 0, jnp.concatenate([x, other], axis=1), jnp.concatenate([other, x], axis=1)
        )

    col_head = jnp.arange(cols, dtype=jnp.int32) // HEAD

    def spread(x):
        picked = [jnp.where(col_head == h, x, jnp.zeros_like(x)) for h in range(heads)]
        return jnp.concatenate(picked, axis=1)

    def gather_heads(x):
        parts = x.reshape(x.shape[0], heads, 2 * lat, cols)
        return sum(jnp.where(col_head == h, parts[:, h], 0.0) for h in range(heads))

    def own_half(x):
        mine = lax.dynamic_slice_in_dim(x, core * lat, lat, 1)
        theirs = lax.dynamic_slice_in_dim(x, (1 - core) * lat, lat, 1)
        return mine + swap_core(theirs, group)

    q_blk = spread(pair_rows(q_own))
    row = jnp.arange(media_rows + lat, dtype=jnp.int32)
    usable = jnp.logical_or((core * media_rows + row) // PATCH < count, row >= media_rows)
    scores = jnp.where(usable, dot("aqe,ake->aqk", q_blk, keys) * scale, NEG)
    top = jnp.max(scores, axis=-1, keepdims=True)
    probs = jnp.exp(scores - top)
    total = jnp.sum(probs, axis=-1, keepdims=True)
    stats = jnp.concatenate([top, total], axis=-1)
    stats_other = swap_core(stats, group)
    top_all = jnp.maximum(top, stats_other[..., :1])
    denom = total * jnp.exp(top - top_all) + stats_other[..., 1:] * jnp.exp(
        stats_other[..., :1] - top_all
    )
    probs = (probs * (jnp.exp(top - top_all) / denom)).astype(BF16)
    attended32 = own_half(gather_heads(dot("aqk,ake->aqe", probs, values)))
    attended = attended32.astype(BF16)
    attn_branch = dot("are,aed->rd", attended, o_all)
    residual = latents + attn_branch
    mid_norm, mid_inv = normalize(residual)
    mid_hat = (mid_norm * gain_ffn).astype(BF16)
    mid_ha = lax.all_gather(mid_hat, "ha", axis=0, tiled=True)
    cot_ha = lax.all_gather(cotangent, "ha", axis=0, tiled=True)
    pre_act = jnp.dot(mid_ha, up_weight, preferred_element_type=F32)
    hidden = gelu_exact(pre_act).astype(BF16)
    ffn_branch = lax.psum_scatter(
        jnp.dot(hidden, down_weight, preferred_element_type=F32).astype(BF16),
        "ha",
        scatter_dimension=0,
        tiled=True,
    ).astype(F32)
    output = residual + ffn_branch
    grad_hidden = dot("rd,fd->rf", cot_ha, down_weight)
    unused_value, gelu_back = jax.vjp(gelu_exact, pre_act)
    grad_pre = gelu_back(grad_hidden)[0].astype(BF16)
    grad_mid = lax.psum_scatter(
        dot("rf,df->rd", grad_pre, up_weight).astype(BF16),
        "ha",
        scatter_dimension=0,
        tiled=True,
    ).astype(F32)
    gain_ffn_part = jnp.sum(grad_mid * mid_norm, axis=0)
    grad_residual = cotangent.astype(F32) + norm_grad(grad_mid * gain_ffn, mid_norm, mid_inv)
    grad_branch = grad_residual.astype(BF16)
    grad_att = dot("rd,aed->are", grad_branch, o_all).astype(BF16)
    inner = attended32 * grad_att.astype(F32)
    inner = jnp.stack(
        [jnp.sum(jnp.where(col_head == h, inner, 0.0), axis=-1) for h in range(heads)], axis=-1
    )
    g_blk = spread(pair_rows(grad_att))
    inner = jnp.moveaxis(pair_rows(inner), 2, 1).reshape(group, heads * 2 * lat, 1)
    grad_probs = dot("aqe,ake->aqk", g_blk, values)
    grad_scores = (probs.astype(F32) * (grad_probs - inner)).astype(BF16)
    grad_values = dot("aqk,aqe->ake", probs, g_blk).astype(BF16)
    grad_keys = (dot("aqk,aqe->ake", grad_scores, q_blk) * scale).astype(BF16)
    grad_q = own_half(gather_heads(dot("aqk,ake->aqe", grad_scores, keys)) * scale).astype(BF16)

    grad_kv = jnp.stack(
        [dot("rd,are->ade", hat, grad_keys), dot("rd,are->ade", hat, grad_values)], axis=1
    ).astype(BF16)
    grad_kv = lax.psum_scatter(grad_kv, "ha", scatter_dimension=0)
    grad_kv = lax.psum(grad_kv, "sa").astype(F32)
    grad_hat = dot("are,ade->rd", grad_keys, w_all[:, 1]) + dot(
        "are,ade->rd", grad_values, w_all[:, 2]
    )
    grad_media_hat = grad_hat[:media_rows]
    grad_latent_hat = grad_hat[media_rows:] + dot("are,ade->rd", grad_q, w_all[:, 0])
    gain_media_part = jnp.sum(grad_media_hat * media_norm, axis=0)
    gain_latent_part = jnp.sum(grad_latent_hat * latent_norm, axis=0)
    grad_media = norm_grad(grad_media_hat * gain_media, media_norm, media_inv)
    grad_latents = grad_residual + norm_grad(grad_latent_hat * gain_latent, latent_norm, latent_inv)

    mid_all = lax.all_gather(mid_hat, both, axis=0, tiled=True)
    branch_all = lax.all_gather(grad_branch, both, axis=0, tiled=True)
    att_q = jnp.concatenate([attended, grad_q], axis=2)
    att_q = lax.all_to_all(att_q, "ha", split_axis=0, concat_axis=1, tiled=True)[0]
    att_q = lax.all_gather(att_q, "sa", axis=0, tiled=True)
    grad_out = dot("rc,rd->cd", att_q[:, :cols], branch_all)
    grad_wq = dot("rd,re->de", lat_all, att_q[:, cols:])
    pre_all = jnp.dot(mid_all, up_weight, preferred_element_type=F32)
    hidden_all, gelu_back_all = jax.vjp(gelu_exact, pre_all)
    grad_pre_all = gelu_back_all(dot("rd,fd->rf", cot_all, down_weight))[0].astype(BF16)
    grad_down = dot("rf,rd->fd", hidden_all.astype(BF16), cot_all)
    grad_up = dot("rd,rf->df", mid_all, grad_pre_all)

    square_parts = jnp.stack(
        [
            jnp.sum(residual * residual),
            jnp.sum(attn_branch * attn_branch),
            jnp.sum(ffn_branch * ffn_branch),
        ]
    )
    gain_one, gain_two, gain_three, square_sums = lax.psum(
        (gain_media_part, gain_latent_part, gain_ffn_part, square_parts), both
    )
    roots = jnp.sqrt(square_sums / entry_total)
    return (
        output,
        grad_media,
        grad_latents,
        gain_one,
        gain_two,
        gain_three,
        jnp.concatenate([grad_wq[None], grad_kv], axis=0),
        grad_out,
        grad_up,
        grad_down,
        roots[0],
        roots[1],
        roots[2],
    )


def solution(mesh):
    placed = (
        P(("sa", "ha"), None),
        P(("sa", "ha"), None),
        P("sa"),
        P(),
        P(),
        P(),
        P(None, None, "ha"),
        P("ha", None),
        P(None, "ha"),
        P("ha", None),
        P(("sa", "ha"), None),
    )
    return jax.shard_map(
        shards,
        mesh=mesh,
        in_specs=placed,
        out_specs=(
            P(("sa", "ha"), None),
            P(("sa", "ha"), None),
            P(("sa", "ha"), None),
            P(),
            P(),
            P(),
            P(None, None, "ha"),
            P("ha", None),
            P(None, "ha"),
            P("ha", None),
            P(),
            P(),
            P(),
        ),
        check_vma=False,
    )
```

```python
import functools

import jax
import jax.numpy as jnp
from jax import lax
from jax.experimental import pallas as pl
from jax.experimental.pallas import tpu as pltpu
from jax.sharding import PartitionSpec as P

HEAD = 96
PATCH = 256
EPS = 1e-05
NEG = -1000000000.0
F32 = jnp.float32
BF16 = jnp.bfloat16


def normalize(values):
    centered = values - jnp.mean(values, axis=-1, keepdims=True)
    inverse = lax.rsqrt(jnp.mean(centered * centered, axis=-1, keepdims=True) + EPS)
    return centered * inverse, inverse


def norm_grad(grad, normed, inverse):
    first = jnp.mean(grad, axis=-1, keepdims=True)
    second = jnp.mean(grad * normed, axis=-1, keepdims=True)
    return inverse * (grad - first - normed * second)


def gelu_exact(values):
    return jax.nn.gelu(values, approximate=False)


def swap_core(x, group):
    return lax.ppermute(x, "ha", [(i, i ^ 1) for i in range(group)])


def dot(spec, a, b):
    return jnp.einsum(spec, a, b, preferred_element_type=F32)


MESH = pl.DeviceIdType.MESH
NZ = 4
CHUNKS = 6


def dg(a, b, ca, cb):
    return lax.dot_general(a, b, (((ca,), (cb,)), ((), ())), preferred_element_type=F32)


class Where:
    def __init__(self, nx, ny):
        self.nx, self.ny = nx, ny
        sa, ha = lax.axis_index("sa"), lax.axis_index("ha")
        self.own = {"z": sa // nx, "x": sa % nx, "y": ha // 2, "c": ha % 2}
        self.size = {"z": NZ, "x": nx, "y": ny, "c": 2}

    def at(self, axis, k):
        return lax.rem(self.own[axis] + k, self.size[axis])

    def device(self, axis, k):
        p = dict(self.own)
        p[axis] = self.at(axis, k)
        return {"sa": p["z"] * self.nx + p["x"], "ha": p["y"] * 2 + p["c"]}


def greet(me):
    barrier = pltpu.get_barrier_semaphore()
    count = 0
    for axis in "cyxz":
        for k in range(1, me.size[axis]):
            pl.semaphore_signal(
                barrier, inc=1, device_id=me.device(axis, k), device_id_type=MESH
            )
            count += 1
    pl.semaphore_wait(barrier, count)


class Gather:
    def __init__(self, me, own, buf, order, send, recv, local, done=""):
        self.me, self.own, self.buf, self.order = me, own, buf, order
        self.send, self.recv, self.local = send, recv, local
        self.done = done

    def slot(self, done):
        me = self.me
        return tuple(
            pl.ds(0, me.size[a]) if a in done else me.own[a] for a in "zxyc"
        )

    def keep(self):
        return pltpu.make_async_copy(
            self.own, self.buf.at[self.slot(self.done)], self.local
        )

    def copies(self, phase):
        done = self.done + self.order[:phase]
        axis = self.order[phase]
        first = sum(self.me.size[a] - 1 for a in self.order[:phase])
        here = self.buf.at[self.slot(done)]
        src = self.own if phase == 0 and self.own is not None else here
        return [
            pltpu.make_async_remote_copy(
                src_ref=src,
                dst_ref=here,
                send_sem=self.send.at[first + k - 1],
                recv_sem=self.recv.at[first + k - 1],
                device_id=self.me.device(axis, k),
                device_id_type=MESH,
            )
            for k in range(1, self.me.size[axis])
        ]

    def start(self, phase):
        if phase == 0 and self.own is not None:
            self.keep().start()
        for c in self.copies(phase):
            c.start()

    def finish(self, phase):
        if phase == 0 and self.own is not None:
            self.keep().wait()
        for c in self.copies(phase):
            c.wait_recv()

    def next(self, phase):
        self.finish(phase)
        self.start(phase + 1)

    def drain(self):
        for phase in range(len(self.order)):
            for c in self.copies(phase):
                c.wait_send()


def tail_kernel(
    nx,
    ny,
    hat_h,
    gkv_h,
    wkv_h,
    up_h,
    down_h,
    media_h,
    cot_all,
    gain_r,
    part_r,
    mid_r,
    branch_r,
    attq_r,
    kv_o,
    gm_o,
    hid_o,
    gp_o,
    mid_all,
    branch_all,
    attq_all,
    gains_o,
    hat,
    gkv,
    wkv,
    up,
    down,
    send_c,
    recv_c,
    acc,
    send_y,
    recv_y,
    send_x,
    recv_x,
    send_z,
    recv_z,
    red,
    attq_y,
    media_t,
    gm_t,
    mid_t,
    cot_t,
    hid_t,
    gp_t,
    gbuf,
    grecv,
    load_sem,
    tile_sem,
    out_sem,
    c_send,
    c_recv,
    y_send,
    y_recv,
    x_send,
    x_recv,
    z_send,
    z_recv,
    za_send,
    za_recv,
    xa_send,
    xa_recv,
    keep_sem,
    g_send,
    g_recv,
    mid_send,
    mid_recv,
    br_send,
    br_recv,
    aq_send,
    aq_recv,
    own_sem,
):
    me = Where(nx, ny)
    z, x, y, c = (me.own[a] for a in "zxyc")
    T = CHUNKS
    pieces = 2 * ny
    chunk = acc.shape[1]
    quarter = send_x.shape[2]
    sub = red.shape[1]
    feat = hat.shape[1]

    def load(i, src, dst):
        return pltpu.make_async_copy(src, dst, load_sem.at[i])

    hat_copy = load(0, hat_h, hat)
    gkv_copy = load(1, gkv_h, gkv)
    wkv_copy = load(2, wkv_h, wkv)
    up_copy = load(3, up_h, up)
    down_copy = load(4, down_h, down)
    for copy in (hat_copy, gkv_copy, wkv_copy, up_copy, down_copy):
        copy.start()
    greet(me)

    mid = Gather(me, mid_r, mid_all, "yzxc", mid_send, mid_recv, own_sem.at[0])
    branch = Gather(me, branch_r, branch_all, "zxyc", br_send, br_recv, own_sem.at[1])

    def attq_y_copies():
        return [
            pltpu.make_async_remote_copy(
                src_ref=attq_r.at[pl.ds(2 * me.at("y", k), 2)],
                dst_ref=attq_y.at[y],
                send_sem=aq_send.at[k - 1],
                recv_sem=aq_recv.at[k - 1],
                device_id=me.device("y", k),
                device_id_type=MESH,
            )
            for k in range(1, ny)
        ]

    attq_own = pltpu.make_async_copy(
        attq_r.at[pl.ds(2 * y, 2)], attq_y.at[y], own_sem.at[2]
    )
    attq_c = pltpu.make_async_remote_copy(
        src_ref=attq_y.at[pl.ds(0, ny), 1 - c],
        dst_ref=attq_all.at[z, x, pl.ds(0, ny), c],
        send_sem=aq_send.at[ny - 1],
        recv_sem=aq_recv.at[ny - 1],
        device_id=me.device("c", 1),
        device_id_type=MESH,
    )
    attq_keep = pltpu.make_async_copy(
        attq_y.at[pl.ds(0, ny), c], attq_all.at[z, x, pl.ds(0, ny), c], own_sem.at[3]
    )
    attq = Gather(
        me,
        None,
        attq_all,
        "zx",
        aq_send.at[pl.ds(ny, NZ + nx - 2)],
        aq_recv.at[pl.ds(ny, NZ + nx - 2)],
        None,
        "yc",
    )

    mid.start(0)
    attq_own.start()
    for copy in attq_y_copies():
        copy.start()
    branch.start(0)

    def grad_rows(k, t, parity):
        piece = 2 * me.at("y", k) + parity
        left = hat[:, pl.ds(pl.multiple_of(t * chunk, 128), chunk)]
        return dg(left, gkv[piece], 0, 0)

    def core_copy(t):
        return pltpu.make_async_remote_copy(
            src_ref=send_c.at[t],
            dst_ref=recv_c.at[t],
            send_sem=c_send.at[t],
            recv_sem=c_recv.at[t],
            device_id=me.device("c", 1),
            device_id_type=MESH,
        )

    def y_copy(k, t):
        return pltpu.make_async_remote_copy(
            src_ref=send_y.at[k - 1, t],
            dst_ref=recv_y.at[k - 1, t],
            send_sem=y_send.at[k - 1, t],
            recv_sem=y_recv.at[k - 1, t],
            device_id=me.device("y", k),
            device_id_type=MESH,
        )

    def x_copy(k, t):
        return pltpu.make_async_remote_copy(
            src_ref=send_x.at[k - 1, t],
            dst_ref=recv_x.at[k - 1, t],
            send_sem=x_send.at[k - 1, t],
            recv_sem=x_recv.at[k - 1, t],
            device_id=me.device("x", k),
            device_id_type=MESH,
        )

    def z_copy(k, t):
        return pltpu.make_async_remote_copy(
            src_ref=send_z.at[k - 1, t],
            dst_ref=recv_z.at[k - 1, t],
            send_sem=z_send.at[k - 1, t],
            recv_sem=z_recv.at[k - 1, t],
            device_id=me.device("z", k),
            device_id_type=MESH,
        )

    def za_copy(k, t):
        return pltpu.make_async_remote_copy(
            src_ref=red.at[t],
            dst_ref=kv_o.at[t, x * NZ + z],
            send_sem=za_send.at[k - 1, t],
            recv_sem=za_recv.at[k - 1, t],
            device_id=me.device("z", k),
            device_id_type=MESH,
        )

    def xa_copy(k, t):
        rows = kv_o.at[t, pl.ds(x * NZ, NZ)]
        return pltpu.make_async_remote_copy(
            src_ref=rows,
            dst_ref=rows,
            send_sem=xa_send.at[k - 1, t],
            recv_sem=xa_recv.at[k - 1, t],
            device_id=me.device("x", k),
            device_id_type=MESH,
        )

    def keep_copy(t):
        return pltpu.make_async_copy(red.at[t], kv_o.at[t, x * NZ + z], keep_sem.at[t])

    hat_copy.wait()
    gkv_copy.wait()
    lag = 2
    steps = ny * T

    @pl.loop(0, steps + lag)
    def _(j):
        @pl.when(j < steps)
        def _():
            k, t = lax.rem(1 + j // T, ny), lax.rem(j, T)

            @pl.when(j >= T)
            def _():
                core_copy(t).wait_send()

            send_c[t] = grad_rows(k, t, 1 - c).astype(BF16)
            core_copy(t).start()

        @pl.when(j >= lag)
        def _():
            i = j - lag
            k, t = lax.rem(1 + i // T, ny), lax.rem(i, T)
            mine = grad_rows(k, t, c)
            core_copy(t).wait_recv()
            mine = mine + recv_c[t].astype(F32)

            @pl.when(i >= steps - T)
            def _():
                acc[t] = mine

            @pl.when(i < steps - T)
            def _():
                for step in range(1, ny):

                    @pl.when(i // T == step - 1)
                    def _():
                        send_y[step - 1, t] = mine.astype(BF16)
                        y_copy(step, t).start()

        @pl.when(j == 3)
        def _():
            mid.next(0)
            attq_own.wait()
            for copy in attq_y_copies():
                copy.wait_recv()
            attq_c.start()
            attq_keep.start()

        @pl.when(j == 9)
        def _():
            attq_keep.wait()
            attq_c.wait_recv()
            attq.start(0)

    for t in range(T):
        core_copy(t).wait_send()
    wkv_copy.wait()
    up_copy.wait()
    down_copy.wait()

    gbuf[...] = part_r[...]
    media_rows = media_h.shape[0]
    tile = media_t.shape[1]
    n_media = media_rows // tile

    def media_load(u):
        return pltpu.make_async_copy(
            media_h.at[pl.ds(pl.multiple_of(u * tile, tile), tile)],
            media_t.at[lax.rem(u, 2)],
            tile_sem.at[lax.rem(u, 2)],
        )

    def gm_store(u):
        return pltpu.make_async_copy(
            gm_t, gm_o.at[pl.ds(pl.multiple_of(u * tile, tile), tile)], out_sem.at[0]
        )

    def media_tile(u):
        @pl.when(u + 1 < n_media)
        def _():
            media_load(u + 1).start()

        rows = pl.ds(pl.multiple_of(u * tile, tile), tile)
        total = dg(gkv[0, rows], wkv[0], 1, 1)
        for a in range(1, pieces):
            total = total + dg(gkv[a, rows], wkv[a], 1, 1)
        media_load(u).wait()
        values = media_t[lax.rem(u, 2)].astype(F32)
        normed, inverse = normalize(values)
        gbuf[0:1] = gbuf[0:1] + jnp.sum(total * normed, axis=0, keepdims=True)
        result = norm_grad(total * gain_r[...], normed, inverse)

        @pl.when(u >= 1)
        def _():
            gm_store(u - 1).wait()

        gm_t[...] = result.astype(BF16)
        gm_store(u).start()

    xt = mid_t.shape[1]
    n_ffn = NZ * (nx // xt)

    def rows_load(u):
        zz, xx = u // (nx // xt), lax.rem(u, nx // xt) * xt
        b = lax.rem(u, 2)
        return [
            pltpu.make_async_copy(
                mid_all.at[zz, pl.ds(xx, xt)], mid_t.at[b], tile_sem.at[2 + b]
            ),
            pltpu.make_async_copy(
                cot_all.at[zz, pl.ds(xx, xt)], cot_t.at[b], tile_sem.at[4 + b]
            ),
        ]

    def ffn_store(u):
        return [
            pltpu.make_async_copy(hid_t, hid_o.at[u], out_sem.at[1]),
            pltpu.make_async_copy(gp_t, gp_o.at[u], out_sem.at[2]),
        ]

    def ffn_tile(u):
        @pl.when(u + 1 < n_ffn)
        def _():
            for copy in rows_load(u + 1):
                copy.start()

        for copy in rows_load(u):
            copy.wait()

        @pl.when(u >= 1)
        def _():
            for copy in ffn_store(u - 1):
                copy.wait()

        b = lax.rem(u, 2)
        mid_rows = mid_t[b].reshape(-1, feat)
        cot_rows = cot_t[b].reshape(-1, feat)
        width = up.shape[1] // 3
        for part in range(3):
            cols = pl.ds(part * width, width)
            pre = dg(mid_rows, up[:, cols], 1, 0)
            grad = dg(cot_rows, down[cols, :], 1, 1)
            cdf = 0.5 * (1.0 + lax.erf(pre * (0.5**0.5)))
            slope = cdf + pre * (jnp.exp(-0.5 * pre * pre) * 0.3989422804014327)
            hid_t[:, cols] = (pre * cdf).astype(BF16)
            gp_t[:, cols] = (grad * slope).astype(BF16)
        for copy in ffn_store(u):
            copy.start()

    def comm(i):
        @pl.when(i < T)
        def _():
            t = i
            for k in range(1, ny):
                y_copy(k, t).wait_recv()
            whole = acc[t]
            for k in range(1, ny):
                whole = whole + recv_y[k - 1, t].astype(F32)
            acc[t] = whole
            for k in range(1, nx):
                there = pl.ds(pl.multiple_of(me.at("x", k) * quarter, 8), quarter)
                send_x[k - 1, t] = acc[t, there].astype(BF16)
                x_copy(k, t).start()

        @pl.when(jnp.logical_and(i >= 1, i < T + 1))
        def _():
            t = i - 1
            for k in range(1, nx):
                x_copy(k, t).wait_recv()
            here = pl.ds(pl.multiple_of(x * quarter, 8), quarter)
            whole = acc[t, here]
            for k in range(1, nx):
                whole = whole + recv_x[k - 1, t].astype(F32)
            acc[t, here] = whole
            for k in range(1, NZ):
                there = pl.ds(
                    pl.multiple_of(x * quarter + me.at("z", k) * sub, 8), sub
                )
                send_z[k - 1, t] = acc[t, there].astype(BF16)
                z_copy(k, t).start()

        @pl.when(jnp.logical_and(i >= 2, i < T + 2))
        def _():
            t = i - 2
            for k in range(1, NZ):
                z_copy(k, t).wait_recv()
            whole = acc[t, pl.ds(pl.multiple_of(x * quarter + z * sub, 8), sub)]
            for k in range(1, NZ):
                whole = whole + recv_z[k - 1, t].astype(F32)
            red[t] = whole.astype(BF16)
            keep_copy(t).start()
            for k in range(1, NZ):
                za_copy(k, t).start()

        @pl.when(jnp.logical_and(i >= 3, i < T + 3))
        def _():
            t = i - 3
            keep_copy(t).wait()
            for k in range(1, NZ):
                za_copy(k, t).wait_recv()
            for k in range(1, nx):
                xa_copy(k, t).start()

        @pl.when(i >= 4)
        def _():
            t = i - 4
            for k in range(1, nx):
                xa_copy(k, t).wait_recv()

    def gain_copies(axis, base):
        return [
            pltpu.make_async_remote_copy(
                src_ref=gbuf,
                dst_ref=grecv.at[base + k - 1],
                send_sem=g_send.at[base + k - 1],
                recv_sem=g_recv.at[base + k - 1],
                device_id=me.device(axis, k),
                device_id_type=MESH,
            )
            for k in range(1, me.size[axis])
        ]

    def gain_base(axis):
        return sum(me.size[a] - 1 for a in "cyxz"[: "cyxz".index(axis)])

    def gain_start(axis):
        for copy in gain_copies(axis, gain_base(axis)):
            copy.start()

    def gain_finish(axis):
        base = gain_base(axis)
        for copy in gain_copies(axis, base):
            copy.wait_send()
            copy.wait_recv()
        total = gbuf[...]
        for k in range(1, me.size[axis]):
            total = total + grecv[base + k - 1]
        gbuf[...] = total

    media_load(0).start()

    @pl.loop(0, T + 4)
    def _(i):
        comm(i)

        @pl.when(i == 0)
        def _():
            mid.next(1)

        @pl.when(i == 1)
        def _():
            branch.next(0)

        @pl.when(i < 2)
        def _():
            @pl.loop(0, n_media // 2)
            def _(u):
                media_tile(i * (n_media // 2) + u)

        @pl.when(i == 2)
        def _():
            gm_store(n_media - 1).wait()
            gain_start("c")
            mid.next(2)
            mid.finish(3)
            for copy in rows_load(0):
                copy.start()

        @pl.when(i == 3)
        def _():
            gain_finish("c")
            gain_start("y")
            attq.next(0)

        @pl.when(jnp.logical_and(i >= 2, i < 4))
        def _():
            @pl.loop(0, n_ffn // 2)
            def _(u):
                ffn_tile((i - 2) * (n_ffn // 2) + u)

        @pl.when(i == 4)
        def _():
            for copy in ffn_store(n_ffn - 1):
                copy.wait()
            gain_finish("y")
            gain_start("x")
            branch.next(1)

        @pl.when(i == 5)
        def _():
            gain_finish("x")
            gain_start("z")

        @pl.when(i == 7)
        def _():
            branch.next(2)

    gain_finish("z")
    gains_o[...] = gbuf[...]
    branch.finish(3)
    attq.finish(1)
    mid.drain()
    branch.drain()
    for copy in attq_y_copies():
        copy.wait_send()
    attq_c.wait_send()
    attq.drain()

    @pl.loop(0, T)
    def _(t):
        for k in range(1, ny):
            y_copy(k, t).wait_send()
        for k in range(1, nx):
            x_copy(k, t).wait_send()
            xa_copy(k, t).wait_send()
        for k in range(1, NZ):
            z_copy(k, t).wait_send()
            za_copy(k, t).wait_send()


def tail(nx, ny, hat, gkv, wkv, up, down, media, cot_all, gain, parts, mid, branch, attq):
    T = CHUNKS
    rows, feat = hat.shape
    pieces, _, two = gkv.shape
    lat = mid.shape[0]
    ff = up.shape[1]
    blocks = nx * NZ
    chunk = feat // T
    sub = chunk // blocks
    xt = 256 // (lat * pieces)
    tile_rows = xt * pieces * lat
    tiles = NZ * nx // xt
    any_ = pl.BlockSpec(memory_space=pl.ANY)
    vm = pl.BlockSpec(memory_space=pltpu.VMEM)
    S = jax.ShapeDtypeStruct
    every = (NZ, nx, ny, 2, lat)
    V = pltpu.VMEM
    D = pltpu.SemaphoreType.DMA
    spread4 = NZ + nx + ny + 2 - 4
    media_rows = media.shape[0]
    outs = (
        S((T, blocks, sub, two), BF16),
        S((media_rows, feat), BF16),
        S((tiles, tile_rows, ff), BF16),
        S((tiles, tile_rows, ff), BF16),
        S(every + (feat,), BF16),
        S(every + (feat,), BF16),
        S(every + (two,), BF16),
        S((8, feat), F32),
    )
    return pl.pallas_call(
        functools.partial(tail_kernel, nx, ny),
        out_shape=outs,
        in_specs=[any_] * 7 + [vm] * 5,
        out_specs=(any_,) * 7 + (vm,),
        scratch_shapes=[
            V(hat.shape, BF16),
            V(gkv.shape, BF16),
            V(wkv.shape, BF16),
            V(up.shape, BF16),
            V(down.shape, BF16),
            V((T, chunk, two), BF16),
            V((T, chunk, two), BF16),
            V((T, chunk, two), F32),
            V((ny - 1, T, chunk, two), BF16),
            V((ny - 1, T, chunk, two), BF16),
            V((nx - 1, T, NZ * sub, two), BF16),
            V((nx - 1, T, NZ * sub, two), BF16),
            V((NZ - 1, T, sub, two), BF16),
            V((NZ - 1, T, sub, two), BF16),
            V((T, sub, two), BF16),
            V((ny, 2, lat, two), BF16),
            V((2, 256, feat), BF16),
            V((256, feat), BF16),
            V((2, xt, ny, 2, lat, feat), BF16),
            V((2, xt, ny, 2, lat, feat), BF16),
            V((tile_rows, ff), BF16),
            V((tile_rows, ff), BF16),
            V((8, feat), F32),
            V((spread4, 8, feat), F32),
            D((5,)),
            D((6,)),
            D((3,)),
            D((T,)),
            D((T,)),
            D((ny - 1, T)),
            D((ny - 1, T)),
            D((nx - 1, T)),
            D((nx - 1, T)),
            D((NZ - 1, T)),
            D((NZ - 1, T)),
            D((NZ - 1, T)),
            D((NZ - 1, T)),
            D((nx - 1, T)),
            D((nx - 1, T)),
            D((T,)),
            D((spread4,)),
            D((spread4,)),
            D((spread4,)),
            D((spread4,)),
            D((spread4,)),
            D((spread4,)),
            D((ny + NZ + nx - 2,)),
            D((ny + NZ + nx - 2,)),
            D((4,)),
        ],
        compiler_params=pltpu.CompilerParams(
            collective_id=3, has_side_effects=True, vmem_limit_bytes=67043328
        ),
        name="tail",
    )(hat, gkv, wkv, up, down, media, cot_all, gain, parts, mid, branch, attq)


def shards(
    media_tokens,
    latents,
    frame_counts,
    gain_media,
    gain_latent,
    gain_ffn,
    qkv_weight,
    out_weight,
    up_weight,
    down_weight,
    cotangent,
):
    group = lax.axis_size("ha")
    media_rows = media_tokens.shape[0]
    lat = latents.shape[0]
    width = media_tokens.shape[1]
    cols = qkv_weight.shape[2]
    heads = cols // HEAD
    place = lax.axis_index("ha")
    core = place % 2
    count = frame_counts[place // 2]
    scale = HEAD ** (-0.5)
    entry_total = float(lat * width * lax.axis_size("sa") * group)
    both = ("sa", "ha")

    media_norm, media_inv = normalize(media_tokens.astype(F32))
    latent_norm, latent_inv = normalize(latents)
    latent_hat = (latent_norm * gain_latent).astype(BF16)
    hat = jnp.concatenate([(media_norm * gain_media).astype(BF16), latent_hat], axis=0)

    w_all = lax.all_gather(qkv_weight, "ha", axis=0)
    o_all = lax.all_gather(out_weight, "ha", axis=0)
    cot_all = lax.all_gather(cotangent, both, axis=0, tiled=True)
    lat_all = lax.all_gather(latent_hat, both, axis=0, tiled=True)
    keys = dot("rd,ade->are", hat, w_all[:, 1]).astype(BF16)
    values = dot("rd,ade->are", hat, w_all[:, 2]).astype(BF16)
    q_own = dot("rd,ade->are", latent_hat, w_all[:, 0]).astype(BF16)

    def pair_rows(x):
        other = swap_core(x, group)
        return jnp.where(
            core == 0, jnp.concatenate([x, other], axis=1), jnp.concatenate([other, x], axis=1)
        )

    col_head = jnp.arange(cols, dtype=jnp.int32) // HEAD

    def spread(x):
        picked = [jnp.where(col_head == h, x, jnp.zeros_like(x)) for h in range(heads)]
        return jnp.concatenate(picked, axis=1)

    def gather_heads(x):
        parts = x.reshape(x.shape[0], heads, 2 * lat, cols)
        return sum(jnp.where(col_head == h, parts[:, h], 0.0) for h in range(heads))

    def own_half(x):
        mine = lax.dynamic_slice_in_dim(x, core * lat, lat, 1)
        theirs = lax.dynamic_slice_in_dim(x, (1 - core) * lat, lat, 1)
        return mine + swap_core(theirs, group)

    q_blk = spread(pair_rows(q_own))
    row = jnp.arange(media_rows + lat, dtype=jnp.int32)
    usable = jnp.logical_or((core * media_rows + row) // PATCH < count, row >= media_rows)
    scores = jnp.where(usable, dot("aqe,ake->aqk", q_blk, keys) * scale, NEG)
    top = jnp.max(scores, axis=-1, keepdims=True)
    probs = jnp.exp(scores - top)
    total = jnp.sum(probs, axis=-1, keepdims=True)
    stats = jnp.concatenate([top, total], axis=-1)
    stats_other = swap_core(stats, group)
    top_all = jnp.maximum(top, stats_other[..., :1])
    denom = total * jnp.exp(top - top_all) + stats_other[..., 1:] * jnp.exp(
        stats_other[..., :1] - top_all
    )
    probs = (probs * (jnp.exp(top - top_all) / denom)).astype(BF16)
    attended32 = own_half(gather_heads(dot("aqk,ake->aqe", probs, values)))
    attended = attended32.astype(BF16)
    attn_branch = dot("are,aed->rd", attended, o_all)
    residual = latents + attn_branch
    mid_norm, mid_inv = normalize(residual)
    mid_hat = (mid_norm * gain_ffn).astype(BF16)
    mid_ha = lax.all_gather(mid_hat, "ha", axis=0, tiled=True)
    cot_ha = lax.all_gather(cotangent, "ha", axis=0, tiled=True)
    pre_act = jnp.dot(mid_ha, up_weight, preferred_element_type=F32)
    hidden = gelu_exact(pre_act).astype(BF16)
    ffn_branch = lax.psum_scatter(
        jnp.dot(hidden, down_weight, preferred_element_type=F32).astype(BF16),
        "ha",
        scatter_dimension=0,
        tiled=True,
    ).astype(F32)
    output = residual + ffn_branch
    grad_hidden = dot("rd,fd->rf", cot_ha, down_weight)
    unused_value, gelu_back = jax.vjp(gelu_exact, pre_act)
    grad_pre = gelu_back(grad_hidden)[0].astype(BF16)
    grad_mid = lax.psum_scatter(
        dot("rf,df->rd", grad_pre, up_weight).astype(BF16),
        "ha",
        scatter_dimension=0,
        tiled=True,
    ).astype(F32)
    gain_ffn_part = jnp.sum(grad_mid * mid_norm, axis=0)
    grad_residual = cotangent.astype(F32) + norm_grad(grad_mid * gain_ffn, mid_norm, mid_inv)
    grad_branch = grad_residual.astype(BF16)
    grad_att = dot("rd,aed->are", grad_branch, o_all).astype(BF16)
    inner = attended32 * grad_att.astype(F32)
    inner = jnp.stack(
        [jnp.sum(jnp.where(col_head == h, inner, 0.0), axis=-1) for h in range(heads)], axis=-1
    )
    g_blk = spread(pair_rows(grad_att))
    inner = jnp.moveaxis(pair_rows(inner), 2, 1).reshape(group, heads * 2 * lat, 1)
    grad_probs = dot("aqe,ake->aqk", g_blk, values)
    grad_scores = (probs.astype(F32) * (grad_probs - inner)).astype(BF16)
    grad_values = dot("aqk,aqe->ake", probs, g_blk).astype(BF16)
    grad_keys = (dot("aqk,aqe->ake", grad_scores, q_blk) * scale).astype(BF16)
    grad_q = own_half(gather_heads(dot("aqk,ake->aqe", grad_scores, keys)) * scale).astype(BF16)

    wkv = jnp.concatenate([w_all[:, 1], w_all[:, 2]], axis=-1)
    gkv = jnp.concatenate([grad_keys, grad_values], axis=-1)
    grad_latent_hat = dot("are,ade->rd", gkv[:, media_rows:], wkv) + dot(
        "are,ade->rd", grad_q, w_all[:, 0]
    )
    gain_latent_part = jnp.sum(grad_latent_hat * latent_norm, axis=0)
    grad_latents = grad_residual + norm_grad(grad_latent_hat * gain_latent, latent_norm, latent_inv)
    squares = jnp.stack(
        [
            jnp.sum(residual * residual),
            jnp.sum(attn_branch * attn_branch),
            jnp.sum(ffn_branch * ffn_branch),
        ]
    )
    parts = jnp.stack(
        [
            jnp.zeros((width,), F32),
            gain_latent_part,
            gain_ffn_part,
            jnp.pad(squares, (0, width - 3)),
        ]
    )
    parts = jnp.pad(parts, ((0, 4), (0, 0)))
    nx, ny = lax.axis_size("sa") // NZ, group // 2
    kv, gm, hid, gp, mid_all, branch_all, attq_all, gains = tail(
        nx,
        ny,
        hat,
        gkv,
        wkv,
        up_weight,
        down_weight,
        media_tokens,
        cot_all.reshape(NZ, nx, ny, 2, lat, width),
        gain_media[None],
        parts,
        mid_hat,
        grad_branch,
        jnp.concatenate([attended, grad_q], axis=2),
    )
    kv = kv.reshape(width, 2 * cols)
    hid = hid.reshape(-1, hid.shape[-1])
    gp = gp.reshape(-1, gp.shape[-1])
    mid_all = mid_all.reshape(-1, width)
    branch_all = branch_all.reshape(-1, width)
    attq_all = attq_all.reshape(-1, 2 * cols)
    grad_media = gm.astype(F32)
    grad_out = dot("rc,rd->cd", attq_all[:, :cols], branch_all)
    grad_wq = dot("rd,re->de", lat_all, attq_all[:, cols:])
    grad_down = dot("rf,rd->fd", hid, cot_all)
    grad_up = dot("rd,rf->df", mid_all, gp)
    grad_kv = jnp.stack([kv[:, :cols], kv[:, cols:]]).astype(F32)
    gain_one, gain_two, gain_three = gains[0], gains[1], gains[2]
    square_sums = gains[3, :3]
    roots = jnp.sqrt(square_sums / entry_total)
    return (
        output,
        grad_media,
        grad_latents,
        gain_one,
        gain_two,
        gain_three,
        jnp.concatenate([grad_wq[None], grad_kv], axis=0),
        grad_out,
        grad_up,
        grad_down,
        roots[0],
        roots[1],
        roots[2],
    )


def solution(mesh):
    placed = (
        P(("sa", "ha"), None),
        P(("sa", "ha"), None),
        P("sa"),
        P(),
        P(),
        P(),
        P(None, None, "ha"),
        P("ha", None),
        P(None, "ha"),
        P("ha", None),
        P(("sa", "ha"), None),
    )
    return jax.shard_map(
        shards,
        mesh=mesh,
        in_specs=placed,
        out_specs=(
            P(("sa", "ha"), None),
            P(("sa", "ha"), None),
            P(("sa", "ha"), None),
            P(),
            P(),
            P(),
            P(None, None, "ha"),
            P("ha", None),
            P(None, "ha"),
            P("ha", None),
            P(),
            P(),
            P(),
        ),
        check_vma=False,
    )
```

```python
import functools

import jax
import jax.numpy as jnp
from jax import lax
from jax.experimental import pallas as pl
from jax.experimental.pallas import tpu as pltpu
from jax.sharding import PartitionSpec as P

HEAD = 96
PATCH = 256
EPS = 1e-05
NEG = -1000000000.0
F32 = jnp.float32
BF16 = jnp.bfloat16


def normalize(values):
    centered = values - jnp.mean(values, axis=-1, keepdims=True)
    inverse = lax.rsqrt(jnp.mean(centered * centered, axis=-1, keepdims=True) + EPS)
    return centered * inverse, inverse


def norm_grad(grad, normed, inverse):
    first = jnp.mean(grad, axis=-1, keepdims=True)
    second = jnp.mean(grad * normed, axis=-1, keepdims=True)
    return inverse * (grad - first - normed * second)


def dot(spec, a, b):
    return jnp.einsum(spec, a, b, preferred_element_type=F32)


MESH = pl.DeviceIdType.MESH
NZ = 4
CHUNKS = 6


def dg(a, b, ca, cb):
    return lax.dot_general(a, b, (((ca,), (cb,)), ((), ())), preferred_element_type=F32)


class Where:
    def __init__(self, nx, ny):
        self.nx, self.ny = nx, ny
        sa, ha = lax.axis_index("sa"), lax.axis_index("ha")
        self.own = {"z": sa // nx, "x": sa % nx, "y": ha // 2, "c": ha % 2}
        self.size = {"z": NZ, "x": nx, "y": ny, "c": 2}

    def at(self, axis, k):
        return lax.rem(self.own[axis] + k, self.size[axis])

    def device(self, axis, k):
        p = dict(self.own)
        p[axis] = self.at(axis, k)
        return {"sa": p["z"] * self.nx + p["x"], "ha": p["y"] * 2 + p["c"]}


def greet(me):
    barrier = pltpu.get_barrier_semaphore()
    count = 0
    for axis in "cyxz":
        for k in range(1, me.size[axis]):
            pl.semaphore_signal(
                barrier, inc=1, device_id=me.device(axis, k), device_id_type=MESH
            )
            count += 1
    pl.semaphore_wait(barrier, count)


class Gather:
    def __init__(self, me, own, buf, order, send, recv, local, done=""):
        self.me, self.own, self.buf, self.order = me, own, buf, order
        self.send, self.recv, self.local = send, recv, local
        self.done = done

    def slot(self, done):
        me = self.me
        return tuple(
            pl.ds(0, me.size[a]) if a in done else me.own[a] for a in "zxyc"
        )

    def keep(self):
        return pltpu.make_async_copy(
            self.own, self.buf.at[self.slot(self.done)], self.local
        )

    def copies(self, phase):
        done = self.done + self.order[:phase]
        axis = self.order[phase]
        first = sum(self.me.size[a] - 1 for a in self.order[:phase])
        here = self.buf.at[self.slot(done)]
        src = self.own if phase == 0 and self.own is not None else here
        return [
            pltpu.make_async_remote_copy(
                src_ref=src,
                dst_ref=here,
                send_sem=self.send.at[first + k - 1],
                recv_sem=self.recv.at[first + k - 1],
                device_id=self.me.device(axis, k),
                device_id_type=MESH,
            )
            for k in range(1, self.me.size[axis])
        ]

    def start(self, phase):
        if phase == 0 and self.own is not None:
            self.keep().start()
        for c in self.copies(phase):
            c.start()

    def finish(self, phase):
        if phase == 0 and self.own is not None:
            self.keep().wait()
        for c in self.copies(phase):
            c.wait_recv()

    def next(self, phase):
        self.finish(phase)
        self.start(phase + 1)

    def drain(self):
        for phase in range(len(self.order)):
            for c in self.copies(phase):
                c.wait_send()


def tail_kernel(
    nx,
    ny,
    hat_h,
    gkv_h,
    wkv_h,
    up_h,
    down_h,
    media_h,
    cot_all,
    wq_h,
    gain_r,
    gain_l,
    lat_r,
    gres_r,
    gq_r,
    part_r,
    mid_r,
    branch_r,
    attq_r,
    kv_o,
    gm_o,
    hid_o,
    gp_o,
    mid_all,
    branch_all,
    attq_all,
    gains_o,
    glat_o,
    hat,
    gkv,
    wkv,
    up,
    down,
    send_c,
    recv_c,
    acc,
    send_y,
    recv_y,
    send_x,
    recv_x,
    send_z,
    recv_z,
    red,
    attq_y,
    media_t,
    gm_t,
    mid_t,
    cot_t,
    hid_t,
    gp_t,
    wqb,
    gbuf,
    grecv,
    load_sem,
    tile_sem,
    out_sem,
    c_send,
    c_recv,
    y_send,
    y_recv,
    x_send,
    x_recv,
    z_send,
    z_recv,
    za_send,
    za_recv,
    xa_send,
    xa_recv,
    keep_sem,
    g_send,
    g_recv,
    mid_send,
    mid_recv,
    br_send,
    br_recv,
    aq_send,
    aq_recv,
    own_sem,
):
    me = Where(nx, ny)
    z, x, y, c = (me.own[a] for a in "zxyc")
    T = CHUNKS
    pieces = 2 * ny
    chunk = acc.shape[1]
    quarter = send_x.shape[2]
    sub = red.shape[1]
    feat = hat.shape[1]

    def load(i, src, dst):
        return pltpu.make_async_copy(src, dst, load_sem.at[i])

    hat_copy = load(0, hat_h, hat)
    gkv_copy = load(1, gkv_h, gkv)
    wkv_copy = load(2, wkv_h, wkv)
    up_copy = load(3, up_h, up)
    down_copy = load(4, down_h, down)
    for copy in (hat_copy, gkv_copy, wkv_copy, up_copy, down_copy):
        copy.start()
    greet(me)

    mid = Gather(me, mid_r, mid_all, "yzxc", mid_send, mid_recv, own_sem.at[0])
    branch = Gather(me, branch_r, branch_all, "zxyc", br_send, br_recv, own_sem.at[1])

    def attq_y_copies():
        return [
            pltpu.make_async_remote_copy(
                src_ref=attq_r.at[pl.ds(2 * me.at("y", k), 2)],
                dst_ref=attq_y.at[y],
                send_sem=aq_send.at[k - 1],
                recv_sem=aq_recv.at[k - 1],
                device_id=me.device("y", k),
                device_id_type=MESH,
            )
            for k in range(1, ny)
        ]

    attq_own = pltpu.make_async_copy(
        attq_r.at[pl.ds(2 * y, 2)], attq_y.at[y], own_sem.at[2]
    )
    attq_c = pltpu.make_async_remote_copy(
        src_ref=attq_y.at[pl.ds(0, ny), 1 - c],
        dst_ref=attq_all.at[z, x, pl.ds(0, ny), c],
        send_sem=aq_send.at[ny - 1],
        recv_sem=aq_recv.at[ny - 1],
        device_id=me.device("c", 1),
        device_id_type=MESH,
    )
    attq_keep = pltpu.make_async_copy(
        attq_y.at[pl.ds(0, ny), c], attq_all.at[z, x, pl.ds(0, ny), c], own_sem.at[3]
    )
    attq = Gather(
        me,
        None,
        attq_all,
        "zx",
        aq_send.at[pl.ds(ny, NZ + nx - 2)],
        aq_recv.at[pl.ds(ny, NZ + nx - 2)],
        None,
        "yc",
    )

    mid.start(0)
    attq_own.start()
    for copy in attq_y_copies():
        copy.start()
    branch.start(0)

    def grad_rows(k, t, parity):
        piece = 2 * me.at("y", k) + parity
        left = hat[:, pl.ds(pl.multiple_of(t * chunk, 128), chunk)]
        return dg(left, gkv[piece], 0, 0)

    def core_copy(t):
        return pltpu.make_async_remote_copy(
            src_ref=send_c.at[t],
            dst_ref=recv_c.at[t],
            send_sem=c_send.at[t],
            recv_sem=c_recv.at[t],
            device_id=me.device("c", 1),
            device_id_type=MESH,
        )

    def y_copy(k, t):
        return pltpu.make_async_remote_copy(
            src_ref=send_y.at[k - 1, t],
            dst_ref=recv_y.at[k - 1, t],
            send_sem=y_send.at[k - 1, t],
            recv_sem=y_recv.at[k - 1, t],
            device_id=me.device("y", k),
            device_id_type=MESH,
        )

    def x_copy(k, t):
        return pltpu.make_async_remote_copy(
            src_ref=send_x.at[k - 1, t],
            dst_ref=recv_x.at[k - 1, t],
            send_sem=x_send.at[k - 1, t],
            recv_sem=x_recv.at[k - 1, t],
            device_id=me.device("x", k),
            device_id_type=MESH,
        )

    def z_copy(k, t):
        return pltpu.make_async_remote_copy(
            src_ref=send_z.at[k - 1, t],
            dst_ref=recv_z.at[k - 1, t],
            send_sem=z_send.at[k - 1, t],
            recv_sem=z_recv.at[k - 1, t],
            device_id=me.device("z", k),
            device_id_type=MESH,
        )

    def za_copy(k, t):
        return pltpu.make_async_remote_copy(
            src_ref=red.at[t],
            dst_ref=kv_o.at[t, x * NZ + z],
            send_sem=za_send.at[k - 1, t],
            recv_sem=za_recv.at[k - 1, t],
            device_id=me.device("z", k),
            device_id_type=MESH,
        )

    def xa_copy(k, t):
        rows = kv_o.at[t, pl.ds(x * NZ, NZ)]
        return pltpu.make_async_remote_copy(
            src_ref=rows,
            dst_ref=rows,
            send_sem=xa_send.at[k - 1, t],
            recv_sem=xa_recv.at[k - 1, t],
            device_id=me.device("x", k),
            device_id_type=MESH,
        )

    def keep_copy(t):
        return pltpu.make_async_copy(red.at[t], kv_o.at[t, x * NZ + z], keep_sem.at[t])

    hat_copy.wait()
    gkv_copy.wait()
    lag = 2
    steps = ny * T

    @pl.loop(0, steps + lag)
    def _(j):
        @pl.when(j < steps)
        def _():
            k, t = lax.rem(1 + j // T, ny), lax.rem(j, T)

            @pl.when(j >= T)
            def _():
                core_copy(t).wait_send()

            send_c[t] = grad_rows(k, t, 1 - c).astype(BF16)
            core_copy(t).start()

        @pl.when(j >= lag)
        def _():
            i = j - lag
            k, t = lax.rem(1 + i // T, ny), lax.rem(i, T)
            mine = grad_rows(k, t, c)
            core_copy(t).wait_recv()
            mine = mine + recv_c[t].astype(F32)

            @pl.when(i >= steps - T)
            def _():
                acc[t] = mine

            @pl.when(i < steps - T)
            def _():
                for step in range(1, ny):

                    @pl.when(i // T == step - 1)
                    def _():
                        send_y[step - 1, t] = mine.astype(BF16)
                        y_copy(step, t).start()

        @pl.when(j == 3)
        def _():
            mid.next(0)
            attq_own.wait()
            for copy in attq_y_copies():
                copy.wait_recv()
            attq_c.start()
            attq_keep.start()

        @pl.when(j == 9)
        def _():
            attq_keep.wait()
            attq_c.wait_recv()
            attq.start(0)

    for t in range(T):
        core_copy(t).wait_send()
    wkv_copy.wait()
    up_copy.wait()
    down_copy.wait()

    gbuf[...] = part_r[...]
    media_rows = media_h.shape[0]
    tile = media_t.shape[1]
    n_media = media_rows // tile

    def media_load(u):
        return pltpu.make_async_copy(
            media_h.at[pl.ds(pl.multiple_of(u * tile, tile), tile)],
            media_t.at[lax.rem(u, 2)],
            tile_sem.at[lax.rem(u, 2)],
        )

    def gm_store(u):
        return pltpu.make_async_copy(
            gm_t, gm_o.at[pl.ds(pl.multiple_of(u * tile, tile), tile)], out_sem.at[0]
        )

    def media_tile(u):
        @pl.when(u + 1 < n_media)
        def _():
            media_load(u + 1).start()

        rows = pl.ds(pl.multiple_of(u * tile, tile), tile)
        total = dg(gkv[0, rows], wkv[0], 1, 1)
        for a in range(1, pieces):
            total = total + dg(gkv[a, rows], wkv[a], 1, 1)
        media_load(u).wait()
        values = media_t[lax.rem(u, 2)].astype(F32)
        normed, inverse = normalize(values)
        gbuf[0:1] = gbuf[0:1] + jnp.sum(total * normed, axis=0, keepdims=True)
        result = norm_grad(total * gain_r[...], normed, inverse)

        @pl.when(u >= 1)
        def _():
            gm_store(u - 1).wait()

        gm_t[...] = result.astype(BF16)
        gm_store(u).start()

    xt = mid_t.shape[1]
    n_ffn = NZ * (nx // xt)

    def rows_load(u):
        zz, xx = u // (nx // xt), lax.rem(u, nx // xt) * xt
        b = lax.rem(u, 2)
        return [
            pltpu.make_async_copy(
                mid_all.at[zz, pl.ds(xx, xt)], mid_t.at[b], tile_sem.at[2 + b]
            ),
            pltpu.make_async_copy(
                cot_all.at[zz, pl.ds(xx, xt)], cot_t.at[b], tile_sem.at[4 + b]
            ),
        ]

    def ffn_store(u):
        return [
            pltpu.make_async_copy(hid_t, hid_o.at[u], out_sem.at[1]),
            pltpu.make_async_copy(gp_t, gp_o.at[u], out_sem.at[2]),
        ]

    def ffn_tile(u):
        @pl.when(u + 1 < n_ffn)
        def _():
            for copy in rows_load(u + 1):
                copy.start()

        for copy in rows_load(u):
            copy.wait()

        @pl.when(u >= 1)
        def _():
            for copy in ffn_store(u - 1):
                copy.wait()

        b = lax.rem(u, 2)
        mid_rows = mid_t[b].reshape(-1, feat)
        cot_rows = cot_t[b].reshape(-1, feat)
        width = up.shape[1] // 3
        for part in range(3):
            cols = pl.ds(part * width, width)
            pre = dg(mid_rows, up[:, cols], 1, 0)
            grad = dg(cot_rows, down[cols, :], 1, 1)
            cdf = 0.5 * (1.0 + lax.erf(pre * (0.5**0.5)))
            slope = cdf + pre * (jnp.exp(-0.5 * pre * pre) * 0.3989422804014327)
            hid_t[:, cols] = (pre * cdf).astype(BF16)
            gp_t[:, cols] = (grad * slope).astype(BF16)
        for copy in ffn_store(u):
            copy.start()

    def wq_load(a):
        return pltpu.make_async_copy(wq_h.at[a], wqb.at[a % 2], load_sem.at[a % 2])

    def latent_rows():
        wq_load(0).start()
        rows = pl.ds(media_rows, lat_r.shape[0])
        total = dg(gkv[0, rows], wkv[0], 1, 1)
        for a in range(1, pieces):
            total = total + dg(gkv[a, rows], wkv[a], 1, 1)
        for a in range(pieces):
            if a + 1 < pieces:
                wq_load(a + 1).start()
            wq_load(a).wait()
            total = total + dg(gq_r[a], wqb[a % 2], 1, 1)
        normed, inverse = normalize(lat_r[...])
        gbuf[1:2] = jnp.sum(total * normed, axis=0, keepdims=True)
        glat_o[...] = gres_r[...] + norm_grad(total * gain_l[...], normed, inverse)

    def comm(i):
        @pl.when(i < T)
        def _():
            t = i
            for k in range(1, ny):
                y_copy(k, t).wait_recv()
            whole = acc[t]
            for k in range(1, ny):
                whole = whole + recv_y[k - 1, t].astype(F32)
            acc[t] = whole
            for k in range(1, nx):
                there = pl.ds(pl.multiple_of(me.at("x", k) * quarter, 8), quarter)
                send_x[k - 1, t] = acc[t, there].astype(BF16)
                x_copy(k, t).start()

        @pl.when(jnp.logical_and(i >= 1, i < T + 1))
        def _():
            t = i - 1
            for k in range(1, nx):
                x_copy(k, t).wait_recv()
            here = pl.ds(pl.multiple_of(x * quarter, 8), quarter)
            whole = acc[t, here]
            for k in range(1, nx):
                whole = whole + recv_x[k - 1, t].astype(F32)
            acc[t, here] = whole
            for k in range(1, NZ):
                there = pl.ds(
                    pl.multiple_of(x * quarter + me.at("z", k) * sub, 8), sub
                )
                send_z[k - 1, t] = acc[t, there].astype(BF16)
                z_copy(k, t).start()

        @pl.when(jnp.logical_and(i >= 2, i < T + 2))
        def _():
            t = i - 2
            for k in range(1, NZ):
                z_copy(k, t).wait_recv()
            whole = acc[t, pl.ds(pl.multiple_of(x * quarter + z * sub, 8), sub)]
            for k in range(1, NZ):
                whole = whole + recv_z[k - 1, t].astype(F32)
            red[t] = whole.astype(BF16)
            keep_copy(t).start()
            for k in range(1, NZ):
                za_copy(k, t).start()

        @pl.when(jnp.logical_and(i >= 3, i < T + 3))
        def _():
            t = i - 3
            keep_copy(t).wait()
            for k in range(1, NZ):
                za_copy(k, t).wait_recv()
            for k in range(1, nx):
                xa_copy(k, t).start()

        @pl.when(i >= 4)
        def _():
            t = i - 4
            for k in range(1, nx):
                xa_copy(k, t).wait_recv()

    def gain_copies(axis, base):
        return [
            pltpu.make_async_remote_copy(
                src_ref=gbuf,
                dst_ref=grecv.at[base + k - 1],
                send_sem=g_send.at[base + k - 1],
                recv_sem=g_recv.at[base + k - 1],
                device_id=me.device(axis, k),
                device_id_type=MESH,
            )
            for k in range(1, me.size[axis])
        ]

    def gain_base(axis):
        return sum(me.size[a] - 1 for a in "cyxz"[: "cyxz".index(axis)])

    def gain_start(axis):
        for copy in gain_copies(axis, gain_base(axis)):
            copy.start()

    def gain_finish(axis):
        base = gain_base(axis)
        for copy in gain_copies(axis, base):
            copy.wait_send()
            copy.wait_recv()
        total = gbuf[...]
        for k in range(1, me.size[axis]):
            total = total + grecv[base + k - 1]
        gbuf[...] = total

    media_load(0).start()

    @pl.loop(0, T + 4)
    def _(i):
        comm(i)

        @pl.when(i == 0)
        def _():
            mid.next(1)

        @pl.when(i == 1)
        def _():
            branch.next(0)

        @pl.when(i < 2)
        def _():
            @pl.loop(0, n_media // 2)
            def _(u):
                media_tile(i * (n_media // 2) + u)

        @pl.when(i == 2)
        def _():
            gm_store(n_media - 1).wait()
            latent_rows()
            gain_start("c")
            mid.next(2)
            mid.finish(3)
            for copy in rows_load(0):
                copy.start()

        @pl.when(i == 3)
        def _():
            gain_finish("c")
            gain_start("y")
            attq.next(0)

        @pl.when(jnp.logical_and(i >= 2, i < 4))
        def _():
            @pl.loop(0, n_ffn // 2)
            def _(u):
                ffn_tile((i - 2) * (n_ffn // 2) + u)

        @pl.when(i == 4)
        def _():
            for copy in ffn_store(n_ffn - 1):
                copy.wait()
            gain_finish("y")
            gain_start("x")
            branch.next(1)

        @pl.when(i == 5)
        def _():
            gain_finish("x")
            gain_start("z")

        @pl.when(i == 7)
        def _():
            branch.next(2)

    gain_finish("z")
    gains_o[...] = gbuf[...]
    branch.finish(3)
    attq.finish(1)
    mid.drain()
    branch.drain()
    for copy in attq_y_copies():
        copy.wait_send()
    attq_c.wait_send()
    attq.drain()

    @pl.loop(0, T)
    def _(t):
        for k in range(1, ny):
            y_copy(k, t).wait_send()
        for k in range(1, nx):
            x_copy(k, t).wait_send()
            xa_copy(k, t).wait_send()
        for k in range(1, NZ):
            z_copy(k, t).wait_send()
            za_copy(k, t).wait_send()


def tail(
    nx, ny, hat, gkv, wkv, up, down, media, cot_all, wq, gain_m, gain_l, lats, gres, gq, parts, mid, branch, attq
):
    T = CHUNKS
    rows, feat = hat.shape
    pieces, _, two = gkv.shape
    lat = mid.shape[0]
    ff = up.shape[1]
    blocks = nx * NZ
    chunk = feat // T
    sub = chunk // blocks
    xt = 256 // (lat * pieces)
    tile_rows = xt * pieces * lat
    tiles = NZ * nx // xt
    any_ = pl.BlockSpec(memory_space=pl.ANY)
    vm = pl.BlockSpec(memory_space=pltpu.VMEM)
    S = jax.ShapeDtypeStruct
    every = (NZ, nx, ny, 2, lat)
    V = pltpu.VMEM
    D = pltpu.SemaphoreType.DMA
    spread4 = NZ + nx + ny + 2 - 4
    media_rows = media.shape[0]
    outs = (
        S((T, blocks, sub, two), BF16),
        S((media_rows, feat), BF16),
        S((tiles, tile_rows, ff), BF16),
        S((tiles, tile_rows, ff), BF16),
        S(every + (feat,), BF16),
        S(every + (feat,), BF16),
        S(every + (two,), BF16),
        S((8, feat), F32),
        S(gres.shape, F32),
    )
    return pl.pallas_call(
        functools.partial(tail_kernel, nx, ny),
        out_shape=outs,
        in_specs=[any_] * 8 + [vm] * 9,
        out_specs=(any_,) * 7 + (vm,) * 2,
        scratch_shapes=[
            V(hat.shape, BF16),
            V(gkv.shape, BF16),
            V(wkv.shape, BF16),
            V(up.shape, BF16),
            V(down.shape, BF16),
            V((T, chunk, two), BF16),
            V((T, chunk, two), BF16),
            V((T, chunk, two), F32),
            V((ny - 1, T, chunk, two), BF16),
            V((ny - 1, T, chunk, two), BF16),
            V((nx - 1, T, NZ * sub, two), BF16),
            V((nx - 1, T, NZ * sub, two), BF16),
            V((NZ - 1, T, sub, two), BF16),
            V((NZ - 1, T, sub, two), BF16),
            V((T, sub, two), BF16),
            V((ny, 2, lat, two), BF16),
            V((2, 256, feat), BF16),
            V((256, feat), BF16),
            V((2, xt, ny, 2, lat, feat), BF16),
            V((2, xt, ny, 2, lat, feat), BF16),
            V((tile_rows, ff), BF16),
            V((tile_rows, ff), BF16),
            V((2,) + wq.shape[1:], BF16),
            V((8, feat), F32),
            V((spread4, 8, feat), F32),
            D((5,)),
            D((6,)),
            D((3,)),
            D((T,)),
            D((T,)),
            D((ny - 1, T)),
            D((ny - 1, T)),
            D((nx - 1, T)),
            D((nx - 1, T)),
            D((NZ - 1, T)),
            D((NZ - 1, T)),
            D((NZ - 1, T)),
            D((NZ - 1, T)),
            D((nx - 1, T)),
            D((nx - 1, T)),
            D((T,)),
            D((spread4,)),
            D((spread4,)),
            D((spread4,)),
            D((spread4,)),
            D((spread4,)),
            D((spread4,)),
            D((ny + NZ + nx - 2,)),
            D((ny + NZ + nx - 2,)),
            D((4,)),
        ],
        compiler_params=pltpu.CompilerParams(
            collective_id=3, has_side_effects=True, vmem_limit_bytes=67043328
        ),
        name="tail",
    )(
        hat, gkv, wkv, up, down, media, cot_all, wq, gain_m, gain_l, lats, gres, gq, parts, mid, branch, attq
    )


def full_sum(x):
    return jnp.sum(jnp.sum(x, axis=1, keepdims=True), axis=0, keepdims=True)


class Relay:
    def __init__(self, me, own, buf, order, send, recv):
        self.me, self.own, self.buf, self.order = me, own, buf, order
        self.send, self.recv = send, recv
        ny, nx = me.size["y"] - 1, me.size["x"] - 1
        sizes = {"o": 1, "y": ny, "x": ny * nx, "z": ny, "c": ny}
        self.base, total = {}, 0
        for a in "oyxzc":
            self.base[a] = total
            total += sizes[a]

    @staticmethod
    def slots(nx, ny):
        return 1 + 3 * (ny - 1) + (ny - 1) * (nx - 1)

    def part(self, done):
        me = self.me
        index = [pl.ds(0, me.size["x"]) if "x" in done else me.own["x"]]
        if "z" in self.order:
            index.append(pl.ds(0, 2) if "z" in done else lax.rem(me.own["z"], 2))
        return tuple(index)

    def copies(self, phase):
        me, buf = self.me, self.buf
        y, c = me.own["y"], me.own["c"]
        out = []

        def add(src, dst, where):
            i = self.base[phase] + len(out)
            out.append(
                pltpu.make_async_remote_copy(
                    src_ref=src,
                    dst_ref=dst,
                    send_sem=self.send.at[i],
                    recv_sem=self.recv.at[i],
                    device_id=where,
                    device_id_type=MESH,
                )
            )

        if phase == "o":
            add(self.own, buf.at[y, c], me.device("c", 1))
            return out
        done = self.order[1 : self.order.index(phase)] if phase in "xz" else ""
        for k in range(1, me.size["y"]):
            if phase == "y":
                at = self.part("")
                add(self.own.at[at], buf.at[(y, c) + at], me.device("y", k))
                continue
            yk = me.at("y", me.size["y"] - k)
            if phase == "c":
                add(buf.at[yk, c], buf.at[yk, c], me.device("c", 1))
                continue
            ref = buf.at[(yk, c) + self.part(done)]
            if phase == "z":
                add(ref, ref, me.device("z", 1 - 2 * lax.rem(me.own["z"], 2) + NZ))
            else:
                for j in range(1, me.size["x"]):
                    add(ref, ref, me.device("x", j))
        return out

    def start(self, phase):
        for copy in self.copies(phase):
            copy.start()

    def wait(self, phase):
        for copy in self.copies(phase):
            copy.wait_recv()

    def next(self, phase):
        self.wait(phase)
        at = self.order.index(phase) + 1
        self.start(self.order[at] if at < len(self.order) else "c")

    def drain(self):
        for phase in "o" + self.order + "c":
            for copy in self.copies(phase):
                copy.wait_send()


def front_kernel(
    nx,
    ny,
    aligned,
    count_s,
    lat_r,
    cot_r,
    gain_m,
    gain_l,
    gain_f,
    media_h,
    kvw_h,
    wq_h,
    out_h,
    up_h,
    down_h,
    hat_o,
    gkv_o,
    wkv_all,
    wq_all,
    o_all,
    cot_all,
    lat_all,
    mid_o,
    branch_o,
    attq_o,
    gq_o,
    gres_o,
    output_o,
    part_o,
    hat,
    kv,
    wkv_own,
    wbuf,
    wqb,
    o_v,
    up,
    down,
    media_t,
    q64,
    pexp,
    probs,
    stat,
    stat_in,
    o64,
    o_in,
    att64,
    g64,
    mid_ha,
    cot_ha,
    hid,
    gpre,
    ghid,
    sums,
    sums_in,
    load_sem,
    tile_sem,
    wload_sem,
    store_sem,
    a_send,
    a_recv,
    b_send,
    b_recv,
    q_send,
    q_recv,
    u_send,
    u_recv,
    pair_send,
    pair_recv,
    st_send,
    st_recv,
    ha_send,
    ha_recv,
    ct_send,
    ct_recv,
    lt_send,
    lt_recv,
    own_sem,
):
    me = Where(nx, ny)
    y, c = me.own["y"], me.own["c"]
    group = 2 * ny
    place = lax.axis_index("ha")
    lat = lat_r.shape[0]
    media_rows = media_h.shape[0]
    rows = hat.shape[0]
    feat = hat.shape[1]
    cols = q64.shape[-1]
    heads = cols // HEAD
    scale = HEAD ** (-0.5)
    partner = me.device("c", 1)

    def load(i, src, dst):
        return pltpu.make_async_copy(src, dst, load_sem.at[i])

    wkv_loads = (
        [
            load(0, kvw_h.at[1], wkv_own.at[..., pl.ds(0, cols)]),
            load(1, kvw_h.at[2], wkv_own.at[..., pl.ds(cols, cols)]),
        ]
        if aligned
        else [load(0, kvw_h, wkv_own)]
    )
    up_load, down_load = load(2, up_h, up), load(3, down_h, down)
    wq_load = load(4, wq_h.at[0], wqb.at[0])
    o_load = load(5, out_h, o_v.at[place])
    for copy in wkv_loads:
        copy.start()
    tile = media_t.shape[1]
    tiles = media_rows // tile

    def media_load(u):
        return pltpu.make_async_copy(
            media_h.at[pl.ds(pl.multiple_of(u * tile, tile), tile)],
            media_t.at[lax.rem(u, 2)],
            tile_sem.at[lax.rem(u, 2)],
        )

    media_load(0).start()
    wq_load.start()
    up_load.start()
    down_load.start()
    o_load.start()

    barrier = pltpu.get_barrier_semaphore()
    greeted = [me.device(a, k) for a in "cyxz" for k in range(1, me.size[a])]
    for k in range(1, ny):
        greeted.append(
            {"sa": lax.axis_index("sa"), "ha": me.at("y", k) * 2 + 1 - c}
        )
    for where in greeted:
        pl.semaphore_signal(barrier, inc=1, device_id=where, device_id_type=MESH)
    pl.semaphore_wait(barrier, len(greeted))

    def views(i):
        full = (pl.ds(0, ny), pl.ds(0, 2), i)
        return wkv_own.at[i], wkv_all.at[full]

    relay_a = Relay(me, *views(0), "yxz", a_send, a_recv)
    relay_b = Relay(me, *views(1), "yzx", b_send, b_recv)
    relay_q = Relay(me, wq_h.at[0], wq_all, "yxz", q_send, q_recv)
    relay_o = Relay(me, out_h, o_all, "yx", u_send, u_recv)
    gather_cot = Gather(me, cot_r, cot_all, "yzxc", ct_send, ct_recv, own_sem.at[0])
    gather_lat = Gather(
        me,
        hat.at[pl.ds(media_rows, lat)],
        lat_all,
        "zyxc",
        lt_send,
        lt_recv,
        own_sem.at[1],
    )

    def pair_copy(i, src, dst):
        return pltpu.make_async_remote_copy(
            src_ref=src,
            dst_ref=dst,
            send_sem=pair_send.at[i],
            recv_sem=pair_recv.at[i],
            device_id=partner,
            device_id_type=MESH,
        )

    def ha_copies(base, source, target):
        out = []
        for k in range(1, group):
            there = lax.rem(place + k, group)
            out.append(
                pltpu.make_async_remote_copy(
                    src_ref=source(there),
                    dst_ref=target(k),
                    send_sem=ha_send.at[base, k - 1],
                    recv_sem=ha_recv.at[base, k - 1],
                    device_id={"sa": lax.axis_index("sa"), "ha": there},
                    device_id_type=MESH,
                )
            )
        return out

    cot_copies = ha_copies(0, lambda there: cot_r, lambda k: cot_ha.at[place])
    mid_copies = ha_copies(1, lambda there: mid_ha.at[place], lambda k: mid_ha.at[place])
    gmid_copies = ha_copies(
        2, lambda there: sums.at[0, there], lambda k: sums_in.at[0, k - 1]
    )
    ffn_copies = ha_copies(
        3, lambda there: sums.at[1, there], lambda k: sums_in.at[1, k - 1]
    )

    for copy in wkv_loads:
        copy.wait()
    for relay in (relay_a, relay_b):
        relay.start("o")
        relay.start("y")
    for copy in cot_copies:
        copy.start()
    cot_ha[place] = cot_r[...]
    own_store = pltpu.make_async_copy(wkv_own, wkv_all.at[y, c], store_sem.at[0])
    own_store.start()

    @pl.loop(0, tiles)
    def _(u):
        @pl.when(u + 1 < tiles)
        def _():
            media_load(u + 1).start()

        media_load(u).wait()
        normed, unused = normalize(media_t[lax.rem(u, 2)].astype(F32))
        hat[pl.ds(pl.multiple_of(u * tile, tile), tile)] = (normed * gain_m[...]).astype(BF16)

    normed, unused = normalize(lat_r[...])
    hat[pl.ds(media_rows, lat)] = (normed * gain_l[...]).astype(BF16)
    hat_store = pltpu.make_async_copy(hat, hat_o, store_sem.at[1])
    hat_store.start()

    step = rows // 4

    def project(weights, piece):
        @pl.loop(0, 4)
        def _(u):
            part = pl.ds(pl.multiple_of(u * step, 8), step)
            w = weights[...].reshape(feat, 2 * cols)
            kv[piece, part] = dg(hat[part], w, 1, 0).astype(BF16)

    project(wkv_own, place)

    def weight_load(slot, ya, ca):
        return pltpu.make_async_copy(wkv_all.at[ya, ca], wbuf.at[slot], wload_sem.at[slot])

    relay_a.wait("o")
    relay_b.wait("o")
    weight_load(0, y, 1 - c).start()
    relay_a.next("y")
    relay_b.next("y")
    relay_q.start("o")
    relay_o.start("o")
    relay_q.start("y")
    gather_cot.start(0)
    weight_load(0, y, 1 - c).wait()
    project(wbuf.at[0], 2 * y + 1 - c)
    relay_a.next("x")
    relay_b.next("z")
    relay_q.next("y")
    relay_o.start("y")
    relay_a.next("z")
    relay_b.next("x")
    for k in range(1, ny):
        yk = me.at("y", ny - k)
        weight_load(k % 2, yk, c).start()
        if k == 1:
            relay_q.next("x")
        weight_load(k % 2, yk, c).wait()
        project(wbuf.at[k % 2], 2 * yk + c)
    relay_o.next("y")
    relay_a.wait("c")
    relay_b.wait("c")
    for k in range(1, ny):
        yk = me.at("y", ny - k)
        weight_load(k % 2, yk, 1 - c).start()
        if k == 1:
            relay_q.next("z")
        weight_load(k % 2, yk, 1 - c).wait()
        project(wbuf.at[k % 2], 2 * yk + 1 - c)
    relay_o.next("x")

    latent_hat = hat[pl.ds(media_rows, lat)]

    def wq_copy(slot, ya, ca):
        return pltpu.make_async_copy(
            wq_all.at[ya, ca], wqb.at[slot], wload_sem.at[2 + slot]
        )

    wq_load.wait()
    q64[place, c] = dg(latent_hat, wqb[0].reshape(feat, cols), 1, 0).astype(BF16)
    wq_store = pltpu.make_async_copy(
        wqb.at[0], wq_all.at[y, c], store_sem.at[2]
    )
    wq_store.start()
    relay_q.wait("o")
    wq_store.wait()
    relay_q.wait("c")
    order = [(y, 1 - c)]
    for k in range(1, ny):
        order += [(me.at("y", ny - k), c), (me.at("y", ny - k), 1 - c)]
    wq_copy(1, *order[0]).start()
    for i, (ya, ca) in enumerate(order):
        slot = (i + 1) % 2
        if i + 1 < len(order):
            wq_copy(1 - slot, *order[i + 1]).start()
        wq_copy(slot, ya, ca).wait()
        q64[2 * ya + ca, c] = dg(latent_hat, wqb[slot].reshape(feat, cols), 1, 0).astype(BF16)
    q_copy = pair_copy(
        0, q64.at[pl.ds(0, group), c], q64.at[pl.ds(0, group), c]
    )
    q_copy.start()

    lane = lax.broadcasted_iota(jnp.int32, (2 * lat, cols), 1)

    def inside(h):
        return jnp.logical_and(lane >= h * HEAD, lane < (h + 1) * HEAD)

    def spread(x):
        return jnp.concatenate(
            [jnp.where(inside(h), x, jnp.zeros_like(x)) for h in range(heads)], axis=0
        )

    def merge(x):
        total = jnp.where(inside(0), x[: 2 * lat], 0.0)
        for h in range(1, heads):
            total = total + jnp.where(inside(h), x[2 * lat * h : 2 * lat * (h + 1)], 0.0)
        return total

    tall = heads * 2 * lat
    limit = count_s[y] * PATCH - c * media_rows
    key = lax.broadcasted_iota(jnp.int32, (tall, rows), 1)
    half = lax.broadcasted_iota(jnp.int32, (tall, 128), 1) < 64
    q_copy.wait_recv()

    def stat_copy(a):
        return pltpu.make_async_remote_copy(
            src_ref=stat.at[a],
            dst_ref=stat_in.at[a],
            send_sem=st_send.at[a],
            recv_sem=st_recv.at[a],
            device_id=partner,
            device_id_type=MESH,
        )

    @pl.loop(0, group)
    def _(a):
        q_blk = spread(q64[a].reshape(2 * lat, cols))
        scores = dg(q_blk, kv[a, :, pl.ds(0, cols)], 1, 1) * scale
        usable = jnp.logical_or(key < limit, key >= media_rows)
        scores = jnp.where(usable, scores, NEG)
        top = jnp.max(scores, axis=-1, keepdims=True)
        value = jnp.exp(scores - top)
        pexp[a] = value
        total = jnp.sum(value, axis=-1, keepdims=True)
        stat[a] = jnp.where(half, top, total)
        stat_copy(a).start()

    relay_o.wait("o")
    relay_o.wait("c")
    o_loads = []
    for i, (ya, ca) in enumerate(order):
        o_loads.append(
            pltpu.make_async_copy(
                o_all.at[ya, ca], o_v.at[2 * ya + ca], load_sem.at[6 + i]
            )
        )
        o_loads[-1].start()

    gather_lat.start(0)
    gather_cot.next(0)

    @pl.loop(0, group)
    def _(a):
        stat_copy(a).wait_recv()
        top, total = stat[a, :, 0:1], stat[a, :, 64:65]
        top_in, total_in = stat_in[a, :, 0:1], stat_in[a, :, 64:65]
        top_all = jnp.maximum(top, top_in)
        mine = jnp.exp(top - top_all)
        denom = total * mine + total_in * jnp.exp(top_in - top_all)
        low = (pexp[a] * (mine / denom)).astype(BF16)
        probs[a] = low
        o64[a] = merge(dg(low, kv[a, :, pl.ds(cols, cols)], 1, 0)).reshape(2, lat, cols)

    o_copy = pair_copy(1, o64.at[pl.ds(0, group), 1 - c], o_in)
    o_copy.start()
    o_copy.wait_recv()
    o_load.wait()
    for copy in o_loads:
        copy.wait()
    branch = jnp.zeros((lat, feat), F32)
    for a in range(group):
        mine = o64[a, c] + o_in[a]
        att64[a, c] = mine
        low = mine.astype(BF16)
        attq_o[a, :, 0:cols] = low
        branch = branch + dg(low, o_v[a].reshape(cols, feat), 1, 0)
    att_copy = pair_copy(
        2, att64.at[pl.ds(0, group), c], att64.at[pl.ds(0, group), c]
    )
    residual = lat_r[...] + branch
    mid_norm, mid_inv = normalize(residual)
    mid_low = (mid_norm * gain_f[...]).astype(BF16)
    mid_ha[place] = mid_low
    for copy in mid_copies:
        copy.start()
    att_copy.start()
    mid_o[...] = mid_low
    part_o[...] = jnp.zeros_like(part_o)
    spot = lax.broadcasted_iota(jnp.int32, (1, feat), 1)
    squares = jnp.where(spot == 0, full_sum(residual * residual), 0.0)
    squares = squares + jnp.where(spot == 1, full_sum(branch * branch), 0.0)
    up_load.wait()
    down_load.wait()
    for copy in cot_copies:
        copy.wait_recv()
    all_cot = cot_ha[...].reshape(group * lat, feat)
    ghid[...] = dg(all_cot, down[...], 1, 1)
    gather_cot.next(1)
    for copy in mid_copies:
        copy.wait_recv()
    pre = dg(mid_ha[...].reshape(group * lat, feat), up[...], 1, 0)
    cdf = 0.5 * (1.0 + lax.erf(pre * (0.5**0.5)))
    slope = cdf + pre * (jnp.exp(-0.5 * pre * pre) * 0.3989422804014327)
    gpre[...] = (ghid[...] * slope).astype(BF16)
    hid[...] = (pre * cdf).astype(BF16)
    part = dg(gpre[...], up[...], 1, 1)
    ghid2 = part.reshape(group, lat, feat)
    sums[0] = ghid2.astype(BF16)
    for copy in gmid_copies:
        copy.start()
    sums_own = sums[0, place].astype(F32)
    part = dg(hid[...], down[...], 1, 0)
    sums[1] = part.reshape(group, lat, feat).astype(BF16)
    gather_lat.next(0)
    for copy in gmid_copies:
        copy.wait_recv()
    for copy in ffn_copies:
        copy.start()
    grad_mid = sums_own
    for k in range(1, group):
        grad_mid = grad_mid + sums_in[0, k - 1].astype(F32)
    grad_res = cot_r[...].astype(F32) + norm_grad(grad_mid * gain_f[...], mid_norm, mid_inv)
    gres_o[...] = grad_res
    grad_low = grad_res.astype(BF16)
    branch_o[...] = grad_low
    for a in range(group):
        g64[a, c] = dg(grad_low, o_v[a].reshape(cols, feat), 1, 1).astype(BF16)
    g_copy = pair_copy(3, g64.at[pl.ds(0, group), c], g64.at[pl.ds(0, group), c])
    g_copy.start()
    part_o[2:3] = jnp.sum(grad_mid * mid_norm, axis=0, keepdims=True)
    gather_cot.next(2)
    att_copy.wait_recv()
    o_copy.wait_send()
    g_copy.wait_recv()

    def gkv_store(a):
        return pltpu.make_async_copy(kv.at[a], gkv_o.at[a], st_send.at[a])

    for a in range(group):
        stat_copy(a).wait_send()

    @pl.loop(0, group)
    def _(a):
        q_blk = spread(q64[a].reshape(2 * lat, cols))
        g_blk = spread(g64[a].reshape(2 * lat, cols))
        att = att64[a].reshape(2 * lat, cols)
        inner = jnp.sum(
            g_blk.astype(F32) * jnp.concatenate([att] * heads, axis=0), axis=-1, keepdims=True
        )
        keys = kv[a, :, pl.ds(0, cols)]
        low = probs[a]
        grad = dg(g_blk, kv[a, :, pl.ds(cols, cols)], 1, 1)
        grad = (low.astype(F32) * (grad - inner)).astype(BF16)
        o64[a] = (merge(dg(grad, keys, 1, 0)) * scale).reshape(2, lat, cols)
        kv[a, :, pl.ds(0, cols)] = (dg(grad, q_blk, 0, 0) * scale).astype(BF16)
        kv[a, :, pl.ds(cols, cols)] = dg(low, g_blk, 0, 0).astype(BF16)
        gkv_store(a).start()

    gq_copy = pair_copy(4, o64.at[pl.ds(0, group), 1 - c], o_in)
    gq_copy.start()
    gather_lat.next(1)
    for copy in ffn_copies:
        copy.wait_recv()
    ffn = sums[1, place].astype(F32)
    for k in range(1, group):
        ffn = ffn + sums_in[1, k - 1].astype(F32)
    output_o[...] = residual + ffn
    squares = squares + jnp.where(spot == 2, full_sum(ffn * ffn), 0.0)
    part_o[3:4] = squares
    gq_copy.wait_recv()
    for a in range(group):
        low = (o64[a, c] + o_in[a]).astype(BF16)
        gq_o[a] = low
        attq_o[a, :, cols : 2 * cols] = low
    gather_cot.finish(3)
    gather_lat.next(2)
    gather_lat.finish(3)
    gather_cot.drain()
    gather_lat.drain()
    own_store.wait()
    hat_store.wait()
    for a in range(group):
        gkv_store(a).wait()
    for relay in (relay_a, relay_b, relay_q, relay_o):
        relay.drain()
    for copy in (q_copy, att_copy, g_copy, gq_copy):
        copy.wait_send()
    for copies in (cot_copies, mid_copies, gmid_copies, ffn_copies):
        for copy in copies:
            copy.wait_send()


def front(nx, ny, counts, latents, cot, gain_m, gain_l, gain_f, media, qkv, out_w, up, down):
    group = 2 * ny
    media_rows, feat = media.shape
    lat = latents.shape[0]
    rows = media_rows + lat
    cols = qkv.shape[-1]
    ff = up.shape[1]
    aligned = cols % 128 == 0
    tall = cols // HEAD * 2 * lat
    any_ = pl.BlockSpec(memory_space=pl.ANY)
    vm = pl.BlockSpec(memory_space=pltpu.VMEM)
    S = jax.ShapeDtypeStruct
    V = pltpu.VMEM
    D = pltpu.SemaphoreType.DMA
    every = (NZ, nx, ny, 2, lat)
    part = (nx, 2, feat // (2 * nx))
    half = (2, nx, 2, feat // (4 * nx))
    o_part = (nx, cols // nx, feat)
    if aligned:
        wkv = qkv.reshape((3,) + half + (cols,))
    else:
        wkv = jnp.concatenate([qkv[1], qkv[2]], axis=-1).reshape(half + (2 * cols,))
    wq = qkv.reshape((3,) + part + (cols,))
    spread4 = NZ + nx + ny + 2 - 4
    slots = Relay.slots(nx, ny)
    outs = (
        S((rows, feat), BF16),
        S((group, rows, 2 * cols), BF16),
        S((ny, 2) + half + (2 * cols,), BF16),
        S((ny, 2) + part + (cols,), BF16),
        S((ny, 2) + o_part, BF16),
        S(every + (feat,), BF16),
        S(every + (feat,), BF16),
        S((lat, feat), BF16),
        S((lat, feat), BF16),
        S((group, lat, 2 * cols), BF16),
        S((group, lat, cols), BF16),
        S((lat, feat), F32),
        S((lat, feat), F32),
        S((8, feat), F32),
    )
    return pl.pallas_call(
        functools.partial(front_kernel, nx, ny, aligned),
        out_shape=outs,
        in_specs=[pl.BlockSpec(memory_space=pltpu.SMEM)] + [vm] * 5 + [any_] * 6,
        out_specs=(any_,) * 7 + (vm,) * 7,
        scratch_shapes=[
            V((rows, feat), BF16),
            V((group, rows, 2 * cols), BF16),
            V(half + (2 * cols,), BF16),
            V((2,) + half + (2 * cols,), BF16),
            V((2,) + part + (cols,), BF16),
            V((group,) + o_part, BF16),
            V(up.shape, BF16),
            V(down.shape, BF16),
            V((2, 256, feat), BF16),
            V((group, 2, lat, cols), BF16),
            V((group, tall, rows), F32),
            V((group, tall, rows), BF16),
            V((group, tall, 128), F32),
            V((group, tall, 128), F32),
            V((group, 2, lat, cols), F32),
            V((group, lat, cols), F32),
            V((group, 2, lat, cols), F32),
            V((group, 2, lat, cols), BF16),
            V((group, lat, feat), BF16),
            V((group, lat, feat), BF16),
            V((group * lat, ff), BF16),
            V((group * lat, ff), BF16),
            V((group * lat, ff), F32),
            V((2, group, lat, feat), BF16),
            V((2, group - 1, lat, feat), BF16),
            D((6 + group,)),
            D((2,)),
            D((4,)),
            D((3,)),
            D((slots,)),
            D((slots,)),
            D((slots,)),
            D((slots,)),
            D((slots,)),
            D((slots,)),
            D((slots,)),
            D((slots,)),
            D((5,)),
            D((5,)),
            D((group,)),
            D((group,)),
            D((4, group - 1)),
            D((4, group - 1)),
            D((spread4,)),
            D((spread4,)),
            D((spread4,)),
            D((spread4,)),
            D((2,)),
        ],
        compiler_params=pltpu.CompilerParams(
            collective_id=2, has_side_effects=True, vmem_limit_bytes=67043328
        ),
        name="front",
    )(counts, latents, cot, gain_m, gain_l, gain_f, media, wkv, wq, out_w.reshape(o_part), up, down)

def shards(
    media_tokens,
    latents,
    frame_counts,
    gain_media,
    gain_latent,
    gain_ffn,
    qkv_weight,
    out_weight,
    up_weight,
    down_weight,
    cotangent,
):
    group = lax.axis_size("ha")
    width = media_tokens.shape[1]
    lat = latents.shape[0]
    cols = qkv_weight.shape[2]
    entry_total = float(lat * width * lax.axis_size("sa") * group)
    nx, ny = lax.axis_size("sa") // NZ, group // 2
    (
        hat,
        gkv,
        wkv_all,
        wq_all,
        unused,
        cot_all,
        lat_all,
        mid_hat,
        grad_branch,
        attq,
        grad_q,
        grad_residual,
        output,
        parts,
    ) = front(
        nx,
        ny,
        frame_counts,
        latents,
        cotangent,
        gain_media[None],
        gain_latent[None],
        gain_ffn[None],
        media_tokens,
        qkv_weight,
        out_weight,
        up_weight,
        down_weight,
    )
    kv, gm, hid, gp, mid_all, branch_all, attq_all, gains, grad_latents = tail(
        nx,
        ny,
        hat,
        gkv,
        wkv_all.reshape(group, width, 2 * cols),
        up_weight,
        down_weight,
        media_tokens,
        cot_all,
        wq_all.reshape(group, width, cols),
        gain_media[None],
        gain_latent[None],
        latents,
        grad_residual,
        grad_q,
        parts,
        mid_hat,
        grad_branch,
        attq,
    )
    cot_all = cot_all.reshape(-1, width)
    lat_all = lat_all.reshape(-1, width)
    kv = kv.reshape(width, 2 * cols)
    hid = hid.reshape(-1, hid.shape[-1])
    gp = gp.reshape(-1, gp.shape[-1])
    mid_all = mid_all.reshape(-1, width)
    branch_all = branch_all.reshape(-1, width)
    attq_all = attq_all.reshape(-1, 2 * cols)
    grad_media = gm.astype(F32)
    grad_out = dot("rc,rd->cd", attq_all[:, :cols], branch_all)
    grad_wq = dot("rd,re->de", lat_all, attq_all[:, cols:])
    grad_down = dot("rf,rd->fd", hid, cot_all)
    grad_up = dot("rd,rf->df", mid_all, gp)
    grad_kv = jnp.stack([kv[:, :cols], kv[:, cols:]]).astype(F32)
    gain_one, gain_two, gain_three = gains[0], gains[1], gains[2]
    square_sums = gains[3, :3]
    roots = jnp.sqrt(square_sums / entry_total)
    return (
        output,
        grad_media,
        grad_latents,
        gain_one,
        gain_two,
        gain_three,
        jnp.concatenate([grad_wq[None], grad_kv], axis=0),
        grad_out,
        grad_up,
        grad_down,
        roots[0],
        roots[1],
        roots[2],
    )


def solution(mesh):
    placed = (
        P(("sa", "ha"), None),
        P(("sa", "ha"), None),
        P("sa"),
        P(),
        P(),
        P(),
        P(None, None, "ha"),
        P("ha", None),
        P(None, "ha"),
        P("ha", None),
        P(("sa", "ha"), None),
    )
    return jax.shard_map(
        shards,
        mesh=mesh,
        in_specs=placed,
        out_specs=(
            P(("sa", "ha"), None),
            P(("sa", "ha"), None),
            P(("sa", "ha"), None),
            P(),
            P(),
            P(),
            P(None, None, "ha"),
            P("ha", None),
            P(None, "ha"),
            P("ha", None),
            P(),
            P(),
            P(),
        ),
        check_vma=False,
    )
```

```python
import functools

import jax
import jax.numpy as jnp
from jax import lax
from jax.experimental import pallas as pl
from jax.experimental.pallas import tpu as pltpu
from jax.sharding import PartitionSpec as P

HEAD = 96
PATCH = 256
EPS = 1e-05
NEG = -1000000000.0
F32 = jnp.float32
BF16 = jnp.bfloat16


def normalize(values):
    centered = values - jnp.mean(values, axis=-1, keepdims=True)
    inverse = lax.rsqrt(jnp.mean(centered * centered, axis=-1, keepdims=True) + EPS)
    return centered * inverse, inverse


def norm_grad(grad, normed, inverse):
    first = jnp.mean(grad, axis=-1, keepdims=True)
    second = jnp.mean(grad * normed, axis=-1, keepdims=True)
    return inverse * (grad - first - normed * second)


def dot(spec, a, b):
    return jnp.einsum(spec, a, b, preferred_element_type=F32)


MESH = pl.DeviceIdType.MESH
NZ = 4
CHUNKS = 6


def dg(a, b, ca, cb):
    return lax.dot_general(a, b, (((ca,), (cb,)), ((), ())), preferred_element_type=F32)


class Where:
    def __init__(self, nx, ny):
        self.nx, self.ny = nx, ny
        sa, ha = lax.axis_index("sa"), lax.axis_index("ha")
        self.own = {"z": sa // nx, "x": sa % nx, "y": ha // 2, "c": ha % 2}
        self.size = {"z": NZ, "x": nx, "y": ny, "c": 2}

    def at(self, axis, k):
        return lax.rem(self.own[axis] + k, self.size[axis])

    def device(self, axis, k):
        p = dict(self.own)
        p[axis] = self.at(axis, k)
        return {"sa": p["z"] * self.nx + p["x"], "ha": p["y"] * 2 + p["c"]}


def greet(me):
    barrier = pltpu.get_barrier_semaphore()
    count = 0
    for axis in "cyxz":
        for k in range(1, me.size[axis]):
            pl.semaphore_signal(
                barrier, inc=1, device_id=me.device(axis, k), device_id_type=MESH
            )
            count += 1
    pl.semaphore_wait(barrier, count)


class Gather:
    def __init__(self, me, own, buf, order, send, recv, local, done=""):
        self.me, self.own, self.buf, self.order = me, own, buf, order
        self.send, self.recv, self.local = send, recv, local
        self.done = done

    def slot(self, done):
        me = self.me
        return tuple(
            pl.ds(0, me.size[a]) if a in done else me.own[a] for a in "zxyc"
        )

    def keep(self):
        return pltpu.make_async_copy(
            self.own, self.buf.at[self.slot(self.done)], self.local
        )

    def copies(self, phase):
        done = self.done + self.order[:phase]
        axis = self.order[phase]
        first = sum(self.me.size[a] - 1 for a in self.order[:phase])
        here = self.buf.at[self.slot(done)]
        src = self.own if phase == 0 and self.own is not None else here
        return [
            pltpu.make_async_remote_copy(
                src_ref=src,
                dst_ref=here,
                send_sem=self.send.at[first + k - 1],
                recv_sem=self.recv.at[first + k - 1],
                device_id=self.me.device(axis, k),
                device_id_type=MESH,
            )
            for k in range(1, self.me.size[axis])
        ]

    def start(self, phase):
        if phase == 0 and self.own is not None:
            self.keep().start()
        for c in self.copies(phase):
            c.start()

    def finish(self, phase):
        if phase == 0 and self.own is not None:
            self.keep().wait()
        for c in self.copies(phase):
            c.wait_recv()

    def next(self, phase):
        self.finish(phase)
        self.start(phase + 1)

    def drain(self):
        for phase in range(len(self.order)):
            for c in self.copies(phase):
                c.wait_send()


class ColumnGather:
    def __init__(self, me, own, land, buf, order, send, recv, local):
        self.me, self.own, self.land, self.buf = me, own, land, buf
        self.send, self.recv, self.local = send, recv, local
        n = NZ + me.size["x"] - 2
        first = me.size["y"]
        self.rest = Gather(
            me, None, buf, order, send.at[pl.ds(first, n)], recv.at[pl.ds(first, n)], None, "yc"
        )

    @staticmethod
    def slots(nx, ny):
        return ny + NZ + nx - 2

    def over_y(self):
        me = self.me
        return [
            pltpu.make_async_remote_copy(
                src_ref=self.own.at[pl.ds(2 * me.at("y", k), 2)],
                dst_ref=self.land.at[me.own["y"]],
                send_sem=self.send.at[k - 1],
                recv_sem=self.recv.at[k - 1],
                device_id=me.device("y", k),
                device_id_type=MESH,
            )
            for k in range(1, me.size["y"])
        ]

    def keep_own(self):
        y = self.me.own["y"]
        return pltpu.make_async_copy(
            self.own.at[pl.ds(2 * y, 2)], self.land.at[y], self.local.at[0]
        )

    def over_c(self):
        me = self.me
        c, full = me.own["c"], pl.ds(0, me.size["y"])
        at = (me.own["z"], me.own["x"], full, c)
        i = me.size["y"] - 1
        return pltpu.make_async_remote_copy(
            src_ref=self.land.at[full, 1 - c],
            dst_ref=self.buf.at[at],
            send_sem=self.send.at[i],
            recv_sem=self.recv.at[i],
            device_id=me.device("c", 1),
            device_id_type=MESH,
        )

    def keep_c(self):
        me = self.me
        c, full = me.own["c"], pl.ds(0, me.size["y"])
        at = (me.own["z"], me.own["x"], full, c)
        return pltpu.make_async_copy(self.land.at[full, c], self.buf.at[at], self.local.at[1])

    def start(self):
        self.keep_own().start()
        for copy in self.over_y():
            copy.start()

    def to_c(self):
        self.keep_own().wait()
        for copy in self.over_y():
            copy.wait_recv()
        self.keep_c().start()
        self.over_c().start()

    def finish_c(self):
        self.keep_c().wait()
        self.over_c().wait_recv()

    def to_rest(self):
        self.finish_c()
        self.rest.start(0)

    def to_last(self):
        self.rest.next(0)

    def finish(self):
        self.rest.finish(1)

    def drain_c(self):
        for copy in self.over_y():
            copy.wait_send()
        self.over_c().wait_send()

    def drain(self):
        self.drain_c()
        self.rest.drain()


def tail_kernel(
    nx,
    ny,
    hat_h,
    gkv_h,
    wkv_h,
    up_h,
    down_h,
    media_h,
    cot_all,
    wq_h,
    gain_r,
    gain_l,
    lat_r,
    gres_r,
    gq_r,
    part_r,
    branch_r,
    unused_mid,
    unused_att,
    kv_o,
    gm_o,
    hid_o,
    gp_o,
    mid_all,
    att_all,
    branch_all,
    gq_all,
    gains_o,
    glat_o,
    hat,
    gkv,
    wkv,
    up,
    down,
    send_c,
    recv_c,
    acc,
    send_y,
    recv_y,
    send_x,
    recv_x,
    send_z,
    recv_z,
    red,
    gq_y,
    ql_out,
    ql_in,
    media_t,
    gm_t,
    mid_t,
    cot_t,
    hid_t,
    gp_t,
    wqb,
    gbuf,
    grecv,
    load_sem,
    tile_sem,
    out_sem,
    c_send,
    c_recv,
    y_send,
    y_recv,
    x_send,
    x_recv,
    z_send,
    z_recv,
    za_send,
    za_recv,
    xa_send,
    xa_recv,
    keep_sem,
    g_send,
    g_recv,
    mid_send,
    mid_recv,
    br_send,
    br_recv,
    aq_send,
    aq_recv,
    ql_send,
    ql_recv,
    at_send,
    at_recv,
    own_sem,
):
    me = Where(nx, ny)
    z, x, y, c = (me.own[a] for a in "zxyc")
    T = CHUNKS
    pieces = 2 * ny
    chunk = acc.shape[1]
    quarter = send_x.shape[2]
    sub = red.shape[1]
    feat = hat.shape[1]

    def load(i, src, dst):
        return pltpu.make_async_copy(src, dst, load_sem.at[i])

    hat_copy = load(0, hat_h, hat)
    wkv_copy = load(2, wkv_h, wkv)
    up_copy = load(3, up_h, up)
    down_copy = load(4, down_h, down)

    def gkv_load(k, parity):
        a = 2 * me.at("y", k) + parity
        return pltpu.make_async_copy(gkv_h.at[a], gkv.at[a], load_sem.at[6 + 2 * k + parity])

    hat_copy.start()
    for k in list(range(1, ny)) + [0]:
        gkv_load(k, 1 - c).start()
        gkv_load(k, c).start()
    greet(me)

    mid = Gather(me, None, mid_all, "xc", mid_send, mid_recv, None, "yz")
    att = Gather(me, None, att_all, "zx", at_send, at_recv, None, "yc")
    branch = Gather(me, branch_r, branch_all, "zxyc", br_send, br_recv, own_sem.at[1])

    gq = ColumnGather(me, gq_r, gq_y, gq_all, "zx", aq_send, aq_recv, own_sem.at[pl.ds(2, 2)])

    def ql_copy(k):
        return pltpu.make_async_remote_copy(
            src_ref=ql_out.at[me.at("y", k)],
            dst_ref=ql_in.at[k - 1],
            send_sem=ql_send.at[k - 1],
            recv_sem=ql_recv.at[k - 1],
            device_id=me.device("y", k),
            device_id_type=MESH,
        )

    mid.start(0)
    branch.start(0)
    gq.start()
    att.start(0)
    wq_load = load(5, wq_h, wqb)

    def grad_rows(k, t, parity):
        piece = 2 * me.at("y", k) + parity
        left = hat[:, pl.ds(pl.multiple_of(t * chunk, 128), chunk)]
        return dg(left, gkv[piece], 0, 0)

    def core_copy(t):
        return pltpu.make_async_remote_copy(
            src_ref=send_c.at[t],
            dst_ref=recv_c.at[t],
            send_sem=c_send.at[t],
            recv_sem=c_recv.at[t],
            device_id=me.device("c", 1),
            device_id_type=MESH,
        )

    def y_copy(k, t):
        return pltpu.make_async_remote_copy(
            src_ref=send_y.at[k - 1, t],
            dst_ref=recv_y.at[k - 1, t],
            send_sem=y_send.at[k - 1, t],
            recv_sem=y_recv.at[k - 1, t],
            device_id=me.device("y", k),
            device_id_type=MESH,
        )

    def x_copy(k, t):
        return pltpu.make_async_remote_copy(
            src_ref=send_x.at[k - 1, t],
            dst_ref=recv_x.at[k - 1, t],
            send_sem=x_send.at[k - 1, t],
            recv_sem=x_recv.at[k - 1, t],
            device_id=me.device("x", k),
            device_id_type=MESH,
        )

    def z_copy(k, t):
        return pltpu.make_async_remote_copy(
            src_ref=send_z.at[k - 1, t],
            dst_ref=recv_z.at[k - 1, t],
            send_sem=z_send.at[k - 1, t],
            recv_sem=z_recv.at[k - 1, t],
            device_id=me.device("z", k),
            device_id_type=MESH,
        )

    def za_copy(k, t):
        return pltpu.make_async_remote_copy(
            src_ref=red.at[t],
            dst_ref=kv_o.at[t, x * NZ + z],
            send_sem=za_send.at[k - 1, t],
            recv_sem=za_recv.at[k - 1, t],
            device_id=me.device("z", k),
            device_id_type=MESH,
        )

    def xa_copy(k, t):
        rows = kv_o.at[t, pl.ds(x * NZ, NZ)]
        return pltpu.make_async_remote_copy(
            src_ref=rows,
            dst_ref=rows,
            send_sem=xa_send.at[k - 1, t],
            recv_sem=xa_recv.at[k - 1, t],
            device_id=me.device("x", k),
            device_id_type=MESH,
        )

    def keep_copy(t):
        return pltpu.make_async_copy(red.at[t], kv_o.at[t, x * NZ + z], keep_sem.at[t])

    def latent_queries():
        wq_load.wait()
        for src in range(ny):
            total = dg(gq_y[src, 0], wqb[0], 1, 1) + dg(gq_y[src, 1], wqb[1], 1, 1)
            ql_out[src] = total.astype(BF16)
        for k in range(1, ny):
            ql_copy(k).start()

    hat_copy.wait()
    lag = 2
    steps = ny * T

    @pl.loop(0, steps + lag)
    def _(j):
        @pl.when(j < steps)
        def _():
            k, t = lax.rem(1 + j // T, ny), lax.rem(j, T)

            @pl.when(t == 0)
            def _():
                gkv_load(k, 1 - c).wait()
                gkv_load(k, c).wait()

            @pl.when(j == 3)
            def _():
                for copy in (wkv_copy, up_copy, down_copy, wq_load):
                    copy.start()

            @pl.when(j >= T)
            def _():
                core_copy(t).wait_send()

            send_c[t] = grad_rows(k, t, 1 - c).astype(BF16)
            core_copy(t).start()

        @pl.when(j >= lag)
        def _():
            i = j - lag
            k, t = lax.rem(1 + i // T, ny), lax.rem(i, T)
            mine = grad_rows(k, t, c)
            core_copy(t).wait_recv()
            mine = mine + recv_c[t].astype(F32)

            @pl.when(i >= steps - T)
            def _():
                acc[t] = mine

            @pl.when(i < steps - T)
            def _():
                for step in range(1, ny):

                    @pl.when(i // T == step - 1)
                    def _():
                        send_y[step - 1, t] = mine.astype(BF16)
                        y_copy(step, t).start()

        @pl.when(j == 3)
        def _():
            gq.to_c()

        @pl.when(j == 5)
        def _():
            branch.next(0)
            latent_queries()

        @pl.when(j == 9)
        def _():
            mid.next(0)
            gq.to_rest()

    for t in range(T):
        core_copy(t).wait_send()
    wkv_copy.wait()
    up_copy.wait()
    down_copy.wait()

    gbuf[...] = part_r[...]
    media_rows = media_h.shape[0]
    tile = media_t.shape[1]
    n_media = media_rows // tile

    def media_load(u):
        return pltpu.make_async_copy(
            media_h.at[pl.ds(pl.multiple_of(u * tile, tile), tile)],
            media_t.at[lax.rem(u, 2)],
            tile_sem.at[lax.rem(u, 2)],
        )

    def gm_store(u):
        return pltpu.make_async_copy(
            gm_t, gm_o.at[pl.ds(pl.multiple_of(u * tile, tile), tile)], out_sem.at[0]
        )

    def media_tile(u):
        @pl.when(u + 1 < n_media)
        def _():
            media_load(u + 1).start()

        rows = pl.ds(pl.multiple_of(u * tile, tile), tile)
        total = dg(gkv[0, rows], wkv[0], 1, 1)
        for a in range(1, pieces):
            total = total + dg(gkv[a, rows], wkv[a], 1, 1)
        media_load(u).wait()
        values = media_t[lax.rem(u, 2)].astype(F32)
        normed, inverse = normalize(values)
        gbuf[0:1] = gbuf[0:1] + jnp.sum(total * normed, axis=0, keepdims=True)
        result = norm_grad(total * gain_r[...], normed, inverse)

        @pl.when(u >= 1)
        def _():
            gm_store(u - 1).wait()

        gm_t[...] = result.astype(BF16)
        gm_store(u).start()

    xt = mid_t.shape[1]
    n_ffn = NZ * (nx // xt)

    def rows_load(u):
        zz, xx = u // (nx // xt), lax.rem(u, nx // xt) * xt
        b = lax.rem(u, 2)
        return [
            pltpu.make_async_copy(
                mid_all.at[zz, pl.ds(xx, xt)], mid_t.at[b], tile_sem.at[2 + b]
            ),
            pltpu.make_async_copy(
                cot_all.at[zz, pl.ds(xx, xt)], cot_t.at[b], tile_sem.at[4 + b]
            ),
        ]

    def ffn_store(u):
        return [
            pltpu.make_async_copy(hid_t, hid_o.at[u], out_sem.at[1]),
            pltpu.make_async_copy(gp_t, gp_o.at[u], out_sem.at[2]),
        ]

    def ffn_tile(u):
        @pl.when(u + 1 < n_ffn)
        def _():
            for copy in rows_load(u + 1):
                copy.start()

        for copy in rows_load(u):
            copy.wait()

        @pl.when(u >= 1)
        def _():
            for copy in ffn_store(u - 1):
                copy.wait()

        b = lax.rem(u, 2)
        mid_rows = mid_t[b].reshape(-1, feat)
        cot_rows = cot_t[b].reshape(-1, feat)
        width = up.shape[1] // 3
        for part in range(3):
            cols = pl.ds(part * width, width)
            pre = dg(mid_rows, up[:, cols], 1, 0)
            grad = dg(cot_rows, down[cols, :], 1, 1)
            cdf = 0.5 * (1.0 + lax.erf(pre * (0.5**0.5)))
            slope = cdf + pre * (jnp.exp(-0.5 * pre * pre) * 0.3989422804014327)
            hid_t[:, cols] = (pre * cdf).astype(BF16)
            gp_t[:, cols] = (grad * slope).astype(BF16)
        for copy in ffn_store(u):
            copy.start()

    def latent_rows():
        rows = pl.ds(media_rows, lat_r.shape[0])
        total = dg(gkv[0, rows], wkv[0], 1, 1)
        for a in range(1, pieces):
            total = total + dg(gkv[a, rows], wkv[a], 1, 1)
        total = total + ql_out[y].astype(F32)
        for k in range(1, ny):
            ql_copy(k).wait_recv()
            total = total + ql_in[k - 1].astype(F32)
        normed, inverse = normalize(lat_r[...])
        gbuf[1:2] = jnp.sum(total * normed, axis=0, keepdims=True)
        glat_o[...] = gres_r[...] + norm_grad(total * gain_l[...], normed, inverse)

    def step_y(t):
        for k in range(1, ny):
            y_copy(k, t).wait_recv()
        whole = acc[t]
        for k in range(1, ny):
            whole = whole + recv_y[k - 1, t].astype(F32)
        acc[t] = whole
        for k in range(1, nx):
            there = pl.ds(pl.multiple_of(me.at("x", k) * quarter, 8), quarter)
            send_x[k - 1, t] = acc[t, there].astype(BF16)
            x_copy(k, t).start()

    def step_x(t):
        for k in range(1, nx):
            x_copy(k, t).wait_recv()
        here = pl.ds(pl.multiple_of(x * quarter, 8), quarter)
        whole = acc[t, here]
        for k in range(1, nx):
            whole = whole + recv_x[k - 1, t].astype(F32)
        acc[t, here] = whole
        for k in range(1, NZ):
            there = pl.ds(pl.multiple_of(x * quarter + me.at("z", k) * sub, 8), sub)
            send_z[k - 1, t] = acc[t, there].astype(BF16)
            z_copy(k, t).start()

    def step_z(t):
        for k in range(1, NZ):
            z_copy(k, t).wait_recv()
        whole = acc[t, pl.ds(pl.multiple_of(x * quarter + z * sub, 8), sub)]
        for k in range(1, NZ):
            whole = whole + recv_z[k - 1, t].astype(F32)
        red[t] = whole.astype(BF16)
        keep_copy(t).start()
        for k in range(1, NZ):
            za_copy(k, t).start()

    def step_za(t):
        keep_copy(t).wait()
        for k in range(1, NZ):
            za_copy(k, t).wait_recv()
        for k in range(1, nx):
            xa_copy(k, t).start()

    def step_xa(t):
        for k in range(1, nx):
            xa_copy(k, t).wait_recv()

    def comm(s):
        for lag_s, action in ((0, step_y), (1, step_x), (2, step_z), (3, step_za), (5, step_xa)):
            ready = jnp.logical_and(s >= lag_s, s < lag_s + 2 * T)

            @pl.when(jnp.logical_and(ready, lax.rem(s + lag_s, 2) == 0))
            def _():
                action((s - lag_s) // 2)

    def gain_copies(axis, base):
        return [
            pltpu.make_async_remote_copy(
                src_ref=gbuf,
                dst_ref=grecv.at[base + k - 1],
                send_sem=g_send.at[base + k - 1],
                recv_sem=g_recv.at[base + k - 1],
                device_id=me.device(axis, k),
                device_id_type=MESH,
            )
            for k in range(1, me.size[axis])
        ]

    def gain_base(axis):
        return sum(me.size[a] - 1 for a in "cyxz"[: "cyxz".index(axis)])

    def gain_start(axis):
        for copy in gain_copies(axis, gain_base(axis)):
            copy.start()

    def gain_finish(axis):
        base = gain_base(axis)
        for copy in gain_copies(axis, base):
            copy.wait_send()
            copy.wait_recv()
        total = gbuf[...]
        for k in range(1, me.size[axis]):
            total = total + grecv[base + k - 1]
        gbuf[...] = total

    media_load(0).start()
    per = n_ffn // 4

    @pl.loop(0, max(2 * T + 4, n_media + 15))
    def _(s):
        comm(s)

        @pl.when(s == 0)
        def _():
            att.next(0)

        @pl.when(s < n_media)
        def _():
            media_tile(s)

        @pl.when(s == n_media)
        def _():
            gm_store(n_media - 1).wait()
            latent_rows()
            gain_start("c")
            mid.finish(1)
            for copy in rows_load(0):
                copy.start()

        @pl.when(s == n_media + 1)
        def _():
            gain_finish("c")
            gain_start("x")

        @pl.when(jnp.logical_and(s > n_media, s < n_media + 5))
        def _():
            @pl.loop(0, per)
            def _(u):
                ffn_tile((s - n_media - 1) * per + u)

        @pl.when(s == 6)
        def _():
            gq.to_last()

        @pl.when(s == n_media + 4)
        def _():
            gain_finish("x")
            gain_start("z")

        @pl.when(s == n_media + 6)
        def _():
            for copy in ffn_store(n_ffn - 1):
                copy.wait()
            branch.next(1)

        @pl.when(s == n_media + 8)
        def _():
            gain_finish("z")
            gain_start("y")

        @pl.when(s == n_media + 14)
        def _():
            branch.next(2)

    gain_finish("y")
    gains_o[...] = gbuf[...]
    branch.finish(3)
    gq.finish()
    att.finish(1)
    att.drain()
    mid.drain()
    branch.drain()
    gq.drain()
    for k in range(1, ny):
        ql_copy(k).wait_send()

    @pl.loop(0, T)
    def _(t):
        for k in range(1, ny):
            y_copy(k, t).wait_send()
        for k in range(1, nx):
            x_copy(k, t).wait_send()
            xa_copy(k, t).wait_send()
        for k in range(1, NZ):
            z_copy(k, t).wait_send()
            za_copy(k, t).wait_send()


def tail(
    nx, ny, hat, gkv, wkv, up, down, media, cot_all, wq, gain_m, gain_l, lats, gres, gq, parts, branch, mid_all, att_all
):
    T = CHUNKS
    rows, feat = hat.shape
    pieces, _, two = gkv.shape
    lat = branch.shape[0]
    ff = up.shape[1]
    blocks = nx * NZ
    chunk = feat // T
    sub = chunk // blocks
    xt = 256 // (lat * pieces)
    tile_rows = xt * pieces * lat
    tiles = NZ * nx // xt
    any_ = pl.BlockSpec(memory_space=pl.ANY)
    vm = pl.BlockSpec(memory_space=pltpu.VMEM)
    S = jax.ShapeDtypeStruct
    every = (NZ, nx, ny, 2, lat)
    V = pltpu.VMEM
    D = pltpu.SemaphoreType.DMA
    spread4 = NZ + nx + ny + 2 - 4
    media_rows = media.shape[0]
    outs = (
        S((T, blocks, sub, two), BF16),
        S((media_rows, feat), BF16),
        S((tiles, tile_rows, ff), BF16),
        S((tiles, tile_rows, ff), BF16),
        S(every + (feat,), BF16),
        S(every + (two // 2,), BF16),
        S(every + (feat,), BF16),
        S(every + (two // 2,), BF16),
        S((8, feat), F32),
        S(gres.shape, F32),
    )
    return pl.pallas_call(
        functools.partial(tail_kernel, nx, ny),
        out_shape=outs,
        in_specs=[any_] * 8 + [vm] * 7 + [any_] * 2,
        out_specs=(any_,) * 8 + (vm,) * 2,
        input_output_aliases={15: 4, 16: 5},
        scratch_shapes=[
            V(hat.shape, BF16),
            V(gkv.shape, BF16),
            V(wkv.shape, BF16),
            V(up.shape, BF16),
            V(down.shape, BF16),
            V((T, chunk, two), BF16),
            V((T, chunk, two), BF16),
            V((T, chunk, two), F32),
            V((ny - 1, T, chunk, two), BF16),
            V((ny - 1, T, chunk, two), BF16),
            V((nx - 1, T, NZ * sub, two), BF16),
            V((nx - 1, T, NZ * sub, two), BF16),
            V((NZ - 1, T, sub, two), BF16),
            V((NZ - 1, T, sub, two), BF16),
            V((T, sub, two), BF16),
            V((ny, 2, lat, two // 2), BF16),
            V((ny, lat, feat), BF16),
            V((ny - 1, lat, feat), BF16),
            V((2, 256, feat), BF16),
            V((256, feat), BF16),
            V((2, xt, ny, 2, lat, feat), BF16),
            V((2, xt, ny, 2, lat, feat), BF16),
            V((tile_rows, ff), BF16),
            V((tile_rows, ff), BF16),
            V(wq.shape, BF16),
            V((8, feat), F32),
            V((spread4, 8, feat), F32),
            D((6 + pieces,)),
            D((6,)),
            D((3,)),
            D((T,)),
            D((T,)),
            D((ny - 1, T)),
            D((ny - 1, T)),
            D((nx - 1, T)),
            D((nx - 1, T)),
            D((NZ - 1, T)),
            D((NZ - 1, T)),
            D((NZ - 1, T)),
            D((NZ - 1, T)),
            D((nx - 1, T)),
            D((nx - 1, T)),
            D((T,)),
            D((spread4,)),
            D((spread4,)),
            D((spread4,)),
            D((spread4,)),
            D((spread4,)),
            D((spread4,)),
            D((ColumnGather.slots(nx, ny),)),
            D((ColumnGather.slots(nx, ny),)),
            D((ny - 1,)),
            D((ny - 1,)),
            D((spread4,)),
            D((spread4,)),
            D((4,)),
        ],
        compiler_params=pltpu.CompilerParams(
            collective_id=3, has_side_effects=True, vmem_limit_bytes=67043328
        ),
        name="tail",
    )(
        hat, gkv, wkv, up, down, media, cot_all, wq, gain_m, gain_l, lats, gres, gq, parts, branch, mid_all, att_all
    )


def full_sum(x):
    return jnp.sum(jnp.sum(x, axis=1, keepdims=True), axis=0, keepdims=True)


class Relay:
    def __init__(self, me, own, buf, order, send, recv):
        self.me, self.own, self.buf, self.order = me, own, buf, order
        self.send, self.recv = send, recv
        ny, nx = me.size["y"] - 1, me.size["x"] - 1
        sizes = {"o": 1, "y": ny, "x": ny * nx, "z": ny, "c": ny}
        self.base, total = {}, 0
        for a in "oyxzc":
            self.base[a] = total
            total += sizes[a]

    @staticmethod
    def slots(nx, ny):
        return 1 + 3 * (ny - 1) + (ny - 1) * (nx - 1)

    def part(self, done):
        me = self.me
        index = []
        if "x" in self.order:
            index.append(pl.ds(0, me.size["x"]) if "x" in done else me.own["x"])
        if "z" in self.order:
            index.append(pl.ds(0, 2) if "z" in done else lax.rem(me.own["z"], 2))
        return tuple(index)

    def copies(self, phase):
        me, buf = self.me, self.buf
        y, c = me.own["y"], me.own["c"]
        out = []

        def add(src, dst, where):
            i = self.base[phase] + len(out)
            out.append(
                pltpu.make_async_remote_copy(
                    src_ref=src,
                    dst_ref=dst,
                    send_sem=self.send.at[i],
                    recv_sem=self.recv.at[i],
                    device_id=where,
                    device_id_type=MESH,
                )
            )

        if phase == "o":
            add(self.own, buf.at[y, c], me.device("c", 1))
            return out
        done = self.order[1 : self.order.index(phase)] if phase in "xz" else ""
        for k in range(1, me.size["y"]):
            if phase == "y":
                at = self.part("")
                src = self.own.at[at] if at else self.own
                add(src, buf.at[(y, c) + at], me.device("y", k))
                continue
            yk = me.at("y", me.size["y"] - k)
            if phase == "c":
                add(buf.at[yk, c], buf.at[yk, c], me.device("c", 1))
                continue
            ref = buf.at[(yk, c) + self.part(done)]
            if phase == "z":
                add(ref, ref, me.device("z", 1 - 2 * lax.rem(me.own["z"], 2) + NZ))
            else:
                for j in range(1, me.size["x"]):
                    add(ref, ref, me.device("x", j))
        return out

    def start(self, phase):
        for copy in self.copies(phase):
            copy.start()

    def wait(self, phase):
        for copy in self.copies(phase):
            copy.wait_recv()

    def next(self, phase):
        self.wait(phase)
        at = self.order.index(phase) + 1
        self.start(self.order[at] if at < len(self.order) else "c")

    def drain(self):
        for phase in "o" + self.order + "c":
            for copy in self.copies(phase):
                copy.wait_send()


def front_kernel(
    nx,
    ny,
    aligned,
    count_s,
    lat_r,
    cot_r,
    gain_m,
    gain_l,
    gain_f,
    media_h,
    kvw_h,
    wq_h,
    out_h,
    up_h,
    down_h,
    hat_o,
    gkv_o,
    wkv_all,
    wq_o,
    o_all,
    cot_all,
    lat_all,
    att_all,
    mid_all,
    branch_o,
    gq_o,
    gres_o,
    output_o,
    part_o,
    hat,
    kv,
    wkv_own,
    wbuf,
    wq_v,
    o_v,
    up,
    down,
    media_t,
    lat_y,
    q_y,
    q64,
    pexp,
    probs,
    stat,
    stat_in,
    o64,
    o_in,
    att64,
    att_low,
    att_y,
    g64,
    mid_ha,
    cot_ha,
    hid,
    gpre,
    ghid,
    sums,
    sums_in,
    load_sem,
    tile_sem,
    wload_sem,
    store_sem,
    w_send,
    w_recv,
    u_send,
    u_recv,
    qy_send,
    qy_recv,
    pair_send,
    pair_recv,
    st_send,
    st_recv,
    ha_send,
    ha_recv,
    ct_send,
    ct_recv,
    lt_send,
    lt_recv,
    at_send,
    at_recv,
    md_send,
    md_recv,
    own_sem,
):
    me = Where(nx, ny)
    y, c = me.own["y"], me.own["c"]
    group = 2 * ny
    place = lax.axis_index("ha")
    lat = lat_r.shape[0]
    media_rows = media_h.shape[0]
    rows = hat.shape[0]
    feat = hat.shape[1]
    cols = q64.shape[-1]
    heads = cols // HEAD
    scale = HEAD ** (-0.5)
    partner = me.device("c", 1)
    n_w = wkv_own.shape[0]
    n_o = o_v.shape[1]

    def load(i, src, dst):
        return pltpu.make_async_copy(src, dst, load_sem.at[i])

    wkv_loads = (
        [
            load(0, kvw_h.at[1], wkv_own.at[..., pl.ds(0, cols)]),
            load(1, kvw_h.at[2], wkv_own.at[..., pl.ds(cols, cols)]),
        ]
        if aligned
        else [load(0, kvw_h, wkv_own)]
    )
    up_load, down_load = load(2, up_h, up), load(3, down_h, down)
    wq_load = load(4, wq_h.at[0], wq_v.at[c])
    o_load = load(5, out_h, o_v.at[place])
    for copy in wkv_loads:
        copy.start()
    tile = media_t.shape[1]
    tiles = media_rows // tile

    def media_load(u):
        return pltpu.make_async_copy(
            media_h.at[pl.ds(pl.multiple_of(u * tile, tile), tile)],
            media_t.at[lax.rem(u, 2)],
            tile_sem.at[lax.rem(u, 2)],
        )

    media_load(0).start()
    wq_load.start()
    down_load.start()
    up_load.start()
    o_load.start()

    barrier = pltpu.get_barrier_semaphore()
    greeted = [me.device(a, k) for a in "cyxz" for k in range(1, me.size[a])]
    for k in range(1, ny):
        greeted.append({"sa": lax.axis_index("sa"), "ha": me.at("y", k) * 2 + 1 - c})
    for where in greeted:
        pl.semaphore_signal(barrier, inc=1, device_id=where, device_id_type=MESH)
    pl.semaphore_wait(barrier, len(greeted))

    both = (pl.ds(0, ny), pl.ds(0, 2))
    relays = [
        Relay(
            me,
            wkv_own.at[i],
            wkv_all.at[both + (i,)],
            ("yxz", "yzx")[i % 2],
            w_send.at[i],
            w_recv.at[i],
        )
        for i in range(n_w)
    ]
    o_relays = [
        Relay(
            me,
            out_h.at[i],
            o_all.at[both + (i,)],
            "yx" if i == 0 else "yz",
            u_send.at[i],
            u_recv.at[i],
        )
        for i in range(n_o)
    ]
    gather_cot = Gather(me, cot_r, cot_all, "zyxc", ct_send, ct_recv, own_sem.at[0])
    own_lat = hat.at[pl.ds(media_rows, lat)]
    gather_lat = Gather(me, own_lat, lat_all, "yzxc", lt_send, lt_recv, own_sem.at[1])
    gather_att = ColumnGather(
        me, att_low, att_y, att_all, "xz", at_send, at_recv, own_sem.at[pl.ds(2, 2)]
    )

    def remote(src, dst, send, recv, where):
        return pltpu.make_async_remote_copy(
            src_ref=src,
            dst_ref=dst,
            send_sem=send,
            recv_sem=recv,
            device_id=where,
            device_id_type=MESH,
        )

    def pair_copy(i, src, dst):
        return remote(src, dst, pair_send.at[i], pair_recv.at[i], partner)

    def ha_copies(base, source, target):
        out = []
        for k in range(1, group):
            there = lax.rem(place + k, group)
            out.append(
                remote(
                    source(there),
                    target(k),
                    ha_send.at[base, k - 1],
                    ha_recv.at[base, k - 1],
                    {"sa": lax.axis_index("sa"), "ha": there},
                )
            )
        return out

    cot_copies = ha_copies(0, lambda there: cot_r, lambda k: cot_ha.at[place])
    mid_copies = ha_copies(1, lambda there: mid_ha.at[y, c], lambda k: mid_ha.at[y, c])
    gmid_copies = ha_copies(2, lambda there: sums.at[0, there], lambda k: sums_in.at[0, k - 1])
    ffn_copies = ha_copies(3, lambda there: sums.at[1, there], lambda k: sums_in.at[1, k - 1])
    lat_copies = [
        remote(own_lat, lat_y.at[y], qy_send.at[0, k - 1], qy_recv.at[0, k - 1], me.device("y", k))
        for k in range(1, ny)
    ]
    back_copies = [
        remote(
            q_y.at[me.at("y", k)],
            q64.at[pl.ds(2 * y, 2), c],
            qy_send.at[1, k - 1],
            qy_recv.at[1, k - 1],
            me.device("y", k),
        )
        for k in range(1, ny)
    ]
    wq_copy = pair_copy(5, wq_h.at[0], wq_v.at[c])

    gather_cot.start(0)
    normed, unused = normalize(lat_r[...])
    low = (normed * gain_l[...]).astype(BF16)
    hat[pl.ds(media_rows, lat)] = low
    lat_y[y] = low
    for copy in lat_copies:
        copy.start()
    for copy in wkv_loads:
        copy.wait()
    for relay in relays:
        relay.start("o")
        relay.start("y")
    wq_copy.start()
    for relay in o_relays:
        relay.start("o")
    cot_ha[place] = cot_r[...]
    own_store = pltpu.make_async_copy(wkv_own, wkv_all.at[y, c], store_sem.at[0])
    own_store.start()

    @pl.loop(0, tiles)
    def _(u):
        @pl.when(u + 1 < tiles)
        def _():
            media_load(u + 1).start()

        media_load(u).wait()
        normed, unused = normalize(media_t[lax.rem(u, 2)].astype(F32))
        hat[pl.ds(pl.multiple_of(u * tile, tile), tile)] = (normed * gain_m[...]).astype(BF16)

    hat_store = pltpu.make_async_copy(hat, hat_o, store_sem.at[1])
    hat_store.start()
    step = rows // 4

    def project(weights, piece):
        @pl.loop(0, 4)
        def _(u):
            part = pl.ds(pl.multiple_of(u * step, 8), step)
            w = weights[...].reshape(feat, 2 * cols)
            kv[piece, part] = dg(hat[part], w, 1, 0).astype(BF16)

    def weight_load(slot, ya, ca):
        return pltpu.make_async_copy(wkv_all.at[ya, ca], wbuf.at[slot], wload_sem.at[slot])

    project(wkv_own, place)
    for relay in relays:
        relay.wait("o")
    weight_load(0, y, 1 - c).start()
    relays[0].next("y")
    weight_load(0, y, 1 - c).wait()
    project(wbuf.at[0], 2 * y + 1 - c)
    relays[1].next("y")
    relays[0].next("x")
    wq_load.wait()
    wq_copy.wait_recv()
    for copy in lat_copies:
        copy.wait_recv()
    wq_store = pltpu.make_async_copy(wq_v, wq_o, store_sem.at[2])
    wq_store.start()
    all_lat = lat_y[...].reshape(ny * lat, feat)
    for ca in range(2):
        w = wq_v[ca].reshape(feat, cols)
        q_y[pl.ds(0, ny), ca] = dg(all_lat, w, 1, 0).astype(BF16).reshape(ny, lat, cols)
    q64[2 * y, c] = q_y[y, 0]
    q64[2 * y + 1, c] = q_y[y, 1]
    for copy in back_copies:
        copy.start()
    relays[2].next("y")
    for relay in o_relays:
        relay.start("y")
    for copy in cot_copies:
        copy.start()
    gather_lat.start(0)
    gather_cot.next(0)
    relays[1].next("z")
    relays[3].next("y")
    for copy in back_copies:
        copy.wait_recv()
    q_copy = pair_copy(0, q64.at[pl.ds(0, group), c], q64.at[pl.ds(0, group), c])
    q_copy.start()
    relays[2].next("x")

    lane = lax.broadcasted_iota(jnp.int32, (2 * lat, cols), 1)

    def inside(h):
        return jnp.logical_and(lane >= h * HEAD, lane < (h + 1) * HEAD)

    def spread(x):
        return jnp.concatenate(
            [jnp.where(inside(h), x, jnp.zeros_like(x)) for h in range(heads)], axis=0
        )

    def merge(x):
        total = jnp.where(inside(0), x[: 2 * lat], 0.0)
        for h in range(1, heads):
            total = total + jnp.where(inside(h), x[2 * lat * h : 2 * lat * (h + 1)], 0.0)
        return total

    tall = heads * 2 * lat
    limit = count_s[y] * PATCH - c * media_rows
    key = lax.broadcasted_iota(jnp.int32, (tall, rows), 1)
    half = lax.broadcasted_iota(jnp.int32, (tall, 128), 1) < 64

    def stat_copy(a):
        return remote(stat.at[a], stat_in.at[a], st_send.at[a], st_recv.at[a], partner)

    def attend(ya):
        @pl.loop(0, 2)
        def _(ca):
            a = 2 * ya + ca
            q_blk = spread(q64[a].reshape(2 * lat, cols))
            scores = dg(q_blk, kv[a, :, pl.ds(0, cols)], 1, 1) * scale
            usable = jnp.logical_or(key < limit, key >= media_rows)
            scores = jnp.where(usable, scores, NEG)
            top = jnp.max(scores, axis=-1, keepdims=True)
            value = jnp.exp(scores - top)
            pexp[a] = value
            total = jnp.sum(value, axis=-1, keepdims=True)
            stat[a] = jnp.where(half, top, total)
            stat_copy(a).start()

    def settle(ya):
        @pl.loop(0, 2)
        def _(ca):
            a = 2 * ya + ca
            stat_copy(a).wait_recv()
            top, total = stat[a, :, 0:1], stat[a, :, 64:65]
            top_in, total_in = stat_in[a, :, 0:1], stat_in[a, :, 64:65]
            top_all = jnp.maximum(top, top_in)
            mine = jnp.exp(top - top_all)
            denom = total * mine + total_in * jnp.exp(top_in - top_all)
            low = (pexp[a] * (mine / denom)).astype(BF16)
            probs[a] = low
            o64[a] = merge(dg(low, kv[a, :, pl.ds(cols, cols)], 1, 0)).reshape(2, lat, cols)

    q_copy.wait_recv()
    attend(y)
    relays[0].next("z")
    relays[3].next("z")
    settle(y)
    relays[1].next("x")
    relays[2].next("z")
    relays[3].next("x")
    for k in range(1, ny):
        yk = me.at("y", ny - k)
        weight_load(1, yk, c).start()
        if k == 1:
            for relay in o_relays:
                relay.next("y")
        weight_load(1, yk, c).wait()
        project(wbuf.at[1], 2 * yk + c)
        if k == 1:
            for relay in relays:
                relay.wait("c")
        weight_load(0, yk, 1 - c).start()
        if k == 1:
            for relay in o_relays:
                relay.next(relay.order[1])
            gather_lat.next(0)
            gather_cot.next(1)
        weight_load(0, yk, 1 - c).wait()
        project(wbuf.at[0], 2 * yk + 1 - c)
        attend(yk)
    down_load.wait()
    for copy in cot_copies:
        copy.wait_recv()
    ghid[...] = dg(cot_ha[...].reshape(group * lat, feat), down[...], 1, 1)
    for k in range(1, ny):
        settle(me.at("y", ny - k))

    o_copy = pair_copy(1, o64.at[pl.ds(0, group), 1 - c], o_in)
    o_copy.start()
    o_loads = []
    for relay in o_relays:
        relay.wait("o")
        relay.wait("c")
    others = [(y, 1 - c)]
    for k in range(1, ny):
        others += [(me.at("y", ny - k), c), (me.at("y", ny - k), 1 - c)]
    for i, (ya, ca) in enumerate(others):
        o_loads.append(load(6 + i, o_all.at[ya, ca], o_v.at[2 * ya + ca]))
        o_loads[-1].start()
    o_load.wait()
    for copy in o_loads:
        copy.wait()
    o_copy.wait_recv()
    branch = jnp.zeros((lat, feat), F32)
    for a in range(group):
        mine = o64[a, c] + o_in[a]
        att64[a, c] = mine
        low = mine.astype(BF16)
        att_low[a] = low
        branch = branch + dg(low, o_v[a].reshape(cols, feat), 1, 0)
    att_copy = pair_copy(2, att64.at[pl.ds(0, group), c], att64.at[pl.ds(0, group), c])
    residual = lat_r[...] + branch
    mid_norm, mid_inv = normalize(residual)
    mid_low = (mid_norm * gain_f[...]).astype(BF16)
    mid_ha[y, c] = mid_low
    for copy in mid_copies:
        copy.start()
    att_copy.start()
    gather_att.start()
    part_o[...] = jnp.zeros_like(part_o)
    spot = lax.broadcasted_iota(jnp.int32, (1, feat), 1)
    squares = jnp.where(spot == 0, full_sum(residual * residual), 0.0)
    squares = squares + jnp.where(spot == 1, full_sum(branch * branch), 0.0)
    up_load.wait()
    for copy in mid_copies:
        copy.wait_recv()
    mid_keep = pltpu.make_async_copy(
        mid_ha.at[pl.ds(0, ny), c],
        mid_all.at[me.own["z"], me.own["x"], pl.ds(0, ny), c],
        own_sem.at[4],
    )
    gather_mid = Gather(me, None, mid_all, "z", md_send, md_recv, None, "y")
    mid_keep.start()
    pre = dg(mid_ha[...].reshape(group * lat, feat), up[...], 1, 0)
    cdf = 0.5 * (1.0 + lax.erf(pre * (0.5**0.5)))
    slope = cdf + pre * (jnp.exp(-0.5 * pre * pre) * 0.3989422804014327)
    gpre[...] = (ghid[...] * slope).astype(BF16)
    hid[...] = (pre * cdf).astype(BF16)
    sums[0] = dg(gpre[...], up[...], 1, 1).reshape(group, lat, feat).astype(BF16)
    for copy in gmid_copies:
        copy.start()
    grad_mid = sums[0, place].astype(F32)
    sums[1] = dg(hid[...], down[...], 1, 0).reshape(group, lat, feat).astype(BF16)
    gather_att.to_c()
    mid_keep.wait()
    gather_mid.start(0)
    gather_cot.next(2)
    for k, copy in enumerate(gmid_copies):
        copy.wait_recv()
        grad_mid = grad_mid + sums_in[0, k].astype(F32)
    for copy in ffn_copies:
        copy.start()
    grad_res = cot_r[...].astype(F32) + norm_grad(grad_mid * gain_f[...], mid_norm, mid_inv)
    gres_o[...] = grad_res
    grad_low = grad_res.astype(BF16)
    branch_o[...] = grad_low
    for a in range(group):
        g64[a, c] = dg(grad_low, o_v[a].reshape(cols, feat), 1, 1).astype(BF16)
    g_copy = pair_copy(3, g64.at[pl.ds(0, group), c], g64.at[pl.ds(0, group), c])
    g_copy.start()
    gather_lat.next(1)
    part_o[2:3] = jnp.sum(grad_mid * mid_norm, axis=0, keepdims=True)
    att_copy.wait_recv()
    o_copy.wait_send()
    for a in range(group):
        stat_copy(a).wait_send()
    g_copy.wait_recv()

    def gkv_store(a):
        return pltpu.make_async_copy(kv.at[a], gkv_o.at[a], st_send.at[a])

    @pl.loop(0, group)
    def _(a):
        q_blk = spread(q64[a].reshape(2 * lat, cols))
        g_blk = spread(g64[a].reshape(2 * lat, cols))
        att = att64[a].reshape(2 * lat, cols)
        inner = jnp.sum(
            g_blk.astype(F32) * jnp.concatenate([att] * heads, axis=0), axis=-1, keepdims=True
        )
        keys = kv[a, :, pl.ds(0, cols)]
        low = probs[a]
        grad = dg(g_blk, kv[a, :, pl.ds(cols, cols)], 1, 1)
        grad = (low.astype(F32) * (grad - inner)).astype(BF16)
        o64[a] = (merge(dg(grad, keys, 1, 0)) * scale).reshape(2, lat, cols)
        kv[a, :, pl.ds(0, cols)] = (dg(grad, q_blk, 0, 0) * scale).astype(BF16)
        kv[a, :, pl.ds(cols, cols)] = dg(low, g_blk, 0, 0).astype(BF16)
        gkv_store(a).start()

    gq_copy = pair_copy(4, o64.at[pl.ds(0, group), 1 - c], o_in)
    gq_copy.start()
    for copy in ffn_copies:
        copy.wait_recv()
    ffn = sums[1, place].astype(F32)
    for k in range(1, group):
        ffn = ffn + sums_in[1, k - 1].astype(F32)
    output_o[...] = residual + ffn
    squares = squares + jnp.where(spot == 2, full_sum(ffn * ffn), 0.0)
    part_o[3:4] = squares
    gq_copy.wait_recv()
    for a in range(group):
        gq_o[a] = (o64[a, c] + o_in[a]).astype(BF16)
    gather_lat.next(2)
    gather_cot.finish(3)
    gather_lat.finish(3)
    gather_att.finish_c()
    gather_mid.finish(0)
    for gather in (gather_cot, gather_lat, gather_mid):
        gather.drain()
    gather_att.drain_c()
    own_store.wait()
    wq_store.wait()
    hat_store.wait()
    for a in range(group):
        gkv_store(a).wait()
    for relay in relays + o_relays:
        relay.drain()
    for copy in (q_copy, att_copy, g_copy, gq_copy, wq_copy):
        copy.wait_send()
    for copies in (cot_copies, mid_copies, gmid_copies, ffn_copies, lat_copies, back_copies):
        for copy in copies:
            copy.wait_send()


def front(nx, ny, counts, latents, cot, gain_m, gain_l, gain_f, media, qkv, out_w, up, down):
    group = 2 * ny
    media_rows, feat = media.shape
    lat = latents.shape[0]
    rows = media_rows + lat
    cols = qkv.shape[-1]
    ff = up.shape[1]
    aligned = cols % 128 == 0
    tall = cols // HEAD * 2 * lat
    any_ = pl.BlockSpec(memory_space=pl.ANY)
    vm = pl.BlockSpec(memory_space=pltpu.VMEM)
    S = jax.ShapeDtypeStruct
    V = pltpu.VMEM
    D = pltpu.SemaphoreType.DMA
    every = (NZ, nx, ny, 2, lat)
    n_w = 4
    n_o = 2 if nx == 2 else 1
    half = (n_w, nx, 2, feat // (2 * nx * n_w))
    o_part = (n_o, nx, cols // (nx * n_o), feat)
    if aligned:
        wkv = qkv.reshape((3,) + half + (cols,))
    else:
        wkv = jnp.concatenate([qkv[1], qkv[2]], axis=-1).reshape(half + (2 * cols,))
    spread4 = NZ + nx + ny + 2 - 4
    slots = Relay.slots(nx, ny)
    outs = (
        S((rows, feat), BF16),
        S((group, rows, 2 * cols), BF16),
        S((ny, 2) + half + (2 * cols,), BF16),
        S((2, feat, cols), BF16),
        S((ny, 2) + o_part, BF16),
        S(every + (feat,), BF16),
        S(every + (feat,), BF16),
        S(every + (cols,), BF16),
        S(every + (feat,), BF16),
        S((lat, feat), BF16),
        S((group, lat, cols), BF16),
        S((lat, feat), F32),
        S((lat, feat), F32),
        S((8, feat), F32),
    )
    return pl.pallas_call(
        functools.partial(front_kernel, nx, ny, aligned),
        out_shape=outs,
        in_specs=[pl.BlockSpec(memory_space=pltpu.SMEM)] + [vm] * 5 + [any_] * 6,
        out_specs=(any_,) * 9 + (vm,) * 5,
        scratch_shapes=[
            V((rows, feat), BF16),
            V((group, rows, 2 * cols), BF16),
            V(half + (2 * cols,), BF16),
            V((2,) + half + (2 * cols,), BF16),
            V((2, feat, cols), BF16),
            V((group,) + o_part, BF16),
            V(up.shape, BF16),
            V(down.shape, BF16),
            V((2, 256, feat), BF16),
            V((ny, lat, feat), BF16),
            V((ny, 2, lat, cols), BF16),
            V((group, 2, lat, cols), BF16),
            V((group, tall, rows), F32),
            V((group, tall, rows), BF16),
            V((group, tall, 128), F32),
            V((group, tall, 128), F32),
            V((group, 2, lat, cols), F32),
            V((group, lat, cols), F32),
            V((group, 2, lat, cols), F32),
            V((group, lat, cols), BF16),
            V((ny, 2, lat, cols), BF16),
            V((group, 2, lat, cols), BF16),
            V((ny, 2, lat, feat), BF16),
            V((group, lat, feat), BF16),
            V((group * lat, ff), BF16),
            V((group * lat, ff), BF16),
            V((group * lat, ff), F32),
            V((2, group, lat, feat), BF16),
            V((2, group - 1, lat, feat), BF16),
            D((6 + group,)),
            D((2,)),
            D((2,)),
            D((3,)),
            D((n_w, slots)),
            D((n_w, slots)),
            D((n_o, slots)),
            D((n_o, slots)),
            D((2, ny - 1)),
            D((2, ny - 1)),
            D((6,)),
            D((6,)),
            D((group,)),
            D((group,)),
            D((4, group - 1)),
            D((4, group - 1)),
            D((spread4,)),
            D((spread4,)),
            D((spread4,)),
            D((spread4,)),
            D((ColumnGather.slots(nx, ny),)),
            D((ColumnGather.slots(nx, ny),)),
            D((NZ - 1,)),
            D((NZ - 1,)),
            D((5,)),
        ],
        compiler_params=pltpu.CompilerParams(
            collective_id=2, has_side_effects=True, vmem_limit_bytes=67043328
        ),
        name="front",
    )(
        counts,
        latents,
        cot,
        gain_m,
        gain_l,
        gain_f,
        media,
        wkv,
        qkv.reshape(3, feat, cols),
        out_w.reshape(o_part),
        up,
        down,
    )


def shards(
    media_tokens,
    latents,
    frame_counts,
    gain_media,
    gain_latent,
    gain_ffn,
    qkv_weight,
    out_weight,
    up_weight,
    down_weight,
    cotangent,
):
    group = lax.axis_size("ha")
    width = media_tokens.shape[1]
    lat = latents.shape[0]
    cols = qkv_weight.shape[2]
    entry_total = float(lat * width * lax.axis_size("sa") * group)
    nx, ny = lax.axis_size("sa") // NZ, group // 2
    gains_in = [g.reshape(1, width) for g in (gain_media, gain_latent, gain_ffn)]
    (
        hat,
        gkv,
        wkv_all,
        wq_pair,
        unused,
        cot_all,
        lat_all,
        att_all,
        mid_all,
        grad_branch,
        grad_q,
        grad_residual,
        output,
        parts,
    ) = front(
        nx,
        ny,
        frame_counts,
        latents,
        cotangent,
        *gains_in,
        media_tokens,
        qkv_weight,
        out_weight,
        up_weight,
        down_weight,
    )
    kv, gm, hid, gp, mid_all, att_all, branch_all, gq_all, gains, grad_latents = tail(
        nx,
        ny,
        hat,
        gkv,
        wkv_all.reshape(group, width, 2 * cols),
        up_weight,
        down_weight,
        media_tokens,
        cot_all,
        wq_pair,
        gains_in[0],
        gains_in[1],
        latents,
        grad_residual,
        grad_q,
        parts,
        grad_branch,
        mid_all,
        att_all,
    )
    cot_all = cot_all.reshape(-1, width)
    lat_all = lat_all.reshape(-1, width)
    kv = kv.reshape(width, 2 * cols)
    hid = hid.reshape(-1, hid.shape[-1])
    gp = gp.reshape(-1, gp.shape[-1])
    mid_all = mid_all.reshape(-1, width)
    branch_all = branch_all.reshape(-1, width)
    att_all = att_all.reshape(-1, cols)
    gq_all = gq_all.reshape(-1, cols)
    grad_media = gm.astype(F32)
    grad_out = dot("rc,rd->cd", att_all, branch_all)
    grad_wq = dot("rd,re->de", lat_all, gq_all)
    grad_down = dot("rf,rd->fd", hid, cot_all)
    grad_up = dot("rd,rf->df", mid_all, gp)
    grad_kv = jnp.stack([kv[:, :cols], kv[:, cols:]]).astype(F32)
    gain_one, gain_two, gain_three = gains[0], gains[1], gains[2]
    square_sums = gains[3, :3]
    roots = jnp.sqrt(square_sums / entry_total)
    return (
        output,
        grad_media,
        grad_latents,
        gain_one,
        gain_two,
        gain_three,
        jnp.concatenate([grad_wq[None], grad_kv], axis=0),
        grad_out,
        grad_up,
        grad_down,
        roots[0],
        roots[1],
        roots[2],
    )


def solution(mesh):
    placed = (
        P(("sa", "ha"), None),
        P(("sa", "ha"), None),
        P("sa"),
        P(),
        P(),
        P(),
        P(None, None, "ha"),
        P("ha", None),
        P(None, "ha"),
        P("ha", None),
        P(("sa", "ha"), None),
    )
    return jax.shard_map(
        shards,
        mesh=mesh,
        in_specs=placed,
        out_specs=(
            P(("sa", "ha"), None),
            P(("sa", "ha"), None),
            P(("sa", "ha"), None),
            P(),
            P(),
            P(),
            P(None, None, "ha"),
            P("ha", None),
            P(None, "ha"),
            P("ha", None),
            P(),
            P(),
            P(),
        ),
        check_vma=False,
    )
```

```python
import functools

import jax
import jax.numpy as jnp
from jax import lax
from jax.experimental import pallas as pl
from jax.experimental.pallas import tpu as pltpu
from jax.sharding import PartitionSpec as P

HEAD = 96
PATCH = 256
EPS = 1e-05
NEG = -1000000000.0
F32 = jnp.float32
BF16 = jnp.bfloat16


def normalize(values):
    centered = values - jnp.mean(values, axis=-1, keepdims=True)
    inverse = lax.rsqrt(jnp.mean(centered * centered, axis=-1, keepdims=True) + EPS)
    return centered * inverse, inverse


def norm_grad(grad, normed, inverse):
    first = jnp.mean(grad, axis=-1, keepdims=True)
    second = jnp.mean(grad * normed, axis=-1, keepdims=True)
    return inverse * (grad - first - normed * second)


def dot(spec, a, b):
    return jnp.einsum(spec, a, b, preferred_element_type=F32)


MESH = pl.DeviceIdType.MESH
NZ = 4
CHUNKS = 6


def dg(a, b, ca, cb):
    return lax.dot_general(a, b, (((ca,), (cb,)), ((), ())), preferred_element_type=F32)


class Where:
    def __init__(self, nx, ny):
        self.nx, self.ny = nx, ny
        sa, ha = lax.axis_index("sa"), lax.axis_index("ha")
        self.own = {"z": sa // nx, "x": sa % nx, "y": ha // 2, "c": ha % 2}
        self.size = {"z": NZ, "x": nx, "y": ny, "c": 2}

    def at(self, axis, k):
        return lax.rem(self.own[axis] + k, self.size[axis])

    def device(self, axis, k):
        p = dict(self.own)
        p[axis] = self.at(axis, k)
        return {"sa": p["z"] * self.nx + p["x"], "ha": p["y"] * 2 + p["c"]}


def greet(me):
    barrier = pltpu.get_barrier_semaphore()
    count = 0
    for axis in "cyxz":
        for k in range(1, me.size[axis]):
            pl.semaphore_signal(
                barrier, inc=1, device_id=me.device(axis, k), device_id_type=MESH
            )
            count += 1
    pl.semaphore_wait(barrier, count)


class Gather:
    def __init__(self, me, own, buf, order, send, recv, local, done=""):
        self.me, self.own, self.buf, self.order = me, own, buf, order
        self.send, self.recv, self.local = send, recv, local
        self.done = done

    def slot(self, done):
        me = self.me
        return tuple(
            pl.ds(0, me.size[a]) if a in done else me.own[a] for a in "zxyc"
        )

    def keep(self):
        return pltpu.make_async_copy(
            self.own, self.buf.at[self.slot(self.done)], self.local
        )

    def copies(self, phase):
        done = self.done + self.order[:phase]
        axis = self.order[phase]
        first = sum(self.me.size[a] - 1 for a in self.order[:phase])
        here = self.buf.at[self.slot(done)]
        src = self.own if phase == 0 and self.own is not None else here
        return [
            pltpu.make_async_remote_copy(
                src_ref=src,
                dst_ref=here,
                send_sem=self.send.at[first + k - 1],
                recv_sem=self.recv.at[first + k - 1],
                device_id=self.me.device(axis, k),
                device_id_type=MESH,
            )
            for k in range(1, self.me.size[axis])
        ]

    def start(self, phase):
        if phase == 0 and self.own is not None:
            self.keep().start()
        for c in self.copies(phase):
            c.start()

    def finish(self, phase):
        if phase == 0 and self.own is not None:
            self.keep().wait()
        for c in self.copies(phase):
            c.wait_recv()

    def next(self, phase):
        self.finish(phase)
        self.start(phase + 1)

    def drain(self):
        for phase in range(len(self.order)):
            for c in self.copies(phase):
                c.wait_send()


class ColumnGather:
    def __init__(self, me, own, land, buf, order, send, recv, local):
        self.me, self.own, self.land, self.buf = me, own, land, buf
        self.send, self.recv, self.local = send, recv, local
        n = NZ + me.size["x"] - 2
        first = me.size["y"]
        self.rest = Gather(
            me, None, buf, order, send.at[pl.ds(first, n)], recv.at[pl.ds(first, n)], None, "yc"
        )

    @staticmethod
    def slots(nx, ny):
        return ny + NZ + nx - 2

    def over_y(self):
        me = self.me
        return [
            pltpu.make_async_remote_copy(
                src_ref=self.own.at[pl.ds(2 * me.at("y", k), 2)],
                dst_ref=self.land.at[me.own["y"]],
                send_sem=self.send.at[k - 1],
                recv_sem=self.recv.at[k - 1],
                device_id=me.device("y", k),
                device_id_type=MESH,
            )
            for k in range(1, me.size["y"])
        ]

    def keep_own(self):
        y = self.me.own["y"]
        return pltpu.make_async_copy(
            self.own.at[pl.ds(2 * y, 2)], self.land.at[y], self.local.at[0]
        )

    def over_c(self):
        me = self.me
        c, full = me.own["c"], pl.ds(0, me.size["y"])
        at = (me.own["z"], me.own["x"], full, c)
        i = me.size["y"] - 1
        return pltpu.make_async_remote_copy(
            src_ref=self.land.at[full, 1 - c],
            dst_ref=self.buf.at[at],
            send_sem=self.send.at[i],
            recv_sem=self.recv.at[i],
            device_id=me.device("c", 1),
            device_id_type=MESH,
        )

    def keep_c(self):
        me = self.me
        c, full = me.own["c"], pl.ds(0, me.size["y"])
        at = (me.own["z"], me.own["x"], full, c)
        return pltpu.make_async_copy(self.land.at[full, c], self.buf.at[at], self.local.at[1])

    def start(self):
        self.keep_own().start()
        for copy in self.over_y():
            copy.start()

    def to_c(self):
        self.keep_own().wait()
        for copy in self.over_y():
            copy.wait_recv()
        self.keep_c().start()
        self.over_c().start()

    def finish_c(self):
        self.keep_c().wait()
        self.over_c().wait_recv()

    def to_rest(self):
        self.finish_c()
        self.rest.start(0)

    def to_last(self):
        self.rest.next(0)

    def finish(self):
        self.rest.finish(1)

    def drain_c(self):
        for copy in self.over_y():
            copy.wait_send()
        self.over_c().wait_send()

    def drain(self):
        self.drain_c()
        self.rest.drain()


def tail_kernel(
    nx,
    ny,
    hat_h,
    gkv_h,
    wkv_h,
    up_h,
    down_h,
    media_h,
    cot_all,
    wq_h,
    gain_r,
    gain_l,
    lat_r,
    gres_r,
    gq_r,
    part_r,
    branch_r,
    unused_mid,
    unused_att,
    kv_o,
    gm_o,
    hid_o,
    gp_o,
    mid_all,
    att_all,
    branch_all,
    gq_all,
    gains_o,
    glat_o,
    hat,
    gkv,
    wkv,
    up,
    down,
    send_c,
    recv_c,
    acc,
    send_y,
    recv_y,
    send_x,
    recv_x,
    send_z,
    recv_z,
    red,
    gq_y,
    ql_out,
    ql_in,
    media_t,
    gm_t,
    mid_t,
    cot_t,
    hid_t,
    gp_t,
    wqb,
    gbuf,
    grecv,
    load_sem,
    tile_sem,
    out_sem,
    c_send,
    c_recv,
    y_send,
    y_recv,
    x_send,
    x_recv,
    z_send,
    z_recv,
    za_send,
    za_recv,
    xa_send,
    xa_recv,
    keep_sem,
    g_send,
    g_recv,
    mid_send,
    mid_recv,
    br_send,
    br_recv,
    aq_send,
    aq_recv,
    ql_send,
    ql_recv,
    at_send,
    at_recv,
    own_sem,
):
    me = Where(nx, ny)
    z, x, y, c = (me.own[a] for a in "zxyc")
    T = CHUNKS
    pieces = 2 * ny
    chunk = acc.shape[1]
    quarter = send_x.shape[2]
    sub = red.shape[1]
    feat = hat.shape[1]

    def load(i, src, dst):
        return pltpu.make_async_copy(src, dst, load_sem.at[i])

    hat_copy = load(0, hat_h, hat)
    wkv_copy = load(2, wkv_h, wkv)
    up_copy = load(3, up_h, up)
    down_copy = load(4, down_h, down)

    def gkv_load(k, parity):
        a = 2 * me.at("y", k) + parity
        return pltpu.make_async_copy(gkv_h.at[a], gkv.at[a], load_sem.at[6 + 2 * k + parity])

    hat_copy.start()
    for k in list(range(1, ny)) + [0]:
        gkv_load(k, 1 - c).start()
        gkv_load(k, c).start()
    greet(me)

    mid = Gather(me, None, mid_all, "xc", mid_send, mid_recv, None, "yz")
    att = Gather(me, None, att_all, "zx", at_send, at_recv, None, "yc")
    branch = Gather(me, branch_r, branch_all, "zxyc", br_send, br_recv, own_sem.at[1])

    gq = ColumnGather(me, gq_r, gq_y, gq_all, "zx", aq_send, aq_recv, own_sem.at[pl.ds(2, 2)])

    def ql_copy(k):
        return pltpu.make_async_remote_copy(
            src_ref=ql_out.at[me.at("y", k)],
            dst_ref=ql_in.at[k - 1],
            send_sem=ql_send.at[k - 1],
            recv_sem=ql_recv.at[k - 1],
            device_id=me.device("y", k),
            device_id_type=MESH,
        )

    mid.start(0)
    branch.start(0)
    gq.start()
    att.start(0)
    wq_load = load(5, wq_h, wqb)

    def grad_rows(k, t, parity):
        piece = 2 * me.at("y", k) + parity
        left = hat[:, pl.ds(pl.multiple_of(t * chunk, 128), chunk)]
        return dg(left, gkv[piece], 0, 0)

    def core_copy(t):
        return pltpu.make_async_remote_copy(
            src_ref=send_c.at[t],
            dst_ref=recv_c.at[t],
            send_sem=c_send.at[t],
            recv_sem=c_recv.at[t],
            device_id=me.device("c", 1),
            device_id_type=MESH,
        )

    def y_copy(k, t):
        return pltpu.make_async_remote_copy(
            src_ref=send_y.at[k - 1, t],
            dst_ref=recv_y.at[k - 1, t],
            send_sem=y_send.at[k - 1, t],
            recv_sem=y_recv.at[k - 1, t],
            device_id=me.device("y", k),
            device_id_type=MESH,
        )

    def x_copy(k, t):
        return pltpu.make_async_remote_copy(
            src_ref=send_x.at[k - 1, t],
            dst_ref=recv_x.at[k - 1, t],
            send_sem=x_send.at[k - 1, t],
            recv_sem=x_recv.at[k - 1, t],
            device_id=me.device("x", k),
            device_id_type=MESH,
        )

    def z_copy(k, t):
        return pltpu.make_async_remote_copy(
            src_ref=send_z.at[k - 1, t],
            dst_ref=recv_z.at[k - 1, t],
            send_sem=z_send.at[k - 1, t],
            recv_sem=z_recv.at[k - 1, t],
            device_id=me.device("z", k),
            device_id_type=MESH,
        )

    def za_copy(k, t):
        return pltpu.make_async_remote_copy(
            src_ref=red.at[t],
            dst_ref=kv_o.at[t, x * NZ + z],
            send_sem=za_send.at[k - 1, t],
            recv_sem=za_recv.at[k - 1, t],
            device_id=me.device("z", k),
            device_id_type=MESH,
        )

    def xa_copy(k, t):
        rows = kv_o.at[t, pl.ds(x * NZ, NZ)]
        return pltpu.make_async_remote_copy(
            src_ref=rows,
            dst_ref=rows,
            send_sem=xa_send.at[k - 1, t],
            recv_sem=xa_recv.at[k - 1, t],
            device_id=me.device("x", k),
            device_id_type=MESH,
        )

    def keep_copy(t):
        return pltpu.make_async_copy(red.at[t], kv_o.at[t, x * NZ + z], keep_sem.at[t])

    def latent_queries():
        wq_load.wait()
        for src in range(ny):
            total = dg(gq_y[src, 0], wqb[0], 1, 1) + dg(gq_y[src, 1], wqb[1], 1, 1)
            ql_out[src] = total.astype(BF16)
        for k in range(1, ny):
            ql_copy(k).start()

    hat_copy.wait()
    lag = 2
    steps = ny * T

    @pl.loop(0, steps + lag)
    def _(j):
        @pl.when(j < steps)
        def _():
            k, t = lax.rem(1 + j // T, ny), lax.rem(j, T)

            @pl.when(t == 0)
            def _():
                gkv_load(k, 1 - c).wait()
                gkv_load(k, c).wait()

            @pl.when(j == 3)
            def _():
                for copy in (wkv_copy, up_copy, down_copy, wq_load):
                    copy.start()

            @pl.when(j >= T)
            def _():
                core_copy(t).wait_send()

            send_c[t] = grad_rows(k, t, 1 - c).astype(BF16)
            core_copy(t).start()

        @pl.when(j >= lag)
        def _():
            i = j - lag
            k, t = lax.rem(1 + i // T, ny), lax.rem(i, T)
            mine = grad_rows(k, t, c)
            core_copy(t).wait_recv()
            mine = mine + recv_c[t].astype(F32)

            @pl.when(i >= steps - T)
            def _():
                acc[t] = mine

            @pl.when(i < steps - T)
            def _():
                for step in range(1, ny):

                    @pl.when(i // T == step - 1)
                    def _():
                        send_y[step - 1, t] = mine.astype(BF16)
                        y_copy(step, t).start()

        @pl.when(j == 3)
        def _():
            gq.to_c()

        @pl.when(j == 5)
        def _():
            branch.next(0)
            latent_queries()

        @pl.when(j == 9)
        def _():
            mid.next(0)
            gq.to_rest()

    for t in range(T):
        core_copy(t).wait_send()
    wkv_copy.wait()
    up_copy.wait()
    down_copy.wait()

    gbuf[...] = part_r[...]
    media_rows = media_h.shape[0]
    tile = media_t.shape[1]
    n_media = media_rows // tile

    def media_load(u):
        return pltpu.make_async_copy(
            media_h.at[pl.ds(pl.multiple_of(u * tile, tile), tile)],
            media_t.at[lax.rem(u, 2)],
            tile_sem.at[lax.rem(u, 2)],
        )

    def gm_store(u):
        return pltpu.make_async_copy(
            gm_t, gm_o.at[pl.ds(pl.multiple_of(u * tile, tile), tile)], out_sem.at[0]
        )

    def media_tile(u):
        @pl.when(u + 1 < n_media)
        def _():
            media_load(u + 1).start()

        rows = pl.ds(pl.multiple_of(u * tile, tile), tile)
        total = dg(gkv[0, rows], wkv[0], 1, 1)
        for a in range(1, pieces):
            total = total + dg(gkv[a, rows], wkv[a], 1, 1)
        media_load(u).wait()
        values = media_t[lax.rem(u, 2)].astype(F32)
        normed, inverse = normalize(values)
        gbuf[0:1] = gbuf[0:1] + jnp.sum(total * normed, axis=0, keepdims=True)
        result = norm_grad(total * gain_r[...].reshape(1, -1), normed, inverse)

        @pl.when(u >= 1)
        def _():
            gm_store(u - 1).wait()

        gm_t[...] = result.astype(BF16)
        gm_store(u).start()

    xt = mid_t.shape[1]
    n_ffn = NZ * (nx // xt)

    def rows_load(u):
        zz, xx = u // (nx // xt), lax.rem(u, nx // xt) * xt
        b = lax.rem(u, 2)
        return [
            pltpu.make_async_copy(
                mid_all.at[zz, pl.ds(xx, xt)], mid_t.at[b], tile_sem.at[2 + b]
            ),
            pltpu.make_async_copy(
                cot_all.at[zz, pl.ds(xx, xt)], cot_t.at[b], tile_sem.at[4 + b]
            ),
        ]

    def ffn_store(u):
        return [
            pltpu.make_async_copy(hid_t, hid_o.at[u], out_sem.at[1]),
            pltpu.make_async_copy(gp_t, gp_o.at[u], out_sem.at[2]),
        ]

    def ffn_tile(u):
        @pl.when(u + 1 < n_ffn)
        def _():
            for copy in rows_load(u + 1):
                copy.start()

        for copy in rows_load(u):
            copy.wait()

        @pl.when(u >= 1)
        def _():
            for copy in ffn_store(u - 1):
                copy.wait()

        b = lax.rem(u, 2)
        mid_rows = mid_t[b].reshape(-1, feat)
        cot_rows = cot_t[b].reshape(-1, feat)
        width = up.shape[1] // 3
        for part in range(3):
            cols = pl.ds(part * width, width)
            pre = dg(mid_rows, up[:, cols], 1, 0)
            grad = dg(cot_rows, down[cols, :], 1, 1)
            cdf = 0.5 * (1.0 + lax.erf(pre * (0.5**0.5)))
            slope = cdf + pre * (jnp.exp(-0.5 * pre * pre) * 0.3989422804014327)
            hid_t[:, cols] = (pre * cdf).astype(BF16)
            gp_t[:, cols] = (grad * slope).astype(BF16)
        for copy in ffn_store(u):
            copy.start()

    def latent_rows():
        rows = pl.ds(media_rows, lat_r.shape[0])
        total = dg(gkv[0, rows], wkv[0], 1, 1)
        for a in range(1, pieces):
            total = total + dg(gkv[a, rows], wkv[a], 1, 1)
        total = total + ql_out[y].astype(F32)
        for k in range(1, ny):
            ql_copy(k).wait_recv()
            total = total + ql_in[k - 1].astype(F32)
        normed, inverse = normalize(lat_r[...])
        gbuf[1:2] = jnp.sum(total * normed, axis=0, keepdims=True)
        glat_o[...] = gres_r[...] + norm_grad(total * gain_l[...].reshape(1, -1), normed, inverse)

    def step_y(t):
        for k in range(1, ny):
            y_copy(k, t).wait_recv()
        whole = acc[t]
        for k in range(1, ny):
            whole = whole + recv_y[k - 1, t].astype(F32)
        acc[t] = whole
        for k in range(1, nx):
            there = pl.ds(pl.multiple_of(me.at("x", k) * quarter, 8), quarter)
            send_x[k - 1, t] = acc[t, there].astype(BF16)
            x_copy(k, t).start()

    def step_x(t):
        for k in range(1, nx):
            x_copy(k, t).wait_recv()
        here = pl.ds(pl.multiple_of(x * quarter, 8), quarter)
        whole = acc[t, here]
        for k in range(1, nx):
            whole = whole + recv_x[k - 1, t].astype(F32)
        acc[t, here] = whole
        for k in range(1, NZ):
            there = pl.ds(pl.multiple_of(x * quarter + me.at("z", k) * sub, 8), sub)
            send_z[k - 1, t] = acc[t, there].astype(BF16)
            z_copy(k, t).start()

    def step_z(t):
        for k in range(1, NZ):
            z_copy(k, t).wait_recv()
        whole = acc[t, pl.ds(pl.multiple_of(x * quarter + z * sub, 8), sub)]
        for k in range(1, NZ):
            whole = whole + recv_z[k - 1, t].astype(F32)
        red[t] = whole.astype(BF16)
        keep_copy(t).start()
        for k in range(1, NZ):
            za_copy(k, t).start()

    def step_za(t):
        keep_copy(t).wait()
        for k in range(1, NZ):
            za_copy(k, t).wait_recv()
        for k in range(1, nx):
            xa_copy(k, t).start()

    def step_xa(t):
        for k in range(1, nx):
            xa_copy(k, t).wait_recv()

    def comm(s):
        for lag_s, action in ((0, step_y), (3, step_x), (4, step_z), (6, step_za), (9, step_xa)):
            ready = jnp.logical_and(s >= lag_s, s < lag_s + 2 * T)

            @pl.when(jnp.logical_and(ready, lax.rem(s + lag_s, 2) == 0))
            def _():
                action((s - lag_s) // 2)

    def gain_copies(axis, base):
        return [
            pltpu.make_async_remote_copy(
                src_ref=gbuf,
                dst_ref=grecv.at[base + k - 1],
                send_sem=g_send.at[base + k - 1],
                recv_sem=g_recv.at[base + k - 1],
                device_id=me.device(axis, k),
                device_id_type=MESH,
            )
            for k in range(1, me.size[axis])
        ]

    def gain_base(axis):
        return sum(me.size[a] - 1 for a in "cyxz"[: "cyxz".index(axis)])

    def gain_start(axis):
        for copy in gain_copies(axis, gain_base(axis)):
            copy.start()

    def gain_finish(axis):
        base = gain_base(axis)
        for copy in gain_copies(axis, base):
            copy.wait_send()
            copy.wait_recv()
        total = gbuf[...]
        for k in range(1, me.size[axis]):
            total = total + grecv[base + k - 1]
        gbuf[...] = total

    media_load(0).start()
    per = n_ffn // 4

    @pl.loop(0, max(2 * T + 8, n_media + 15))
    def _(s):
        comm(s)

        @pl.when(s == 0)
        def _():
            att.next(0)

        @pl.when(s < n_media)
        def _():
            media_tile(s)

        @pl.when(s == n_media)
        def _():
            gm_store(n_media - 1).wait()
            latent_rows()
            gain_start("c")
            mid.finish(1)
            for copy in rows_load(0):
                copy.start()

        @pl.when(s == n_media + 1)
        def _():
            gain_finish("c")
            gain_start("x")

        @pl.when(jnp.logical_and(s > n_media, s < n_media + 5))
        def _():
            @pl.loop(0, per)
            def _(u):
                ffn_tile((s - n_media - 1) * per + u)

        @pl.when(s == 6)
        def _():
            gq.to_last()

        @pl.when(s == n_media + 4)
        def _():
            gain_finish("x")
            gain_start("z")

        @pl.when(s == n_media + 6)
        def _():
            for copy in ffn_store(n_ffn - 1):
                copy.wait()
            branch.next(1)

        @pl.when(s == n_media + 8)
        def _():
            gain_finish("z")
            gain_start("y")

        @pl.when(s == n_media + 14)
        def _():
            branch.next(2)

    gain_finish("y")
    gains_o[...] = gbuf[...]
    branch.finish(3)
    gq.finish()
    att.finish(1)
    att.drain()
    mid.drain()
    branch.drain()
    gq.drain()
    for k in range(1, ny):
        ql_copy(k).wait_send()

    @pl.loop(0, T)
    def _(t):
        for k in range(1, ny):
            y_copy(k, t).wait_send()
        for k in range(1, nx):
            x_copy(k, t).wait_send()
            xa_copy(k, t).wait_send()
        for k in range(1, NZ):
            z_copy(k, t).wait_send()
            za_copy(k, t).wait_send()


def tail(
    nx, ny, hat, gkv, wkv, up, down, media, cot_all, wq, gain_m, gain_l, lats, gres, gq, parts, branch, mid_all, att_all
):
    T = CHUNKS
    rows, feat = hat.shape
    pieces, _, two = gkv.shape
    lat = branch.shape[0]
    ff = up.shape[1]
    blocks = nx * NZ
    chunk = feat // T
    sub = chunk // blocks
    xt = 256 // (lat * pieces)
    tile_rows = xt * pieces * lat
    tiles = NZ * nx // xt
    any_ = pl.BlockSpec(memory_space=pl.ANY)
    vm = pl.BlockSpec(memory_space=pltpu.VMEM)
    S = jax.ShapeDtypeStruct
    every = (NZ, nx, ny, 2, lat)
    V = pltpu.VMEM
    D = pltpu.SemaphoreType.DMA
    spread4 = NZ + nx + ny + 2 - 4
    media_rows = media.shape[0]
    outs = (
        S((T, blocks, sub, two), BF16),
        S((media_rows, feat), BF16),
        S((tiles, tile_rows, ff), BF16),
        S((tiles, tile_rows, ff), BF16),
        S(every + (feat,), BF16),
        S(every + (two // 2,), BF16),
        S(every + (feat,), BF16),
        S(every + (two // 2,), BF16),
        S((8, feat), F32),
        S(gres.shape, F32),
    )
    return pl.pallas_call(
        functools.partial(tail_kernel, nx, ny),
        out_shape=outs,
        in_specs=[any_] * 8 + [vm] * 7 + [any_] * 2,
        out_specs=(any_,) * 8 + (vm,) * 2,
        input_output_aliases={15: 4, 16: 5},
        scratch_shapes=[
            V(hat.shape, BF16),
            V(gkv.shape, BF16),
            V(wkv.shape, BF16),
            V(up.shape, BF16),
            V(down.shape, BF16),
            V((T, chunk, two), BF16),
            V((T, chunk, two), BF16),
            V((T, chunk, two), F32),
            V((ny - 1, T, chunk, two), BF16),
            V((ny - 1, T, chunk, two), BF16),
            V((nx - 1, T, NZ * sub, two), BF16),
            V((nx - 1, T, NZ * sub, two), BF16),
            V((NZ - 1, T, sub, two), BF16),
            V((NZ - 1, T, sub, two), BF16),
            V((T, sub, two), BF16),
            V((ny, 2, lat, two // 2), BF16),
            V((ny, lat, feat), BF16),
            V((ny - 1, lat, feat), BF16),
            V((2, 256, feat), BF16),
            V((256, feat), BF16),
            V((2, xt, ny, 2, lat, feat), BF16),
            V((2, xt, ny, 2, lat, feat), BF16),
            V((tile_rows, ff), BF16),
            V((tile_rows, ff), BF16),
            V(wq.shape, BF16),
            V((8, feat), F32),
            V((spread4, 8, feat), F32),
            D((6 + pieces,)),
            D((6,)),
            D((3,)),
            D((T,)),
            D((T,)),
            D((ny - 1, T)),
            D((ny - 1, T)),
            D((nx - 1, T)),
            D((nx - 1, T)),
            D((NZ - 1, T)),
            D((NZ - 1, T)),
            D((NZ - 1, T)),
            D((NZ - 1, T)),
            D((nx - 1, T)),
            D((nx - 1, T)),
            D((T,)),
            D((spread4,)),
            D((spread4,)),
            D((spread4,)),
            D((spread4,)),
            D((spread4,)),
            D((spread4,)),
            D((ColumnGather.slots(nx, ny),)),
            D((ColumnGather.slots(nx, ny),)),
            D((ny - 1,)),
            D((ny - 1,)),
            D((spread4,)),
            D((spread4,)),
            D((4,)),
        ],
        compiler_params=pltpu.CompilerParams(
            collective_id=3, has_side_effects=True, vmem_limit_bytes=67043328
        ),
        name="tail",
    )(
        hat, gkv, wkv, up, down, media, cot_all, wq, gain_m, gain_l, lats, gres, gq, parts, branch, mid_all, att_all
    )


def post_kernel(
    hid_h,
    gp_h,
    mid_h,
    cot_h,
    branch_h,
    lat_h,
    att_h,
    gq_h,
    kv_h,
    gm_h,
    res_r,
    lat_r,
    gains_r,
    down_o,
    up_o,
    out_o,
    qkv_o,
    media_o,
    res_o,
    lat_o,
    one_o,
    two_o,
    three_o,
    left,
    right,
    small,
    tiles,
    media_in,
    media_out,
    in_sem,
    tile_sem,
    min_sem,
    mout_sem,
):
    rows = left.shape[1]
    n_k = hid_h.shape[0] // rows
    cols = att_h.shape[1]
    width = tiles.shape[1]
    n_media = gm_h.shape[0] // media_in.shape[1]
    counts = {"tile": 0, "media": 0}
    depth = media_out.shape[0]

    def media_load(i):
        size = media_in.shape[1]
        return pltpu.make_async_copy(
            gm_h.at[pl.ds(i * size, size)], media_in.at[i], min_sem.at[i]
        )

    def media_store(i):
        size = media_in.shape[1]
        return pltpu.make_async_copy(
            media_out.at[i % depth], media_o.at[pl.ds(i * size, size)], mout_sem.at[i % depth]
        )

    def media_step():
        i = counts["media"]
        if i >= n_media:
            return
        counts["media"] = i + 1
        media_load(i).wait()
        if i >= depth:
            media_store(i - depth).wait()
        media_out[i % depth] = media_in[i].astype(F32)
        media_store(i).start()

    pending = [None] * tiles.shape[0]

    def emit(value, target):
        i = counts["tile"] % len(pending)
        counts["tile"] += 1
        if pending[i] is not None:
            pending[i].wait()
        a, b = value.shape
        tiles[i, 0:a, 0:b] = value
        pending[i] = pltpu.make_async_copy(
            tiles.at[i, pl.ds(0, a), pl.ds(0, b)], target, tile_sem.at[i]
        )
        pending[i].start()

    def load(slot, a, b, k):
        part = pl.ds(k * rows, rows)
        return [
            pltpu.make_async_copy(a.at[part], left.at[slot, :, pl.ds(0, a.shape[1])], in_sem.at[2 * slot]),
            pltpu.make_async_copy(b.at[part], right.at[slot, :, pl.ds(0, b.shape[1])], in_sem.at[2 * slot + 1]),
        ]

    jobs = [
        (hid_h, cot_h, down_o),
        (mid_h, gp_h, up_o),
        (att_h, branch_h, out_o),
        (lat_h, gq_h, qkv_o.at[0]),
    ]
    loads = [load(i, a, b, 0) for i, (a, b, unused) in enumerate(jobs)]
    kv_loads = [
        pltpu.make_async_copy(kv_h.at[:, pl.ds(i * cols, cols)], small.at[i], in_sem.at[8 + i])
        for i in range(2)
    ]
    for copy in loads[0] + loads[1]:
        copy.start()
    for i in range(n_media):
        media_load(i).start()
    for copy in loads[2] + loads[3] + kv_loads:
        copy.start()
    res_o[...] = res_r[...]
    lat_o[...] = lat_r[...]
    for i, ref in enumerate((one_o, two_o, three_o)):
        ref[...] = gains_r[i]
    for i, (a, b, target) in enumerate(jobs):
        for copy in loads[i]:
            copy.wait()
        slot = i
        m, n = a.shape[1], b.shape[1]
        for at in range(0, m, width):
            step = min(width, m - at)
            value = dg(left[slot, :, at : at + step], right[slot, :, 0:n], 0, 0)
            emit(value, target.at[pl.ds(at, step), pl.ds(0, n)])
            media_step()
    while counts["media"] < n_media:
        media_step()
    for i in range(2):
        kv_loads[i].wait()
        for at in range(0, kv_h.shape[0], width):
            value = small[i, at : at + width].astype(F32)
            emit(value, qkv_o.at[1 + i, pl.ds(at, width)])
    for copy in pending:
        copy.wait()
    for i in range(max(n_media - depth, 0), n_media):
        media_store(i).wait()


def post(hid, gp, mid, cot, branch, lat, att, gq, kv, gm, res, glat, gains):
    S = jax.ShapeDtypeStruct
    V = pltpu.VMEM
    D = pltpu.SemaphoreType.DMA
    any_ = pl.BlockSpec(memory_space=pl.ANY)
    rows, ff = hid.shape
    feat = mid.shape[1]
    cols = att.shape[1]
    wide = max(feat, ff)
    args = (hid, gp, mid, cot, branch, lat, att, gq, kv, gm)
    vm = pl.BlockSpec(memory_space=pltpu.VMEM)
    return pl.pallas_call(
        post_kernel,
        out_shape=(
            S((ff, feat), F32),
            S((feat, ff), F32),
            S((cols, feat), F32),
            S((3, feat, cols), F32),
            S(gm.shape, F32),
            S(res.shape, F32),
            S(glat.shape, F32),
            S((feat,), F32),
            S((feat,), F32),
            S((feat,), F32),
        ),
        in_specs=[any_] * len(args) + [vm] * 3,
        out_specs=(any_,) * 5 + (vm,) * 5,
        scratch_shapes=[
            V((4, rows, wide), BF16),
            V((4, rows, wide), BF16),
            V((2, feat, cols), BF16),
            V((4, 256, wide), F32),
            V((gm.shape[0] // 64, 64, feat), BF16),
            V((4, 64, feat), F32),
            D((10,)),
            D((4,)),
            D((gm.shape[0] // 64,)),
            D((4,)),
        ],
        compiler_params=pltpu.CompilerParams(vmem_limit_bytes=67043328),
        name="weights",
    )(*args, res, glat, gains)


def full_sum(x):
    return jnp.sum(jnp.sum(x, axis=1, keepdims=True), axis=0, keepdims=True)


class Relay:
    def __init__(self, me, own, buf, order, send, recv):
        self.me, self.own, self.buf, self.order = me, own, buf, order
        self.send, self.recv = send, recv
        ny, nx = me.size["y"] - 1, me.size["x"] - 1
        sizes = {"o": 1, "y": ny, "x": ny * nx, "z": ny, "c": ny}
        self.base, total = {}, 0
        for a in "oyxzc":
            self.base[a] = total
            total += sizes[a]

    @staticmethod
    def slots(nx, ny):
        return 1 + 3 * (ny - 1) + (ny - 1) * (nx - 1)

    def part(self, done):
        me = self.me
        index = []
        if "x" in self.order:
            index.append(pl.ds(0, me.size["x"]) if "x" in done else me.own["x"])
        if "z" in self.order:
            index.append(pl.ds(0, 2) if "z" in done else lax.rem(me.own["z"], 2))
        return tuple(index)

    def copies(self, phase):
        me, buf = self.me, self.buf
        y, c = me.own["y"], me.own["c"]
        out = []

        def add(src, dst, where):
            i = self.base[phase] + len(out)
            out.append(
                pltpu.make_async_remote_copy(
                    src_ref=src,
                    dst_ref=dst,
                    send_sem=self.send.at[i],
                    recv_sem=self.recv.at[i],
                    device_id=where,
                    device_id_type=MESH,
                )
            )

        if phase == "o":
            add(self.own, buf.at[y, c], me.device("c", 1))
            return out
        done = self.order[1 : self.order.index(phase)] if phase in "xz" else ""
        for k in range(1, me.size["y"]):
            if phase == "y":
                at = self.part("")
                src = self.own.at[at] if at else self.own
                add(src, buf.at[(y, c) + at], me.device("y", k))
                continue
            yk = me.at("y", me.size["y"] - k)
            if phase == "c":
                add(buf.at[yk, c], buf.at[yk, c], me.device("c", 1))
                continue
            ref = buf.at[(yk, c) + self.part(done)]
            if phase == "z":
                add(ref, ref, me.device("z", 1 - 2 * lax.rem(me.own["z"], 2) + NZ))
            else:
                for j in range(1, me.size["x"]):
                    add(ref, ref, me.device("x", j))
        return out

    def start(self, phase):
        for copy in self.copies(phase):
            copy.start()

    def wait(self, phase):
        for copy in self.copies(phase):
            copy.wait_recv()

    def next(self, phase):
        self.wait(phase)
        at = self.order.index(phase) + 1
        self.start(self.order[at] if at < len(self.order) else "c")

    def drain(self):
        for phase in "o" + self.order + "c":
            for copy in self.copies(phase):
                copy.wait_send()


def front_kernel(
    nx,
    ny,
    aligned,
    count_s,
    lat_r,
    cot_r,
    gain_m,
    gain_l,
    gain_f,
    media_h,
    kvw_h,
    wq_h,
    out_h,
    up_h,
    down_h,
    hat_o,
    gkv_o,
    wkv_all,
    wq_o,
    o_all,
    cot_all,
    lat_all,
    att_all,
    mid_all,
    branch_o,
    gq_o,
    gres_o,
    output_o,
    part_o,
    hat,
    kv,
    wkv_own,
    wbuf,
    wq_v,
    o_v,
    up,
    down,
    media_t,
    lat_y,
    q_y,
    q64,
    pexp,
    probs,
    stat,
    stat_in,
    o64,
    o_in,
    att64,
    att_low,
    att_y,
    g64,
    mid_ha,
    cot_ha,
    hid,
    gpre,
    ghid,
    sums,
    sums_in,
    load_sem,
    tile_sem,
    wload_sem,
    store_sem,
    w_send,
    w_recv,
    u_send,
    u_recv,
    qy_send,
    qy_recv,
    pair_send,
    pair_recv,
    st_send,
    st_recv,
    ha_send,
    ha_recv,
    ct_send,
    ct_recv,
    lt_send,
    lt_recv,
    at_send,
    at_recv,
    md_send,
    md_recv,
    own_sem,
):
    me = Where(nx, ny)
    y, c = me.own["y"], me.own["c"]
    group = 2 * ny
    place = lax.axis_index("ha")
    lat = lat_r.shape[0]
    media_rows = media_h.shape[0]
    rows = hat.shape[0]
    feat = hat.shape[1]
    cols = q64.shape[-1]
    heads = cols // HEAD
    scale = HEAD ** (-0.5)
    partner = me.device("c", 1)
    n_w = wkv_own.shape[0]
    n_o = o_v.shape[1]

    def load(i, src, dst):
        return pltpu.make_async_copy(src, dst, load_sem.at[i])

    wkv_loads = (
        [
            load(0, kvw_h.at[1], wkv_own.at[..., pl.ds(0, cols)]),
            load(1, kvw_h.at[2], wkv_own.at[..., pl.ds(cols, cols)]),
        ]
        if aligned
        else [load(0, kvw_h, wkv_own)]
    )
    up_load, down_load = load(2, up_h, up), load(3, down_h, down)
    wq_load = load(4, wq_h.at[0], wq_v.at[c])
    o_load = load(5, out_h, o_v.at[place])
    for copy in wkv_loads:
        copy.start()
    tile = media_t.shape[1]
    tiles = media_rows // tile

    def media_load(u):
        return pltpu.make_async_copy(
            media_h.at[pl.ds(pl.multiple_of(u * tile, tile), tile)],
            media_t.at[lax.rem(u, 2)],
            tile_sem.at[lax.rem(u, 2)],
        )

    media_load(0).start()
    wq_load.start()
    down_load.start()
    up_load.start()
    o_load.start()

    barrier = pltpu.get_barrier_semaphore()
    greeted = [me.device(a, k) for a in "cyxz" for k in range(1, me.size[a])]
    for k in range(1, ny):
        greeted.append({"sa": lax.axis_index("sa"), "ha": me.at("y", k) * 2 + 1 - c})
    for where in greeted:
        pl.semaphore_signal(barrier, inc=1, device_id=where, device_id_type=MESH)
    pl.semaphore_wait(barrier, len(greeted))

    both = (pl.ds(0, ny), pl.ds(0, 2))
    relays = [
        Relay(
            me,
            wkv_own.at[i],
            wkv_all.at[both + (i,)],
            ("yxz", "yzx")[i % 2],
            w_send.at[i],
            w_recv.at[i],
        )
        for i in range(n_w)
    ]
    o_relays = [
        Relay(
            me,
            out_h.at[i],
            o_all.at[both + (i,)],
            "yx" if i == 0 else "yz",
            u_send.at[i],
            u_recv.at[i],
        )
        for i in range(n_o)
    ]
    gather_cot = Gather(me, cot_r, cot_all, "zyxc", ct_send, ct_recv, own_sem.at[0])
    own_lat = hat.at[pl.ds(media_rows, lat)]
    gather_lat = Gather(me, own_lat, lat_all, "yzxc", lt_send, lt_recv, own_sem.at[1])
    gather_att = ColumnGather(
        me, att_low, att_y, att_all, "xz", at_send, at_recv, own_sem.at[pl.ds(2, 2)]
    )

    def remote(src, dst, send, recv, where):
        return pltpu.make_async_remote_copy(
            src_ref=src,
            dst_ref=dst,
            send_sem=send,
            recv_sem=recv,
            device_id=where,
            device_id_type=MESH,
        )

    def pair_copy(i, src, dst):
        return remote(src, dst, pair_send.at[i], pair_recv.at[i], partner)

    def ha_copies(base, source, target):
        out = []
        for k in range(1, group):
            there = lax.rem(place + k, group)
            out.append(
                remote(
                    source(there),
                    target(k),
                    ha_send.at[base, k - 1],
                    ha_recv.at[base, k - 1],
                    {"sa": lax.axis_index("sa"), "ha": there},
                )
            )
        return out

    cot_copies = ha_copies(0, lambda there: cot_r, lambda k: cot_ha.at[place])
    mid_copies = ha_copies(1, lambda there: mid_ha.at[y, c], lambda k: mid_ha.at[y, c])
    gmid_copies = ha_copies(2, lambda there: sums.at[0, there], lambda k: sums_in.at[0, k - 1])
    ffn_copies = ha_copies(3, lambda there: sums.at[1, there], lambda k: sums_in.at[1, k - 1])
    lat_copies = [
        remote(own_lat, lat_y.at[y], qy_send.at[0, k - 1], qy_recv.at[0, k - 1], me.device("y", k))
        for k in range(1, ny)
    ]
    back_copies = [
        remote(
            q_y.at[me.at("y", k)],
            q64.at[pl.ds(2 * y, 2), c],
            qy_send.at[1, k - 1],
            qy_recv.at[1, k - 1],
            me.device("y", k),
        )
        for k in range(1, ny)
    ]
    wq_copy = pair_copy(5, wq_h.at[0], wq_v.at[c])

    gather_cot.start(0)
    normed, unused = normalize(lat_r[...])
    low = (normed * gain_l[...].reshape(1, -1)).astype(BF16)
    hat[pl.ds(media_rows, lat)] = low
    lat_y[y] = low
    for copy in lat_copies:
        copy.start()
    for copy in wkv_loads:
        copy.wait()
    for relay in relays:
        relay.start("o")
        relay.start("y")
    wq_copy.start()
    for relay in o_relays:
        relay.start("o")
    cot_ha[place] = cot_r[...]
    own_store = pltpu.make_async_copy(wkv_own, wkv_all.at[y, c], store_sem.at[0])
    own_store.start()

    @pl.loop(0, tiles)
    def _(u):
        @pl.when(u + 1 < tiles)
        def _():
            media_load(u + 1).start()

        media_load(u).wait()
        normed, unused = normalize(media_t[lax.rem(u, 2)].astype(F32))
        hat[pl.ds(pl.multiple_of(u * tile, tile), tile)] = (normed * gain_m[...].reshape(1, -1)).astype(BF16)

    hat_store = pltpu.make_async_copy(hat, hat_o, store_sem.at[1])
    hat_store.start()
    step = rows // 4

    def project(weights, piece):
        @pl.loop(0, 4)
        def _(u):
            part = pl.ds(pl.multiple_of(u * step, 8), step)
            w = weights[...].reshape(feat, 2 * cols)
            kv[piece, part] = dg(hat[part], w, 1, 0).astype(BF16)

    def weight_load(slot, ya, ca):
        return pltpu.make_async_copy(wkv_all.at[ya, ca], wbuf.at[slot], wload_sem.at[slot])

    project(wkv_own, place)
    for relay in relays:
        relay.wait("o")
    weight_load(0, y, 1 - c).start()
    relays[0].next("y")
    weight_load(0, y, 1 - c).wait()
    project(wbuf.at[0], 2 * y + 1 - c)
    relays[1].next("y")
    relays[0].next("x")
    wq_load.wait()
    wq_copy.wait_recv()
    for copy in lat_copies:
        copy.wait_recv()
    wq_store = pltpu.make_async_copy(wq_v, wq_o, store_sem.at[2])
    wq_store.start()
    all_lat = lat_y[...].reshape(ny * lat, feat)
    for ca in range(2):
        w = wq_v[ca].reshape(feat, cols)
        q_y[pl.ds(0, ny), ca] = dg(all_lat, w, 1, 0).astype(BF16).reshape(ny, lat, cols)
    q64[2 * y, c] = q_y[y, 0]
    q64[2 * y + 1, c] = q_y[y, 1]
    for copy in back_copies:
        copy.start()
    relays[2].next("y")
    for relay in o_relays:
        relay.start("y")
    for copy in cot_copies:
        copy.start()
    gather_lat.start(0)
    gather_cot.next(0)
    relays[1].next("z")
    relays[3].next("y")
    for copy in back_copies:
        copy.wait_recv()
    q_copy = pair_copy(0, q64.at[pl.ds(0, group), c], q64.at[pl.ds(0, group), c])
    q_copy.start()
    relays[2].next("x")

    lane = lax.broadcasted_iota(jnp.int32, (2 * lat, cols), 1)

    def inside(h):
        return jnp.logical_and(lane >= h * HEAD, lane < (h + 1) * HEAD)

    def spread(x):
        return jnp.concatenate(
            [jnp.where(inside(h), x, jnp.zeros_like(x)) for h in range(heads)], axis=0
        )

    def merge(x):
        total = jnp.where(inside(0), x[: 2 * lat], 0.0)
        for h in range(1, heads):
            total = total + jnp.where(inside(h), x[2 * lat * h : 2 * lat * (h + 1)], 0.0)
        return total

    tall = heads * 2 * lat
    limit = count_s[y] * PATCH - c * media_rows
    key = lax.broadcasted_iota(jnp.int32, (tall, rows), 1)
    half = lax.broadcasted_iota(jnp.int32, (tall, 128), 1) < 64

    def stat_copy(a):
        return remote(stat.at[a], stat_in.at[a], st_send.at[a], st_recv.at[a], partner)

    def attend(ya):
        @pl.loop(0, 2)
        def _(ca):
            a = 2 * ya + ca
            q_blk = spread(q64[a].reshape(2 * lat, cols))
            scores = dg(q_blk, kv[a, :, pl.ds(0, cols)], 1, 1) * scale
            usable = jnp.logical_or(key < limit, key >= media_rows)
            scores = jnp.where(usable, scores, NEG)
            top = jnp.max(scores, axis=-1, keepdims=True)
            value = jnp.exp(scores - top)
            pexp[a] = value
            total = jnp.sum(value, axis=-1, keepdims=True)
            stat[a] = jnp.where(half, top, total)
            stat_copy(a).start()

    def settle(ya):
        @pl.loop(0, 2)
        def _(ca):
            a = 2 * ya + ca
            stat_copy(a).wait_recv()
            top, total = stat[a, :, 0:1], stat[a, :, 64:65]
            top_in, total_in = stat_in[a, :, 0:1], stat_in[a, :, 64:65]
            top_all = jnp.maximum(top, top_in)
            mine = jnp.exp(top - top_all)
            denom = total * mine + total_in * jnp.exp(top_in - top_all)
            low = (pexp[a] * (mine / denom)).astype(BF16)
            probs[a] = low
            o64[a] = merge(dg(low, kv[a, :, pl.ds(cols, cols)], 1, 0)).reshape(2, lat, cols)

    q_copy.wait_recv()
    attend(y)
    relays[0].next("z")
    relays[3].next("z")
    settle(y)
    relays[1].next("x")
    relays[2].next("z")
    relays[3].next("x")
    for k in range(1, ny):
        yk = me.at("y", ny - k)
        weight_load(1, yk, c).start()
        if k == 1:
            for relay in o_relays:
                relay.next("y")
        weight_load(1, yk, c).wait()
        project(wbuf.at[1], 2 * yk + c)
        if k == 1:
            for relay in relays:
                relay.wait("c")
        weight_load(0, yk, 1 - c).start()
        if k == 1:
            for relay in o_relays:
                relay.next(relay.order[1])
            gather_lat.next(0)
            gather_cot.next(1)
        weight_load(0, yk, 1 - c).wait()
        project(wbuf.at[0], 2 * yk + 1 - c)
        attend(yk)
    down_load.wait()
    for copy in cot_copies:
        copy.wait_recv()
    ghid[...] = dg(cot_ha[...].reshape(group * lat, feat), down[...], 1, 1)
    for k in range(1, ny):
        settle(me.at("y", ny - k))

    o_copy = pair_copy(1, o64.at[pl.ds(0, group), 1 - c], o_in)
    o_copy.start()
    o_loads = []
    for relay in o_relays:
        relay.wait("o")
        relay.wait("c")
    others = [(y, 1 - c)]
    for k in range(1, ny):
        others += [(me.at("y", ny - k), c), (me.at("y", ny - k), 1 - c)]
    for i, (ya, ca) in enumerate(others):
        o_loads.append(load(6 + i, o_all.at[ya, ca], o_v.at[2 * ya + ca]))
        o_loads[-1].start()
    o_load.wait()
    for copy in o_loads:
        copy.wait()
    o_copy.wait_recv()
    branch = jnp.zeros((lat, feat), F32)
    for a in range(group):
        mine = o64[a, c] + o_in[a]
        att64[a, c] = mine
        low = mine.astype(BF16)
        att_low[a] = low
        branch = branch + dg(low, o_v[a].reshape(cols, feat), 1, 0)
    att_copy = pair_copy(2, att64.at[pl.ds(0, group), c], att64.at[pl.ds(0, group), c])
    residual = lat_r[...] + branch
    mid_norm, mid_inv = normalize(residual)
    mid_low = (mid_norm * gain_f[...].reshape(1, -1)).astype(BF16)
    mid_ha[y, c] = mid_low
    for copy in mid_copies:
        copy.start()
    att_copy.start()
    gather_att.start()
    part_o[...] = jnp.zeros_like(part_o)
    spot = lax.broadcasted_iota(jnp.int32, (1, feat), 1)
    squares = jnp.where(spot == 0, full_sum(residual * residual), 0.0)
    squares = squares + jnp.where(spot == 1, full_sum(branch * branch), 0.0)
    up_load.wait()
    for copy in mid_copies:
        copy.wait_recv()
    mid_keep = pltpu.make_async_copy(
        mid_ha.at[pl.ds(0, ny), c],
        mid_all.at[me.own["z"], me.own["x"], pl.ds(0, ny), c],
        own_sem.at[4],
    )
    gather_mid = Gather(me, None, mid_all, "z", md_send, md_recv, None, "y")
    mid_keep.start()
    pre = dg(mid_ha[...].reshape(group * lat, feat), up[...], 1, 0)
    cdf = 0.5 * (1.0 + lax.erf(pre * (0.5**0.5)))
    slope = cdf + pre * (jnp.exp(-0.5 * pre * pre) * 0.3989422804014327)
    gpre[...] = (ghid[...] * slope).astype(BF16)
    hid[...] = (pre * cdf).astype(BF16)
    sums[0] = dg(gpre[...], up[...], 1, 1).reshape(group, lat, feat).astype(BF16)
    for copy in gmid_copies:
        copy.start()
    grad_mid = sums[0, place].astype(F32)
    sums[1] = dg(hid[...], down[...], 1, 0).reshape(group, lat, feat).astype(BF16)
    gather_att.to_c()
    mid_keep.wait()
    gather_mid.start(0)
    gather_lat.next(1)
    gather_cot.next(2)
    for k, copy in enumerate(gmid_copies):
        copy.wait_recv()
        grad_mid = grad_mid + sums_in[0, k].astype(F32)
    for copy in ffn_copies:
        copy.start()
    grad_res = cot_r[...].astype(F32) + norm_grad(grad_mid * gain_f[...].reshape(1, -1), mid_norm, mid_inv)
    gres_o[...] = grad_res
    grad_low = grad_res.astype(BF16)
    branch_o[...] = grad_low
    for a in range(group):
        g64[a, c] = dg(grad_low, o_v[a].reshape(cols, feat), 1, 1).astype(BF16)
    g_copy = pair_copy(3, g64.at[pl.ds(0, group), c], g64.at[pl.ds(0, group), c])
    g_copy.start()
    part_o[2:3] = jnp.sum(grad_mid * mid_norm, axis=0, keepdims=True)
    att_copy.wait_recv()
    o_copy.wait_send()
    for a in range(group):
        stat_copy(a).wait_send()
    g_copy.wait_recv()

    def gkv_store(a):
        return pltpu.make_async_copy(kv.at[a], gkv_o.at[a], st_send.at[a])

    @pl.loop(0, group)
    def _(a):
        q_blk = spread(q64[a].reshape(2 * lat, cols))
        g_blk = spread(g64[a].reshape(2 * lat, cols))
        att = att64[a].reshape(2 * lat, cols)
        inner = jnp.sum(
            g_blk.astype(F32) * jnp.concatenate([att] * heads, axis=0), axis=-1, keepdims=True
        )
        keys = kv[a, :, pl.ds(0, cols)]
        low = probs[a]
        grad = dg(g_blk, kv[a, :, pl.ds(cols, cols)], 1, 1)
        grad = (low.astype(F32) * (grad - inner)).astype(BF16)
        o64[a] = (merge(dg(grad, keys, 1, 0)) * scale).reshape(2, lat, cols)
        kv[a, :, pl.ds(0, cols)] = (dg(grad, q_blk, 0, 0) * scale).astype(BF16)
        kv[a, :, pl.ds(cols, cols)] = dg(low, g_blk, 0, 0).astype(BF16)
        gkv_store(a).start()

    gq_copy = pair_copy(4, o64.at[pl.ds(0, group), 1 - c], o_in)
    gq_copy.start()
    for copy in ffn_copies:
        copy.wait_recv()
    ffn = sums[1, place].astype(F32)
    for k in range(1, group):
        ffn = ffn + sums_in[1, k - 1].astype(F32)
    output_o[...] = residual + ffn
    squares = squares + jnp.where(spot == 2, full_sum(ffn * ffn), 0.0)
    part_o[3:4] = squares
    gq_copy.wait_recv()
    for a in range(group):
        gq_o[a] = (o64[a, c] + o_in[a]).astype(BF16)
    gather_lat.next(2)
    gather_cot.finish(3)
    gather_lat.finish(3)
    gather_att.finish_c()
    gather_mid.finish(0)
    for gather in (gather_cot, gather_lat, gather_mid):
        gather.drain()
    gather_att.drain_c()
    own_store.wait()
    wq_store.wait()
    hat_store.wait()
    for a in range(group):
        gkv_store(a).wait()
    for relay in relays + o_relays:
        relay.drain()
    for copy in (q_copy, att_copy, g_copy, gq_copy, wq_copy):
        copy.wait_send()
    for copies in (cot_copies, mid_copies, gmid_copies, ffn_copies, lat_copies, back_copies):
        for copy in copies:
            copy.wait_send()


def front(nx, ny, counts, latents, cot, gain_m, gain_l, gain_f, media, qkv, out_w, up, down):
    group = 2 * ny
    media_rows, feat = media.shape
    lat = latents.shape[0]
    rows = media_rows + lat
    cols = qkv.shape[-1]
    ff = up.shape[1]
    aligned = cols % 128 == 0
    tall = cols // HEAD * 2 * lat
    any_ = pl.BlockSpec(memory_space=pl.ANY)
    vm = pl.BlockSpec(memory_space=pltpu.VMEM)
    S = jax.ShapeDtypeStruct
    V = pltpu.VMEM
    D = pltpu.SemaphoreType.DMA
    every = (NZ, nx, ny, 2, lat)
    n_w = 4
    n_o = 2 if nx == 2 else 1
    half = (n_w, nx, 2, feat // (2 * nx * n_w))
    o_part = (n_o, nx, cols // (nx * n_o), feat)
    if aligned:
        wkv = qkv.reshape((3,) + half + (cols,))
    else:
        wkv = jnp.concatenate([qkv[1], qkv[2]], axis=-1).reshape(half + (2 * cols,))
    spread4 = NZ + nx + ny + 2 - 4
    slots = Relay.slots(nx, ny)
    outs = (
        S((rows, feat), BF16),
        S((group, rows, 2 * cols), BF16),
        S((ny, 2) + half + (2 * cols,), BF16),
        S((2, feat, cols), BF16),
        S((ny, 2) + o_part, BF16),
        S(every + (feat,), BF16),
        S(every + (feat,), BF16),
        S(every + (cols,), BF16),
        S(every + (feat,), BF16),
        S((lat, feat), BF16),
        S((group, lat, cols), BF16),
        S((lat, feat), F32),
        S((lat, feat), F32),
        S((8, feat), F32),
    )
    return pl.pallas_call(
        functools.partial(front_kernel, nx, ny, aligned),
        out_shape=outs,
        in_specs=[pl.BlockSpec(memory_space=pltpu.SMEM)] + [vm] * 5 + [any_] * 6,
        out_specs=(any_,) * 9 + (vm,) * 5,
        scratch_shapes=[
            V((rows, feat), BF16),
            V((group, rows, 2 * cols), BF16),
            V(half + (2 * cols,), BF16),
            V((2,) + half + (2 * cols,), BF16),
            V((2, feat, cols), BF16),
            V((group,) + o_part, BF16),
            V(up.shape, BF16),
            V(down.shape, BF16),
            V((2, 256, feat), BF16),
            V((ny, lat, feat), BF16),
            V((ny, 2, lat, cols), BF16),
            V((group, 2, lat, cols), BF16),
            V((group, tall, rows), F32),
            V((group, tall, rows), BF16),
            V((group, tall, 128), F32),
            V((group, tall, 128), F32),
            V((group, 2, lat, cols), F32),
            V((group, lat, cols), F32),
            V((group, 2, lat, cols), F32),
            V((group, lat, cols), BF16),
            V((ny, 2, lat, cols), BF16),
            V((group, 2, lat, cols), BF16),
            V((ny, 2, lat, feat), BF16),
            V((group, lat, feat), BF16),
            V((group * lat, ff), BF16),
            V((group * lat, ff), BF16),
            V((group * lat, ff), F32),
            V((2, group, lat, feat), BF16),
            V((2, group - 1, lat, feat), BF16),
            D((6 + group,)),
            D((2,)),
            D((2,)),
            D((3,)),
            D((n_w, slots)),
            D((n_w, slots)),
            D((n_o, slots)),
            D((n_o, slots)),
            D((2, ny - 1)),
            D((2, ny - 1)),
            D((6,)),
            D((6,)),
            D((group,)),
            D((group,)),
            D((4, group - 1)),
            D((4, group - 1)),
            D((spread4,)),
            D((spread4,)),
            D((spread4,)),
            D((spread4,)),
            D((ColumnGather.slots(nx, ny),)),
            D((ColumnGather.slots(nx, ny),)),
            D((NZ - 1,)),
            D((NZ - 1,)),
            D((5,)),
        ],
        compiler_params=pltpu.CompilerParams(
            collective_id=2, has_side_effects=True, vmem_limit_bytes=67043328
        ),
        name="front",
    )(
        counts,
        latents,
        cot,
        gain_m,
        gain_l,
        gain_f,
        media,
        wkv,
        qkv.reshape(3, feat, cols),
        out_w.reshape(o_part),
        up,
        down,
    )


def shards(
    media_tokens,
    latents,
    frame_counts,
    gain_media,
    gain_latent,
    gain_ffn,
    qkv_weight,
    out_weight,
    up_weight,
    down_weight,
    cotangent,
):
    group = lax.axis_size("ha")
    width = media_tokens.shape[1]
    lat = latents.shape[0]
    cols = qkv_weight.shape[2]
    entry_total = float(lat * width * lax.axis_size("sa") * group)
    nx, ny = lax.axis_size("sa") // NZ, group // 2
    gains_in = (gain_media, gain_latent, gain_ffn)
    (
        hat,
        gkv,
        wkv_all,
        wq_pair,
        unused,
        cot_all,
        lat_all,
        att_all,
        mid_all,
        grad_branch,
        grad_q,
        grad_residual,
        output,
        parts,
    ) = front(
        nx,
        ny,
        frame_counts,
        latents,
        cotangent,
        *gains_in,
        media_tokens,
        qkv_weight,
        out_weight,
        up_weight,
        down_weight,
    )
    kv, gm, hid, gp, mid_all, att_all, branch_all, gq_all, gains, grad_latents = tail(
        nx,
        ny,
        hat,
        gkv,
        wkv_all.reshape(group, width, 2 * cols),
        up_weight,
        down_weight,
        media_tokens,
        cot_all,
        wq_pair,
        gains_in[0],
        gains_in[1],
        latents,
        grad_residual,
        grad_q,
        parts,
        grad_branch,
        mid_all,
        att_all,
    )
    cot_all = cot_all.reshape(-1, width)
    lat_all = lat_all.reshape(-1, width)
    kv = kv.reshape(width, 2 * cols)
    hid = hid.reshape(-1, hid.shape[-1])
    gp = gp.reshape(-1, gp.shape[-1])
    mid_all = mid_all.reshape(-1, width)
    branch_all = branch_all.reshape(-1, width)
    att_all = att_all.reshape(-1, cols)
    gq_all = gq_all.reshape(-1, cols)
    args = (hid, gp, mid_all, cot_all, branch_all, lat_all, att_all, gq_all, kv, gm)
    if hid.shape[0] <= 1024:
        (
            grad_down,
            grad_up,
            grad_out,
            grad_qkv,
            grad_media,
            output,
            grad_latents,
            gain_one,
            gain_two,
            gain_three,
        ) = post(*args, output, grad_latents, gains)
    else:
        grad_media = gm.astype(F32)
        grad_out = dot("rc,rd->cd", att_all, branch_all)
        grad_wq = dot("rd,re->de", lat_all, gq_all)
        grad_down = dot("rf,rd->fd", hid, cot_all)
        grad_up = dot("rd,rf->df", mid_all, gp)
        grad_kv = jnp.stack([kv[:, :cols], kv[:, cols:]]).astype(F32)
        grad_qkv = jnp.concatenate([grad_wq[None], grad_kv], axis=0)
        gain_one, gain_two, gain_three = gains[0], gains[1], gains[2]
    square_sums = gains[3, :3]
    roots = jnp.sqrt(square_sums / entry_total)
    return (
        output,
        grad_media,
        grad_latents,
        gain_one,
        gain_two,
        gain_three,
        grad_qkv,
        grad_out,
        grad_up,
        grad_down,
        roots[0],
        roots[1],
        roots[2],
    )


def solution(mesh):
    placed = (
        P(("sa", "ha"), None),
        P(("sa", "ha"), None),
        P("sa"),
        P(),
        P(),
        P(),
        P(None, None, "ha"),
        P("ha", None),
        P(None, "ha"),
        P("ha", None),
        P(("sa", "ha"), None),
    )
    return jax.shard_map(
        shards,
        mesh=mesh,
        in_specs=placed,
        out_specs=(
            P(("sa", "ha"), None),
            P(("sa", "ha"), None),
            P(("sa", "ha"), None),
            P(),
            P(),
            P(),
            P(None, None, "ha"),
            P("ha", None),
            P(None, "ha"),
            P("ha", None),
            P(),
            P(),
            P(),
        ),
        check_vma=False,
    )
```

```python
import functools

import jax
import jax.numpy as jnp
from jax import lax
from jax.experimental import pallas as pl
from jax.experimental.pallas import tpu as pltpu
from jax.sharding import PartitionSpec as P

HEAD = 96
PATCH = 256
EPS = 1e-05
NEG = -1000000000.0
F32 = jnp.float32
BF16 = jnp.bfloat16


def normalize(values):
    centered = values - jnp.mean(values, axis=-1, keepdims=True)
    inverse = lax.rsqrt(jnp.mean(centered * centered, axis=-1, keepdims=True) + EPS)
    return centered * inverse, inverse


def norm_grad(grad, normed, inverse):
    first = jnp.mean(grad, axis=-1, keepdims=True)
    second = jnp.mean(grad * normed, axis=-1, keepdims=True)
    return inverse * (grad - first - normed * second)


def dot(spec, a, b):
    return jnp.einsum(spec, a, b, preferred_element_type=F32)


MESH = pl.DeviceIdType.MESH
NZ = 4
CHUNKS = 12


def dg(a, b, ca, cb):
    return lax.dot_general(a, b, (((ca,), (cb,)), ((), ())), preferred_element_type=F32)


class Where:
    def __init__(self, nx, ny):
        self.nx, self.ny = nx, ny
        sa, ha = lax.axis_index("sa"), lax.axis_index("ha")
        self.own = {"z": sa // nx, "x": sa % nx, "y": ha // 2, "c": ha % 2}
        self.size = {"z": NZ, "x": nx, "y": ny, "c": 2}

    def at(self, axis, k):
        return lax.rem(self.own[axis] + k, self.size[axis])

    def device(self, axis, k):
        p = dict(self.own)
        p[axis] = self.at(axis, k)
        return {"sa": p["z"] * self.nx + p["x"], "ha": p["y"] * 2 + p["c"]}


def greet(me):
    barrier = pltpu.get_barrier_semaphore()
    count = 0
    for axis in "cyxz":
        for k in range(1, me.size[axis]):
            pl.semaphore_signal(
                barrier, inc=1, device_id=me.device(axis, k), device_id_type=MESH
            )
            count += 1
    pl.semaphore_wait(barrier, count)


class Gather:
    def __init__(self, me, own, buf, order, send, recv, local, done=""):
        self.me, self.own, self.buf, self.order = me, own, buf, order
        self.send, self.recv, self.local = send, recv, local
        self.done = done

    def slot(self, done):
        me = self.me
        return tuple(
            pl.ds(0, me.size[a]) if a in done else me.own[a] for a in "zxyc"
        )

    def keep(self):
        return pltpu.make_async_copy(
            self.own, self.buf.at[self.slot(self.done)], self.local
        )

    def copies(self, phase):
        done = self.done + self.order[:phase]
        axis = self.order[phase]
        first = sum(self.me.size[a] - 1 for a in self.order[:phase])
        here = self.buf.at[self.slot(done)]
        src = self.own if phase == 0 and self.own is not None else here
        return [
            pltpu.make_async_remote_copy(
                src_ref=src,
                dst_ref=here,
                send_sem=self.send.at[first + k - 1],
                recv_sem=self.recv.at[first + k - 1],
                device_id=self.me.device(axis, k),
                device_id_type=MESH,
            )
            for k in range(1, self.me.size[axis])
        ]

    def start(self, phase):
        if phase == 0 and self.own is not None:
            self.keep().start()
        for c in self.copies(phase):
            c.start()

    def finish(self, phase):
        if phase == 0 and self.own is not None:
            self.keep().wait()
        for c in self.copies(phase):
            c.wait_recv()

    def next(self, phase):
        self.finish(phase)
        self.start(phase + 1)

    def drain(self):
        for phase in range(len(self.order)):
            for c in self.copies(phase):
                c.wait_send()


class ColumnGather:
    def __init__(self, me, own, land, buf, order, send, recv, local):
        self.me, self.own, self.land, self.buf = me, own, land, buf
        self.send, self.recv, self.local = send, recv, local
        n = NZ + me.size["x"] - 2
        first = me.size["y"]
        self.rest = Gather(
            me, None, buf, order, send.at[pl.ds(first, n)], recv.at[pl.ds(first, n)], None, "yc"
        )

    @staticmethod
    def slots(nx, ny):
        return ny + NZ + nx - 2

    def over_y(self):
        me = self.me
        return [
            pltpu.make_async_remote_copy(
                src_ref=self.own.at[pl.ds(2 * me.at("y", k), 2)],
                dst_ref=self.land.at[me.own["y"]],
                send_sem=self.send.at[k - 1],
                recv_sem=self.recv.at[k - 1],
                device_id=me.device("y", k),
                device_id_type=MESH,
            )
            for k in range(1, me.size["y"])
        ]

    def keep_own(self):
        y = self.me.own["y"]
        return pltpu.make_async_copy(
            self.own.at[pl.ds(2 * y, 2)], self.land.at[y], self.local.at[0]
        )

    def over_c(self):
        me = self.me
        c, full = me.own["c"], pl.ds(0, me.size["y"])
        at = (me.own["z"], me.own["x"], full, c)
        i = me.size["y"] - 1
        return pltpu.make_async_remote_copy(
            src_ref=self.land.at[full, 1 - c],
            dst_ref=self.buf.at[at],
            send_sem=self.send.at[i],
            recv_sem=self.recv.at[i],
            device_id=me.device("c", 1),
            device_id_type=MESH,
        )

    def keep_c(self):
        me = self.me
        c, full = me.own["c"], pl.ds(0, me.size["y"])
        at = (me.own["z"], me.own["x"], full, c)
        return pltpu.make_async_copy(self.land.at[full, c], self.buf.at[at], self.local.at[1])

    def start(self):
        self.keep_own().start()
        for copy in self.over_y():
            copy.start()

    def to_c(self):
        self.keep_own().wait()
        for copy in self.over_y():
            copy.wait_recv()
        self.keep_c().start()
        self.over_c().start()

    def finish_c(self):
        self.keep_c().wait()
        self.over_c().wait_recv()

    def to_rest(self):
        self.finish_c()
        self.rest.start(0)

    def to_last(self):
        self.rest.next(0)

    def finish(self):
        self.rest.finish(1)

    def drain_c(self):
        for copy in self.over_y():
            copy.wait_send()
        self.over_c().wait_send()

    def drain(self):
        self.drain_c()
        self.rest.drain()


def tail_kernel(
    nx,
    ny,
    hat_h,
    gkv_h,
    wkv_h,
    up_h,
    down_h,
    media_h,
    cot_all,
    wq_h,
    gain_r,
    gain_l,
    lat_r,
    gres_r,
    gq_r,
    part_r,
    branch_r,
    unused_mid,
    unused_att,
    kv_o,
    gm_o,
    hid_o,
    gp_o,
    mid_all,
    att_all,
    branch_all,
    gq_all,
    gains_o,
    glat_o,
    hat,
    gkv,
    wkv,
    up,
    down,
    send_c,
    recv_c,
    acc,
    send_y,
    recv_y,
    send_x,
    recv_x,
    send_n,
    recv_n,
    send_f,
    recv_f,
    red,
    gq_y,
    ql_out,
    ql_in,
    media_t,
    gm_t,
    mid_t,
    cot_t,
    hid_t,
    gp_t,
    wqb,
    gbuf,
    grecv,
    load_sem,
    tile_sem,
    out_sem,
    c_send,
    c_recv,
    y_send,
    y_recv,
    x_send,
    x_recv,
    z_send,
    z_recv,
    xa_send,
    xa_recv,
    keep_sem,
    g_send,
    g_recv,
    mid_send,
    mid_recv,
    br_send,
    br_recv,
    aq_send,
    aq_recv,
    ql_send,
    ql_recv,
    at_send,
    at_recv,
    own_sem,
):
    me = Where(nx, ny)
    z, x, y, c = (me.own[a] for a in "zxyc")
    T = CHUNKS
    TG = send_c.shape[0]
    per_g = T // TG
    pieces = 2 * ny
    big = send_c.shape[1]
    chunk = acc.shape[1]
    quarter = send_x.shape[2]
    sub = red.shape[1]
    feat = hat.shape[1]

    def load(i, src, dst):
        return pltpu.make_async_copy(src, dst, load_sem.at[i])

    hat_copy = load(0, hat_h, hat)
    wkv_copy = load(2, wkv_h, wkv)
    up_copy = load(3, up_h, up)
    down_copy = load(4, down_h, down)

    def gkv_load(k, parity):
        a = 2 * me.at("y", k) + parity
        return pltpu.make_async_copy(gkv_h.at[a], gkv.at[a], load_sem.at[6 + 2 * k + parity])

    hat_copy.start()
    for k in list(range(1, ny)) + [0]:
        gkv_load(k, 1 - c).start()
        gkv_load(k, c).start()
    greet(me)

    mid = Gather(me, None, mid_all, "xc", mid_send, mid_recv, None, "yz")
    att = Gather(me, None, att_all, "xz", at_send, at_recv, None, "yc")
    branch = Gather(me, branch_r, branch_all, "zxyc", br_send, br_recv, own_sem.at[1])

    gq = ColumnGather(me, gq_r, gq_y, gq_all, "zx", aq_send, aq_recv, own_sem.at[pl.ds(2, 2)])

    def ql_copy(k):
        return pltpu.make_async_remote_copy(
            src_ref=ql_out.at[me.at("y", k)],
            dst_ref=ql_in.at[k - 1],
            send_sem=ql_send.at[k - 1],
            recv_sem=ql_recv.at[k - 1],
            device_id=me.device("y", k),
            device_id_type=MESH,
        )

    att.start(0)
    mid.start(0)
    branch.start(0)
    gq.start()
    wq_load = load(5, wq_h, wqb)

    def grad_rows(k, t, parity):
        piece = 2 * me.at("y", k) + parity
        left = hat[:, pl.ds(pl.multiple_of(t * big, 128), big)]
        return dg(left, gkv[piece], 0, 0)

    def core_copy(t):
        return pltpu.make_async_remote_copy(
            src_ref=send_c.at[t],
            dst_ref=recv_c.at[t],
            send_sem=c_send.at[t],
            recv_sem=c_recv.at[t],
            device_id=me.device("c", 1),
            device_id_type=MESH,
        )

    def y_copy(k, t):
        return pltpu.make_async_remote_copy(
            src_ref=send_y.at[k - 1, t],
            dst_ref=recv_y.at[k - 1, t],
            send_sem=y_send.at[k - 1, t],
            recv_sem=y_recv.at[k - 1, t],
            device_id=me.device("y", k),
            device_id_type=MESH,
        )

    def x_copy(k, t):
        return pltpu.make_async_remote_copy(
            src_ref=send_x.at[k - 1, t],
            dst_ref=recv_x.at[k - 1, t],
            send_sem=x_send.at[k - 1, t],
            recv_sem=x_recv.at[k - 1, t],
            device_id=me.device("x", k),
            device_id_type=MESH,
        )

    odd, half = lax.rem(z, 2), z // 2
    near = me.device("z", 1 - 2 * odd + NZ)
    far = me.device("z", 2)
    mine_at = x * NZ + odd * 2 + half

    def z_hop(i, src, dst, where, t):
        return pltpu.make_async_remote_copy(
            src_ref=src,
            dst_ref=dst,
            send_sem=z_send.at[i, t],
            recv_sem=z_recv.at[i, t],
            device_id=where,
            device_id_type=MESH,
        )

    def near_copy(t):
        return z_hop(0, send_n.at[t], recv_n.at[t], near, t)

    def far_copy(t):
        return z_hop(1, send_f.at[t], recv_f.at[t], far, t)

    def far_back(t):
        return z_hop(2, red.at[t], kv_o.at[t, mine_at], far, t)

    def near_back(t):
        rows = kv_o.at[t, pl.ds(x * NZ + odd * 2, 2)]
        return z_hop(3, rows, rows, near, t)

    def xa_copy(k, t):
        rows = kv_o.at[t, pl.ds(x * NZ, NZ)]
        return pltpu.make_async_remote_copy(
            src_ref=rows,
            dst_ref=rows,
            send_sem=xa_send.at[k - 1, t],
            recv_sem=xa_recv.at[k - 1, t],
            device_id=me.device("x", k),
            device_id_type=MESH,
        )

    def keep_copy(t):
        return pltpu.make_async_copy(red.at[t], kv_o.at[t, mine_at], keep_sem.at[t])

    def latent_queries():
        wq_load.wait()
        for src in range(ny):
            total = dg(gq_y[src, 0], wqb[0], 1, 1) + dg(gq_y[src, 1], wqb[1], 1, 1)
            ql_out[src] = total.astype(BF16)
        for k in range(1, ny):
            ql_copy(k).start()

    def step_y(t):
        for k in range(1, ny):
            y_copy(k, t).wait_recv()
        whole = acc[t]
        for k in range(1, ny):
            whole = whole + recv_y[k - 1, t].astype(F32)
        acc[t] = whole
        for k in range(1, nx):
            there = pl.ds(pl.multiple_of(me.at("x", k) * quarter, 8), quarter)
            send_x[k - 1, t] = acc[t, there].astype(BF16)
            x_copy(k, t).start()

    def step_x(t):
        for k in range(1, nx):
            x_copy(k, t).wait_recv()
        here = pl.ds(pl.multiple_of(x * quarter, 8), quarter)
        whole = acc[t, here]
        for k in range(1, nx):
            whole = whole + recv_x[k - 1, t].astype(F32)
        acc[t, here] = whole
        away = pl.ds(pl.multiple_of(x * quarter + (1 - odd) * 2 * sub, 8), 2 * sub)
        send_n[t] = acc[t, away].astype(BF16)
        near_copy(t).start()

    def step_near(t):
        near_copy(t).wait_recv()
        here = pl.ds(pl.multiple_of(x * quarter + odd * 2 * sub, 8), 2 * sub)
        acc[t, here] = acc[t, here] + recv_n[t].astype(F32)
        away = x * quarter + odd * 2 * sub + (1 - half) * sub
        send_f[t] = acc[t, pl.ds(pl.multiple_of(away, 8), sub)].astype(BF16)
        far_copy(t).start()

    def step_far(t):
        far_copy(t).wait_recv()
        here = x * quarter + odd * 2 * sub + half * sub
        whole = acc[t, pl.ds(pl.multiple_of(here, 8), sub)] + recv_f[t].astype(F32)
        red[t] = whole.astype(BF16)
        keep_copy(t).start()
        far_back(t).start()

    def step_far_back(t):
        keep_copy(t).wait()
        far_back(t).wait_recv()
        near_back(t).start()

    def step_near_back(t):
        near_back(t).wait_recv()
        for k in range(1, nx):
            xa_copy(k, t).start()

    def step_xa(t):
        for k in range(1, nx):
            xa_copy(k, t).wait_recv()

    hat_copy.wait()
    lag = 2
    steps = ny * TG

    @pl.loop(0, steps + lag)
    def _(j):
        @pl.when(j < steps)
        def _():
            k, t = lax.rem(1 + j, ny), j // ny
            slot = lax.rem(j, TG)

            @pl.when(j < ny)
            def _():
                gkv_load(k, 1 - c).wait()
                gkv_load(k, c).wait()

            @pl.when(j == 3)
            def _():
                for copy in (wkv_copy, up_copy, down_copy, wq_load):
                    copy.start()

            @pl.when(j >= TG)
            def _():
                core_copy(slot).wait_send()

            send_c[slot] = grad_rows(k, t, 1 - c).astype(BF16)
            core_copy(slot).start()

        @pl.when(j >= lag)
        def _():
            i = j - lag
            k, t = lax.rem(1 + i, ny), i // ny
            slot = lax.rem(i, TG)
            mine = grad_rows(k, t, c)
            core_copy(slot).wait_recv()
            mine = mine + recv_c[slot].astype(F32)

            @pl.when(k == 0)
            def _():
                for h in range(per_g):
                    acc[per_g * t + h] = mine[h * chunk : (h + 1) * chunk]

            @pl.when(k > 0)
            def _():
                for step in range(1, ny):

                    @pl.when(k == step)
                    def _():
                        for h in range(per_g):
                            low = mine[h * chunk : (h + 1) * chunk].astype(BF16)
                            send_y[step - 1, per_g * t + h] = low
                            y_copy(step, per_g * t + h).start()

        @pl.when(j == 3)
        def _():
            att.next(0)
            gq.to_c()

        @pl.when(j == 5)
        def _():
            latent_queries()

        for at, action, t in ((6, step_y, 0), (9, step_y, 1), (10, step_x, 0)):

            @pl.when(j == at)
            def _():
                action(t)

        @pl.when(j == 11)
        def _():
            branch.next(0)

        @pl.when(j == 9)
        def _():
            mid.next(0)
            gq.finish_c()

    for t in range(TG):
        core_copy(t).wait_send()
    wkv_copy.wait()
    up_copy.wait()
    down_copy.wait()

    gbuf[...] = part_r[...]
    media_rows = media_h.shape[0]
    tile = media_t.shape[1]
    n_media = media_rows // tile

    def media_load(u):
        return pltpu.make_async_copy(
            media_h.at[pl.ds(pl.multiple_of(u * tile, tile), tile)],
            media_t.at[lax.rem(u, 2)],
            tile_sem.at[lax.rem(u, 2)],
        )

    def gm_store(u):
        return pltpu.make_async_copy(
            gm_t, gm_o.at[pl.ds(pl.multiple_of(u * tile, tile), tile)], out_sem.at[0]
        )

    def media_tile(u):
        @pl.when(u + 1 < n_media)
        def _():
            media_load(u + 1).start()

        rows = pl.ds(pl.multiple_of(u * tile, tile), tile)
        total = dg(gkv[0, rows], wkv[0], 1, 1)
        for a in range(1, pieces):
            total = total + dg(gkv[a, rows], wkv[a], 1, 1)
        media_load(u).wait()
        values = media_t[lax.rem(u, 2)].astype(F32)
        normed, inverse = normalize(values)
        gbuf[0:1] = gbuf[0:1] + jnp.sum(total * normed, axis=0, keepdims=True)
        result = norm_grad(total * gain_r[...].reshape(1, -1), normed, inverse)

        @pl.when(u >= 1)
        def _():
            gm_store(u - 1).wait()

        gm_t[...] = result.astype(BF16)
        gm_store(u).start()

    xt = mid_t.shape[1]
    n_ffn = NZ * (nx // xt)

    def rows_load(u):
        zz, xx = u // (nx // xt), lax.rem(u, nx // xt) * xt
        b = lax.rem(u, 2)
        return [
            pltpu.make_async_copy(
                mid_all.at[zz, pl.ds(xx, xt)], mid_t.at[b], tile_sem.at[2 + b]
            ),
            pltpu.make_async_copy(
                cot_all.at[zz, pl.ds(xx, xt)], cot_t.at[b], tile_sem.at[4 + b]
            ),
        ]

    def ffn_store(u):
        return [
            pltpu.make_async_copy(hid_t, hid_o.at[u], out_sem.at[1]),
            pltpu.make_async_copy(gp_t, gp_o.at[u], out_sem.at[2]),
        ]

    def ffn_tile(u):
        @pl.when(u + 1 < n_ffn)
        def _():
            for copy in rows_load(u + 1):
                copy.start()

        for copy in rows_load(u):
            copy.wait()

        @pl.when(u >= 1)
        def _():
            for copy in ffn_store(u - 1):
                copy.wait()

        b = lax.rem(u, 2)
        mid_rows = mid_t[b].reshape(-1, feat)
        cot_rows = cot_t[b].reshape(-1, feat)
        width = up.shape[1] // 3
        for part in range(3):
            cols = pl.ds(part * width, width)
            pre = dg(mid_rows, up[:, cols], 1, 0)
            grad = dg(cot_rows, down[cols, :], 1, 1)
            cdf = 0.5 * (1.0 + lax.erf(pre * (0.5**0.5)))
            slope = cdf + pre * (jnp.exp(-0.5 * pre * pre) * 0.3989422804014327)
            hid_t[:, cols] = (pre * cdf).astype(BF16)
            gp_t[:, cols] = (grad * slope).astype(BF16)
        for copy in ffn_store(u):
            copy.start()

    def latent_rows():
        rows = pl.ds(media_rows, lat_r.shape[0])
        total = dg(gkv[0, rows], wkv[0], 1, 1)
        for a in range(1, pieces):
            total = total + dg(gkv[a, rows], wkv[a], 1, 1)
        total = total + ql_out[y].astype(F32)
        for k in range(1, ny):
            ql_copy(k).wait_recv()
            total = total + ql_in[k - 1].astype(F32)
        normed, inverse = normalize(lat_r[...])
        gbuf[1:2] = jnp.sum(total * normed, axis=0, keepdims=True)
        glat_o[...] = gres_r[...] + norm_grad(total * gain_l[...].reshape(1, -1), normed, inverse)

    def comm(s):
        for lead, action in (
            (2, step_y),
            (1, step_x),
            (0, step_near),
            (-1, step_far),
            (-2, step_far_back),
            (-3, step_near_back),
        ):

            @pl.when(jnp.logical_and(s + lead >= max(lead, 0), s + lead < T))
            def _():
                action(s + lead)

    def gain_copies(axis, base):
        return [
            pltpu.make_async_remote_copy(
                src_ref=gbuf,
                dst_ref=grecv.at[base + k - 1],
                send_sem=g_send.at[base + k - 1],
                recv_sem=g_recv.at[base + k - 1],
                device_id=me.device(axis, k),
                device_id_type=MESH,
            )
            for k in range(1, me.size[axis])
        ]

    def gain_base(axis):
        return sum(me.size[a] - 1 for a in "cyxz"[: "cyxz".index(axis)])

    def gain_start(axis):
        for copy in gain_copies(axis, gain_base(axis)):
            copy.start()

    def gain_finish(axis):
        base = gain_base(axis)
        for copy in gain_copies(axis, base):
            copy.wait_send()
            copy.wait_recv()
        total = gbuf[...]
        for k in range(1, me.size[axis]):
            total = total + grecv[base + k - 1]
        gbuf[...] = total

    media_load(0).start()
    per = n_ffn // 4

    @pl.loop(0, T + 4)
    def _(s):
        comm(s)

        for i, copy in enumerate(gq.rest.copies(0)):

            @pl.when(s == i)
            def _():
                copy.start()

        @pl.when(s < n_media)
        def _():
            media_tile(s)

        @pl.when(s == n_media)
        def _():
            gm_store(n_media - 1).wait()
            latent_rows()
            gain_start("c")
            mid.finish(1)
            for copy in rows_load(0):
                copy.start()

        @pl.when(s == n_media + 1)
        def _():
            gain_finish("c")
            gain_start("x")

        @pl.when(jnp.logical_and(s > n_media, s < n_media + 5))
        def _():
            @pl.loop(0, per)
            def _(u):
                ffn_tile((s - n_media - 1) * per + u)

        @pl.when(s == 9)
        def _():
            gq.to_last()

        @pl.when(s == n_media + 4)
        def _():
            gain_finish("x")
            gain_start("z")

        @pl.when(s == n_media + 5)
        def _():
            for copy in ffn_store(n_ffn - 1):
                copy.wait()
            branch.next(1)

        @pl.when(s == n_media + 7)
        def _():
            gain_finish("z")
            gain_start("y")

        @pl.when(s == n_media + 10)
        def _():
            branch.next(2)

    @pl.loop(0, T)
    def _(t):
        step_xa(t)

    gain_finish("y")
    gains_o[...] = gbuf[...]
    branch.finish(3)
    gq.finish()
    att.finish(1)
    att.drain()
    mid.drain()
    branch.drain()
    gq.drain()
    for k in range(1, ny):
        ql_copy(k).wait_send()

    @pl.loop(0, T)
    def _(t):
        for k in range(1, ny):
            y_copy(k, t).wait_send()
        for k in range(1, nx):
            x_copy(k, t).wait_send()
            xa_copy(k, t).wait_send()
        for copy in (near_copy(t), far_copy(t), far_back(t), near_back(t)):
            copy.wait_send()


def tail(
    nx, ny, hat, gkv, wkv, up, down, media, cot_all, wq, gain_m, gain_l, lats, gres, gq, parts, branch, mid_all, att_all
):
    T = CHUNKS
    TG = 6
    rows, feat = hat.shape
    pieces, _, two = gkv.shape
    lat = branch.shape[0]
    ff = up.shape[1]
    blocks = nx * NZ
    chunk = feat // T
    sub = chunk // blocks
    xt = 256 // (lat * pieces)
    tile_rows = xt * pieces * lat
    tiles = NZ * nx // xt
    any_ = pl.BlockSpec(memory_space=pl.ANY)
    vm = pl.BlockSpec(memory_space=pltpu.VMEM)
    S = jax.ShapeDtypeStruct
    every = (NZ, nx, ny, 2, lat)
    V = pltpu.VMEM
    D = pltpu.SemaphoreType.DMA
    spread4 = NZ + nx + ny + 2 - 4
    media_rows = media.shape[0]
    outs = (
        S((T, blocks, sub, two), BF16),
        S((media_rows, feat), BF16),
        S((tiles, tile_rows, ff), BF16),
        S((tiles, tile_rows, ff), BF16),
        S(every + (feat,), BF16),
        S(every + (two // 2,), BF16),
        S(every + (feat,), BF16),
        S(every + (two // 2,), BF16),
        S((8, feat), F32),
        S(gres.shape, F32),
    )
    return pl.pallas_call(
        functools.partial(tail_kernel, nx, ny),
        out_shape=outs,
        in_specs=[any_] * 8 + [vm] * 7 + [any_] * 2,
        out_specs=(any_,) * 8 + (vm,) * 2,
        input_output_aliases={15: 4, 16: 5},
        scratch_shapes=[
            V(hat.shape, BF16),
            V(gkv.shape, BF16),
            V(wkv.shape, BF16),
            V(up.shape, BF16),
            V(down.shape, BF16),
            V((TG, feat // TG, two), BF16),
            V((TG, feat // TG, two), BF16),
            V((T, chunk, two), F32),
            V((ny - 1, T, chunk, two), BF16),
            V((ny - 1, T, chunk, two), BF16),
            V((nx - 1, T, NZ * sub, two), BF16),
            V((nx - 1, T, NZ * sub, two), BF16),
            V((T, 2 * sub, two), BF16),
            V((T, 2 * sub, two), BF16),
            V((T, sub, two), BF16),
            V((T, sub, two), BF16),
            V((T, sub, two), BF16),
            V((ny, 2, lat, two // 2), BF16),
            V((ny, lat, feat), BF16),
            V((ny - 1, lat, feat), BF16),
            V((2, 256, feat), BF16),
            V((256, feat), BF16),
            V((2, xt, ny, 2, lat, feat), BF16),
            V((2, xt, ny, 2, lat, feat), BF16),
            V((tile_rows, ff), BF16),
            V((tile_rows, ff), BF16),
            V(wq.shape, BF16),
            V((8, feat), F32),
            V((spread4, 8, feat), F32),
            D((6 + pieces,)),
            D((6,)),
            D((3,)),
            D((TG,)),
            D((TG,)),
            D((ny - 1, T)),
            D((ny - 1, T)),
            D((nx - 1, T)),
            D((nx - 1, T)),
            D((4, T)),
            D((4, T)),
            D((nx - 1, T)),
            D((nx - 1, T)),
            D((T,)),
            D((spread4,)),
            D((spread4,)),
            D((spread4,)),
            D((spread4,)),
            D((spread4,)),
            D((spread4,)),
            D((ColumnGather.slots(nx, ny),)),
            D((ColumnGather.slots(nx, ny),)),
            D((ny - 1,)),
            D((ny - 1,)),
            D((spread4,)),
            D((spread4,)),
            D((4,)),
        ],
        compiler_params=pltpu.CompilerParams(
            collective_id=3, has_side_effects=True, vmem_limit_bytes=67043328
        ),
        name="tail",
    )(
        hat, gkv, wkv, up, down, media, cot_all, wq, gain_m, gain_l, lats, gres, gq, parts, branch, mid_all, att_all
    )


def post_kernel(
    hid_h,
    gp_h,
    mid_h,
    cot_h,
    branch_h,
    lat_h,
    att_h,
    gq_h,
    kv_h,
    gm_h,
    res_r,
    lat_r,
    gains_r,
    down_o,
    up_o,
    out_o,
    qkv_o,
    media_o,
    res_o,
    lat_o,
    one_o,
    two_o,
    three_o,
    left,
    right,
    small,
    tiles,
    media_in,
    media_out,
    in_sem,
    tile_sem,
    min_sem,
    mout_sem,
):
    rows = left.shape[1]
    n_k = hid_h.shape[0] // rows
    cols = att_h.shape[1]
    width = tiles.shape[1]
    n_media = gm_h.shape[0] // media_in.shape[1]
    counts = {"tile": 0, "media": 0}
    depth = media_out.shape[0]

    def media_load(i):
        size = media_in.shape[1]
        return pltpu.make_async_copy(
            gm_h.at[pl.ds(i * size, size)], media_in.at[i], min_sem.at[i]
        )

    def media_store(i):
        size = media_in.shape[1]
        return pltpu.make_async_copy(
            media_out.at[i % depth], media_o.at[pl.ds(i * size, size)], mout_sem.at[i % depth]
        )

    def media_step():
        i = counts["media"]
        if i >= n_media:
            return
        counts["media"] = i + 1
        media_load(i).wait()
        if i >= depth:
            media_store(i - depth).wait()
        media_out[i % depth] = media_in[i].astype(F32)
        media_store(i).start()

    pending = [None] * tiles.shape[0]

    def emit(value, target):
        i = counts["tile"] % len(pending)
        counts["tile"] += 1
        if pending[i] is not None:
            pending[i].wait()
        a, b = value.shape
        tiles[i, 0:a, 0:b] = value
        pending[i] = pltpu.make_async_copy(
            tiles.at[i, pl.ds(0, a), pl.ds(0, b)], target, tile_sem.at[i]
        )
        pending[i].start()

    def load(slot, a, b, k):
        part = pl.ds(k * rows, rows)
        return [
            pltpu.make_async_copy(a.at[part], left.at[slot, :, pl.ds(0, a.shape[1])], in_sem.at[2 * slot]),
            pltpu.make_async_copy(b.at[part], right.at[slot, :, pl.ds(0, b.shape[1])], in_sem.at[2 * slot + 1]),
        ]

    jobs = [
        (hid_h, cot_h, down_o),
        (mid_h, gp_h, up_o),
        (att_h, branch_h, out_o),
        (lat_h, gq_h, qkv_o.at[0]),
    ]
    loads = [load(i, a, b, 0) for i, (a, b, unused) in enumerate(jobs)]
    kv_loads = [
        pltpu.make_async_copy(kv_h.at[:, pl.ds(i * cols, cols)], small.at[i], in_sem.at[8 + i])
        for i in range(2)
    ]
    for copy in loads[0] + loads[1]:
        copy.start()
    for i in range(n_media):
        media_load(i).start()
    for copy in loads[2] + loads[3] + kv_loads:
        copy.start()
    res_o[...] = res_r[...]
    lat_o[...] = lat_r[...]
    for i, ref in enumerate((one_o, two_o, three_o)):
        ref[...] = gains_r[i]
    for i, (a, b, target) in enumerate(jobs):
        for copy in loads[i]:
            copy.wait()
        slot = i
        m, n = a.shape[1], b.shape[1]
        for at in range(0, m, width):
            step = min(width, m - at)
            value = dg(left[slot, :, at : at + step], right[slot, :, 0:n], 0, 0)
            emit(value, target.at[pl.ds(at, step), pl.ds(0, n)])
            media_step()
    while counts["media"] < n_media:
        media_step()
    for i in range(2):
        kv_loads[i].wait()
        for at in range(0, kv_h.shape[0], width):
            value = small[i, at : at + width].astype(F32)
            emit(value, qkv_o.at[1 + i, pl.ds(at, width)])
    for copy in pending:
        copy.wait()
    for i in range(max(n_media - depth, 0), n_media):
        media_store(i).wait()


def post(hid, gp, mid, cot, branch, lat, att, gq, kv, gm, res, glat, gains):
    S = jax.ShapeDtypeStruct
    V = pltpu.VMEM
    D = pltpu.SemaphoreType.DMA
    any_ = pl.BlockSpec(memory_space=pl.ANY)
    rows, ff = hid.shape
    feat = mid.shape[1]
    cols = att.shape[1]
    wide = max(feat, ff)
    args = (hid, gp, mid, cot, branch, lat, att, gq, kv, gm)
    vm = pl.BlockSpec(memory_space=pltpu.VMEM)
    return pl.pallas_call(
        post_kernel,
        out_shape=(
            S((ff, feat), F32),
            S((feat, ff), F32),
            S((cols, feat), F32),
            S((3, feat, cols), F32),
            S(gm.shape, F32),
            S(res.shape, F32),
            S(glat.shape, F32),
            S((feat,), F32),
            S((feat,), F32),
            S((feat,), F32),
        ),
        in_specs=[any_] * len(args) + [vm] * 3,
        out_specs=(any_,) * 5 + (vm,) * 5,
        scratch_shapes=[
            V((4, rows, wide), BF16),
            V((4, rows, wide), BF16),
            V((2, feat, cols), BF16),
            V((4, 256, wide), F32),
            V((gm.shape[0] // 64, 64, feat), BF16),
            V((4, 64, feat), F32),
            D((10,)),
            D((4,)),
            D((gm.shape[0] // 64,)),
            D((4,)),
        ],
        compiler_params=pltpu.CompilerParams(vmem_limit_bytes=67043328),
        name="weights",
    )(*args, res, glat, gains)


def full_sum(x):
    return jnp.sum(jnp.sum(x, axis=1, keepdims=True), axis=0, keepdims=True)


class Relay:
    def __init__(self, me, own, buf, order, send, recv):
        self.me, self.own, self.buf, self.order = me, own, buf, order
        self.send, self.recv = send, recv
        ny, nx = me.size["y"] - 1, me.size["x"] - 1
        sizes = {"o": 1, "y": ny, "x": ny * nx, "z": ny, "c": ny}
        self.base, total = {}, 0
        for a in "oyxzc":
            self.base[a] = total
            total += sizes[a]

    @staticmethod
    def slots(nx, ny):
        return 1 + 3 * (ny - 1) + (ny - 1) * (nx - 1)

    def part(self, done):
        me = self.me
        index = []
        if "x" in self.order:
            index.append(pl.ds(0, me.size["x"]) if "x" in done else me.own["x"])
        if "z" in self.order:
            index.append(pl.ds(0, 2) if "z" in done else lax.rem(me.own["z"], 2))
        return tuple(index)

    def copies(self, phase):
        me, buf = self.me, self.buf
        y, c = me.own["y"], me.own["c"]
        out = []

        def add(src, dst, where):
            i = self.base[phase] + len(out)
            out.append(
                pltpu.make_async_remote_copy(
                    src_ref=src,
                    dst_ref=dst,
                    send_sem=self.send.at[i],
                    recv_sem=self.recv.at[i],
                    device_id=where,
                    device_id_type=MESH,
                )
            )

        if phase == "o":
            add(self.own, buf.at[y, c], me.device("c", 1))
            return out
        done = self.order[1 : self.order.index(phase)] if phase in "xz" else ""
        for k in range(1, me.size["y"]):
            if phase == "y":
                at = self.part("")
                src = self.own.at[at] if at else self.own
                add(src, buf.at[(y, c) + at], me.device("y", k))
                continue
            yk = me.at("y", me.size["y"] - k)
            if phase == "c":
                add(buf.at[yk, c], buf.at[yk, c], me.device("c", 1))
                continue
            ref = buf.at[(yk, c) + self.part(done)]
            if phase == "z":
                add(ref, ref, me.device("z", 1 - 2 * lax.rem(me.own["z"], 2) + NZ))
            else:
                for j in range(1, me.size["x"]):
                    add(ref, ref, me.device("x", j))
        return out

    def start(self, phase):
        for copy in self.copies(phase):
            copy.start()

    def wait(self, phase):
        for copy in self.copies(phase):
            copy.wait_recv()

    def next(self, phase):
        self.wait(phase)
        at = self.order.index(phase) + 1
        self.start(self.order[at] if at < len(self.order) else "c")

    def drain(self):
        for phase in "o" + self.order + "c":
            for copy in self.copies(phase):
                copy.wait_send()


def front_kernel(
    nx,
    ny,
    aligned,
    count_s,
    lat_r,
    cot_r,
    gain_m,
    gain_l,
    gain_f,
    media_h,
    kvw_h,
    wq_h,
    out_h,
    up_h,
    down_h,
    hat_o,
    gkv_o,
    wkv_all,
    wq_o,
    o_all,
    cot_all,
    lat_all,
    att_all,
    mid_all,
    branch_o,
    gq_o,
    gres_o,
    output_o,
    part_o,
    hat,
    kv,
    wkv_own,
    wbuf,
    wq_v,
    o_v,
    up,
    down,
    media_t,
    lat_y,
    q_y,
    q64,
    pexp,
    probs,
    stat,
    stat_in,
    o64,
    o_in,
    att64,
    att_low,
    att_y,
    g64,
    mid_ha,
    cot_ha,
    hid,
    gpre,
    ghid,
    sums,
    sums_in,
    load_sem,
    tile_sem,
    wload_sem,
    store_sem,
    w_send,
    w_recv,
    u_send,
    u_recv,
    qy_send,
    qy_recv,
    pair_send,
    pair_recv,
    st_send,
    st_recv,
    ha_send,
    ha_recv,
    ct_send,
    ct_recv,
    lt_send,
    lt_recv,
    at_send,
    at_recv,
    md_send,
    md_recv,
    own_sem,
):
    me = Where(nx, ny)
    y, c = me.own["y"], me.own["c"]
    group = 2 * ny
    place = lax.axis_index("ha")
    lat = lat_r.shape[0]
    media_rows = media_h.shape[0]
    rows = hat.shape[0]
    feat = hat.shape[1]
    cols = q64.shape[-1]
    heads = cols // HEAD
    scale = HEAD ** (-0.5)
    partner = me.device("c", 1)
    n_w = wkv_own.shape[0]
    n_o = o_v.shape[1]

    def load(i, src, dst):
        return pltpu.make_async_copy(src, dst, load_sem.at[i])

    wkv_loads = (
        [
            load(0, kvw_h.at[1], wkv_own.at[..., pl.ds(0, cols)]),
            load(1, kvw_h.at[2], wkv_own.at[..., pl.ds(cols, cols)]),
        ]
        if aligned
        else [load(0, kvw_h, wkv_own)]
    )
    up_load, down_load = load(2, up_h, up), load(3, down_h, down)
    wq_load = load(4, wq_h.at[0], wq_v.at[c])
    o_load = load(5, out_h, o_v.at[place])
    for copy in wkv_loads:
        copy.start()
    tile = media_t.shape[1]
    tiles = media_rows // tile

    def media_load(u):
        return pltpu.make_async_copy(
            media_h.at[pl.ds(pl.multiple_of(u * tile, tile), tile)],
            media_t.at[lax.rem(u, 2)],
            tile_sem.at[lax.rem(u, 2)],
        )

    media_load(0).start()
    wq_load.start()
    down_load.start()
    up_load.start()
    o_load.start()

    barrier = pltpu.get_barrier_semaphore()
    greeted = [me.device(a, k) for a in "cyxz" for k in range(1, me.size[a])]
    for k in range(1, ny):
        greeted.append({"sa": lax.axis_index("sa"), "ha": me.at("y", k) * 2 + 1 - c})
    for where in greeted:
        pl.semaphore_signal(barrier, inc=1, device_id=where, device_id_type=MESH)
    pl.semaphore_wait(barrier, len(greeted))

    both = (pl.ds(0, ny), pl.ds(0, 2))
    relays = [
        Relay(
            me,
            wkv_own.at[i],
            wkv_all.at[both + (i,)],
            ("yxz", "yzx")[i % 2],
            w_send.at[i],
            w_recv.at[i],
        )
        for i in range(n_w)
    ]
    o_relays = [
        Relay(
            me,
            out_h.at[i],
            o_all.at[both + (i,)],
            "yx" if i == 0 else "yz",
            u_send.at[i],
            u_recv.at[i],
        )
        for i in range(n_o)
    ]
    gather_cot = Gather(me, cot_r, cot_all, "zyxc", ct_send, ct_recv, own_sem.at[0])
    own_lat = hat.at[pl.ds(media_rows, lat)]
    gather_lat = Gather(me, own_lat, lat_all, "yzxc", lt_send, lt_recv, own_sem.at[1])
    gather_att = ColumnGather(
        me, att_low, att_y, att_all, "xz", at_send, at_recv, own_sem.at[pl.ds(2, 2)]
    )

    def remote(src, dst, send, recv, where):
        return pltpu.make_async_remote_copy(
            src_ref=src,
            dst_ref=dst,
            send_sem=send,
            recv_sem=recv,
            device_id=where,
            device_id_type=MESH,
        )

    def pair_copy(i, src, dst):
        return remote(src, dst, pair_send.at[i], pair_recv.at[i], partner)

    def ha_copies(base, source, target):
        out = []
        for k in range(1, group):
            there = lax.rem(place + k, group)
            out.append(
                remote(
                    source(there),
                    target(k),
                    ha_send.at[base, k - 1],
                    ha_recv.at[base, k - 1],
                    {"sa": lax.axis_index("sa"), "ha": there},
                )
            )
        return out

    cot_copies = ha_copies(0, lambda there: cot_r, lambda k: cot_ha.at[place])
    mid_copies = ha_copies(1, lambda there: mid_ha.at[y, c], lambda k: mid_ha.at[y, c])
    gmid_copies = ha_copies(2, lambda there: sums.at[0, there], lambda k: sums_in.at[0, k - 1])
    ffn_copies = ha_copies(3, lambda there: sums.at[1, there], lambda k: sums_in.at[1, k - 1])
    lat_copies = [
        remote(own_lat, lat_y.at[y], qy_send.at[0, k - 1], qy_recv.at[0, k - 1], me.device("y", k))
        for k in range(1, ny)
    ]
    back_copies = [
        remote(
            q_y.at[me.at("y", k)],
            q64.at[pl.ds(2 * y, 2), c],
            qy_send.at[1, k - 1],
            qy_recv.at[1, k - 1],
            me.device("y", k),
        )
        for k in range(1, ny)
    ]
    wq_copy = pair_copy(5, wq_h.at[0], wq_v.at[c])

    gather_cot.start(0)
    normed, unused = normalize(lat_r[...])
    low = (normed * gain_l[...].reshape(1, -1)).astype(BF16)
    hat[pl.ds(media_rows, lat)] = low
    lat_y[y] = low
    for copy in lat_copies:
        copy.start()
    for copy in wkv_loads:
        copy.wait()
    for relay in relays:
        relay.start("o")
        relay.start("y")
    wq_copy.start()
    for relay in o_relays:
        relay.start("o")
    cot_ha[place] = cot_r[...]
    own_store = pltpu.make_async_copy(wkv_own, wkv_all.at[y, c], store_sem.at[0])
    own_store.start()

    @pl.loop(0, tiles)
    def _(u):
        @pl.when(u + 1 < tiles)
        def _():
            media_load(u + 1).start()

        media_load(u).wait()
        normed, unused = normalize(media_t[lax.rem(u, 2)].astype(F32))
        hat[pl.ds(pl.multiple_of(u * tile, tile), tile)] = (normed * gain_m[...].reshape(1, -1)).astype(BF16)

    hat_store = pltpu.make_async_copy(hat, hat_o, store_sem.at[1])
    hat_store.start()
    step = rows // 4

    def project(weights, piece):
        @pl.loop(0, 4)
        def _(u):
            part = pl.ds(pl.multiple_of(u * step, 8), step)
            w = weights[...].reshape(feat, 2 * cols)
            kv[piece, part] = dg(hat[part], w, 1, 0).astype(BF16)

    def weight_load(slot, ya, ca):
        return pltpu.make_async_copy(wkv_all.at[ya, ca], wbuf.at[slot], wload_sem.at[slot])

    project(wkv_own, place)
    for relay in relays:
        relay.wait("o")
    weight_load(0, y, 1 - c).start()
    relays[0].next("y")
    weight_load(0, y, 1 - c).wait()
    project(wbuf.at[0], 2 * y + 1 - c)
    relays[1].next("y")
    relays[0].next("x")
    wq_load.wait()
    wq_copy.wait_recv()
    for copy in lat_copies:
        copy.wait_recv()
    wq_store = pltpu.make_async_copy(wq_v, wq_o, store_sem.at[2])
    wq_store.start()
    all_lat = lat_y[...].reshape(ny * lat, feat)
    for ca in range(2):
        w = wq_v[ca].reshape(feat, cols)
        q_y[pl.ds(0, ny), ca] = dg(all_lat, w, 1, 0).astype(BF16).reshape(ny, lat, cols)
    q64[2 * y, c] = q_y[y, 0]
    q64[2 * y + 1, c] = q_y[y, 1]
    for copy in back_copies:
        copy.start()
    relays[2].next("y")
    for relay in o_relays:
        relay.start("y")
    for copy in cot_copies:
        copy.start()
    gather_lat.start(0)
    gather_cot.next(0)
    relays[1].next("z")
    relays[3].next("y")
    for copy in back_copies:
        copy.wait_recv()
    q_copy = pair_copy(0, q64.at[pl.ds(0, group), c], q64.at[pl.ds(0, group), c])
    q_copy.start()
    relays[2].next("x")

    lane = lax.broadcasted_iota(jnp.int32, (2 * lat, cols), 1)

    def inside(h):
        return jnp.logical_and(lane >= h * HEAD, lane < (h + 1) * HEAD)

    def spread(x):
        return jnp.concatenate(
            [jnp.where(inside(h), x, jnp.zeros_like(x)) for h in range(heads)], axis=0
        )

    def merge(x):
        total = jnp.where(inside(0), x[: 2 * lat], 0.0)
        for h in range(1, heads):
            total = total + jnp.where(inside(h), x[2 * lat * h : 2 * lat * (h + 1)], 0.0)
        return total

    tall = heads * 2 * lat
    limit = count_s[y] * PATCH - c * media_rows
    key = lax.broadcasted_iota(jnp.int32, (tall, rows), 1)
    half = lax.broadcasted_iota(jnp.int32, (tall, 128), 1) < 64

    def stat_copy(a):
        return remote(stat.at[a], stat_in.at[a], st_send.at[a], st_recv.at[a], partner)

    def attend(ya):
        @pl.loop(0, 2)
        def _(ca):
            a = 2 * ya + ca
            q_blk = spread(q64[a].reshape(2 * lat, cols))
            scores = dg(q_blk, kv[a, :, pl.ds(0, cols)], 1, 1) * scale
            usable = jnp.logical_or(key < limit, key >= media_rows)
            scores = jnp.where(usable, scores, NEG)
            top = jnp.max(scores, axis=-1, keepdims=True)
            value = jnp.exp(scores - top)
            pexp[a] = value
            total = jnp.sum(value, axis=-1, keepdims=True)
            stat[a] = jnp.where(half, top, total)
            stat_copy(a).start()

    def settle(ya):
        @pl.loop(0, 2)
        def _(ca):
            a = 2 * ya + ca
            stat_copy(a).wait_recv()
            top, total = stat[a, :, 0:1], stat[a, :, 64:65]
            top_in, total_in = stat_in[a, :, 0:1], stat_in[a, :, 64:65]
            top_all = jnp.maximum(top, top_in)
            mine = jnp.exp(top - top_all)
            denom = total * mine + total_in * jnp.exp(top_in - top_all)
            low = (pexp[a] * (mine / denom)).astype(BF16)
            probs[a] = low
            o64[a] = merge(dg(low, kv[a, :, pl.ds(cols, cols)], 1, 0)).reshape(2, lat, cols)

    q_copy.wait_recv()
    attend(y)
    relays[0].next("z")
    relays[3].next("z")
    settle(y)
    relays[1].next("x")
    relays[2].next("z")
    relays[3].next("x")
    for k in range(1, ny):
        yk = me.at("y", ny - k)
        weight_load(1, yk, c).start()
        if k == 1:
            for relay in o_relays:
                relay.next("y")
        weight_load(1, yk, c).wait()
        project(wbuf.at[1], 2 * yk + c)
        if k == 1:
            for relay in relays:
                relay.wait("c")
        weight_load(0, yk, 1 - c).start()
        if k == 1:
            for relay in o_relays:
                relay.next(relay.order[1])
            gather_lat.next(0)
            gather_cot.next(1)
        weight_load(0, yk, 1 - c).wait()
        project(wbuf.at[0], 2 * yk + 1 - c)
        attend(yk)
    down_load.wait()
    for copy in cot_copies:
        copy.wait_recv()
    ghid[...] = dg(cot_ha[...].reshape(group * lat, feat), down[...], 1, 1)
    for k in range(1, ny):
        settle(me.at("y", ny - k))

    o_copy = pair_copy(1, o64.at[pl.ds(0, group), 1 - c], o_in)
    o_copy.start()
    o_loads = []
    for relay in o_relays:
        relay.wait("o")
        relay.wait("c")
    others = [(y, 1 - c)]
    for k in range(1, ny):
        others += [(me.at("y", ny - k), c), (me.at("y", ny - k), 1 - c)]
    for i, (ya, ca) in enumerate(others):
        o_loads.append(load(6 + i, o_all.at[ya, ca], o_v.at[2 * ya + ca]))
        o_loads[-1].start()
    o_load.wait()
    for copy in o_loads:
        copy.wait()
    o_copy.wait_recv()
    branch = jnp.zeros((lat, feat), F32)
    for a in range(group):
        mine = o64[a, c] + o_in[a]
        att64[a, c] = mine
        low = mine.astype(BF16)
        att_low[a] = low
        branch = branch + dg(low, o_v[a].reshape(cols, feat), 1, 0)
    att_copy = pair_copy(2, att64.at[pl.ds(0, group), c], att64.at[pl.ds(0, group), c])
    residual = lat_r[...] + branch
    mid_norm, mid_inv = normalize(residual)
    mid_low = (mid_norm * gain_f[...].reshape(1, -1)).astype(BF16)
    mid_ha[y, c] = mid_low
    for copy in mid_copies:
        copy.start()
    att_copy.start()
    gather_att.start()
    part_o[...] = jnp.zeros_like(part_o)
    spot = lax.broadcasted_iota(jnp.int32, (1, feat), 1)
    squares = jnp.where(spot == 0, full_sum(residual * residual), 0.0)
    squares = squares + jnp.where(spot == 1, full_sum(branch * branch), 0.0)
    up_load.wait()
    for copy in mid_copies:
        copy.wait_recv()
    mid_keep = pltpu.make_async_copy(
        mid_ha.at[pl.ds(0, ny), c],
        mid_all.at[me.own["z"], me.own["x"], pl.ds(0, ny), c],
        own_sem.at[4],
    )
    gather_mid = Gather(me, None, mid_all, "z", md_send, md_recv, None, "y")
    mid_keep.start()
    pre = dg(mid_ha[...].reshape(group * lat, feat), up[...], 1, 0)
    cdf = 0.5 * (1.0 + lax.erf(pre * (0.5**0.5)))
    slope = cdf + pre * (jnp.exp(-0.5 * pre * pre) * 0.3989422804014327)
    gpre[...] = (ghid[...] * slope).astype(BF16)
    hid[...] = (pre * cdf).astype(BF16)
    sums[0] = dg(gpre[...], up[...], 1, 1).reshape(group, lat, feat).astype(BF16)
    for copy in gmid_copies:
        copy.start()
    grad_mid = sums[0, place].astype(F32)
    sums[1] = dg(hid[...], down[...], 1, 0).reshape(group, lat, feat).astype(BF16)
    gather_att.to_c()
    mid_keep.wait()
    gather_mid.start(0)
    gather_lat.next(1)
    gather_cot.next(2)
    for k, copy in enumerate(gmid_copies):
        copy.wait_recv()
        grad_mid = grad_mid + sums_in[0, k].astype(F32)
    for copy in ffn_copies:
        copy.start()
    grad_res = cot_r[...].astype(F32) + norm_grad(grad_mid * gain_f[...].reshape(1, -1), mid_norm, mid_inv)
    gres_o[...] = grad_res
    grad_low = grad_res.astype(BF16)
    branch_o[...] = grad_low
    for a in range(group):
        g64[a, c] = dg(grad_low, o_v[a].reshape(cols, feat), 1, 1).astype(BF16)
    g_copy = pair_copy(3, g64.at[pl.ds(0, group), c], g64.at[pl.ds(0, group), c])
    g_copy.start()
    part_o[2:3] = jnp.sum(grad_mid * mid_norm, axis=0, keepdims=True)
    att_copy.wait_recv()
    o_copy.wait_send()
    for a in range(group):
        stat_copy(a).wait_send()
    g_copy.wait_recv()

    def gkv_store(a):
        return pltpu.make_async_copy(kv.at[a], gkv_o.at[a], st_send.at[a])

    @pl.loop(0, group)
    def _(a):
        q_blk = spread(q64[a].reshape(2 * lat, cols))
        g_blk = spread(g64[a].reshape(2 * lat, cols))
        att = att64[a].reshape(2 * lat, cols)
        inner = jnp.sum(
            g_blk.astype(F32) * jnp.concatenate([att] * heads, axis=0), axis=-1, keepdims=True
        )
        keys = kv[a, :, pl.ds(0, cols)]
        low = probs[a]
        grad = dg(g_blk, kv[a, :, pl.ds(cols, cols)], 1, 1)
        grad = (low.astype(F32) * (grad - inner)).astype(BF16)
        o64[a] = (merge(dg(grad, keys, 1, 0)) * scale).reshape(2, lat, cols)
        kv[a, :, pl.ds(0, cols)] = (dg(grad, q_blk, 0, 0) * scale).astype(BF16)
        kv[a, :, pl.ds(cols, cols)] = dg(low, g_blk, 0, 0).astype(BF16)
        gkv_store(a).start()

    gq_copy = pair_copy(4, o64.at[pl.ds(0, group), 1 - c], o_in)
    gq_copy.start()
    for copy in ffn_copies:
        copy.wait_recv()
    ffn = sums[1, place].astype(F32)
    for k in range(1, group):
        ffn = ffn + sums_in[1, k - 1].astype(F32)
    output_o[...] = residual + ffn
    squares = squares + jnp.where(spot == 2, full_sum(ffn * ffn), 0.0)
    part_o[3:4] = squares
    gq_copy.wait_recv()
    for a in range(group):
        gq_o[a] = (o64[a, c] + o_in[a]).astype(BF16)
    gather_lat.next(2)
    gather_cot.finish(3)
    gather_lat.finish(3)
    gather_att.finish_c()
    gather_mid.finish(0)
    for gather in (gather_cot, gather_lat, gather_mid):
        gather.drain()
    gather_att.drain_c()
    own_store.wait()
    wq_store.wait()
    hat_store.wait()
    for a in range(group):
        gkv_store(a).wait()
    for relay in relays + o_relays:
        relay.drain()
    for copy in (q_copy, att_copy, g_copy, gq_copy, wq_copy):
        copy.wait_send()
    for copies in (cot_copies, mid_copies, gmid_copies, ffn_copies, lat_copies, back_copies):
        for copy in copies:
            copy.wait_send()


def front(nx, ny, counts, latents, cot, gain_m, gain_l, gain_f, media, qkv, out_w, up, down):
    group = 2 * ny
    media_rows, feat = media.shape
    lat = latents.shape[0]
    rows = media_rows + lat
    cols = qkv.shape[-1]
    ff = up.shape[1]
    aligned = cols % 128 == 0
    tall = cols // HEAD * 2 * lat
    any_ = pl.BlockSpec(memory_space=pl.ANY)
    vm = pl.BlockSpec(memory_space=pltpu.VMEM)
    S = jax.ShapeDtypeStruct
    V = pltpu.VMEM
    D = pltpu.SemaphoreType.DMA
    every = (NZ, nx, ny, 2, lat)
    n_w = 4
    n_o = 2 if nx == 2 else 1
    half = (n_w, nx, 2, feat // (2 * nx * n_w))
    o_part = (n_o, nx, cols // (nx * n_o), feat)
    if aligned:
        wkv = qkv.reshape((3,) + half + (cols,))
    else:
        wkv = jnp.concatenate([qkv[1], qkv[2]], axis=-1).reshape(half + (2 * cols,))
    spread4 = NZ + nx + ny + 2 - 4
    slots = Relay.slots(nx, ny)
    outs = (
        S((rows, feat), BF16),
        S((group, rows, 2 * cols), BF16),
        S((ny, 2) + half + (2 * cols,), BF16),
        S((2, feat, cols), BF16),
        S((ny, 2) + o_part, BF16),
        S(every + (feat,), BF16),
        S(every + (feat,), BF16),
        S(every + (cols,), BF16),
        S(every + (feat,), BF16),
        S((lat, feat), BF16),
        S((group, lat, cols), BF16),
        S((lat, feat), F32),
        S((lat, feat), F32),
        S((8, feat), F32),
    )
    return pl.pallas_call(
        functools.partial(front_kernel, nx, ny, aligned),
        out_shape=outs,
        in_specs=[pl.BlockSpec(memory_space=pltpu.SMEM)] + [vm] * 5 + [any_] * 6,
        out_specs=(any_,) * 9 + (vm,) * 5,
        scratch_shapes=[
            V((rows, feat), BF16),
            V((group, rows, 2 * cols), BF16),
            V(half + (2 * cols,), BF16),
            V((2,) + half + (2 * cols,), BF16),
            V((2, feat, cols), BF16),
            V((group,) + o_part, BF16),
            V(up.shape, BF16),
            V(down.shape, BF16),
            V((2, 256, feat), BF16),
            V((ny, lat, feat), BF16),
            V((ny, 2, lat, cols), BF16),
            V((group, 2, lat, cols), BF16),
            V((group, tall, rows), F32),
            V((group, tall, rows), BF16),
            V((group, tall, 128), F32),
            V((group, tall, 128), F32),
            V((group, 2, lat, cols), F32),
            V((group, lat, cols), F32),
            V((group, 2, lat, cols), F32),
            V((group, lat, cols), BF16),
            V((ny, 2, lat, cols), BF16),
            V((group, 2, lat, cols), BF16),
            V((ny, 2, lat, feat), BF16),
            V((group, lat, feat), BF16),
            V((group * lat, ff), BF16),
            V((group * lat, ff), BF16),
            V((group * lat, ff), F32),
            V((2, group, lat, feat), BF16),
            V((2, group - 1, lat, feat), BF16),
            D((6 + group,)),
            D((2,)),
            D((2,)),
            D((3,)),
            D((n_w, slots)),
            D((n_w, slots)),
            D((n_o, slots)),
            D((n_o, slots)),
            D((2, ny - 1)),
            D((2, ny - 1)),
            D((6,)),
            D((6,)),
            D((group,)),
            D((group,)),
            D((4, group - 1)),
            D((4, group - 1)),
            D((spread4,)),
            D((spread4,)),
            D((spread4,)),
            D((spread4,)),
            D((ColumnGather.slots(nx, ny),)),
            D((ColumnGather.slots(nx, ny),)),
            D((NZ - 1,)),
            D((NZ - 1,)),
            D((5,)),
        ],
        compiler_params=pltpu.CompilerParams(
            collective_id=2, has_side_effects=True, vmem_limit_bytes=67043328
        ),
        name="front",
    )(
        counts,
        latents,
        cot,
        gain_m,
        gain_l,
        gain_f,
        media,
        wkv,
        qkv.reshape(3, feat, cols),
        out_w.reshape(o_part),
        up,
        down,
    )


def shards(
    media_tokens,
    latents,
    frame_counts,
    gain_media,
    gain_latent,
    gain_ffn,
    qkv_weight,
    out_weight,
    up_weight,
    down_weight,
    cotangent,
):
    group = lax.axis_size("ha")
    width = media_tokens.shape[1]
    lat = latents.shape[0]
    cols = qkv_weight.shape[2]
    entry_total = float(lat * width * lax.axis_size("sa") * group)
    nx, ny = lax.axis_size("sa") // NZ, group // 2
    gains_in = (gain_media, gain_latent, gain_ffn)
    (
        hat,
        gkv,
        wkv_all,
        wq_pair,
        unused,
        cot_all,
        lat_all,
        att_all,
        mid_all,
        grad_branch,
        grad_q,
        grad_residual,
        output,
        parts,
    ) = front(
        nx,
        ny,
        frame_counts,
        latents,
        cotangent,
        *gains_in,
        media_tokens,
        qkv_weight,
        out_weight,
        up_weight,
        down_weight,
    )
    kv, gm, hid, gp, mid_all, att_all, branch_all, gq_all, gains, grad_latents = tail(
        nx,
        ny,
        hat,
        gkv,
        wkv_all.reshape(group, width, 2 * cols),
        up_weight,
        down_weight,
        media_tokens,
        cot_all,
        wq_pair,
        gains_in[0],
        gains_in[1],
        latents,
        grad_residual,
        grad_q,
        parts,
        grad_branch,
        mid_all,
        att_all,
    )
    cot_all = cot_all.reshape(-1, width)
    lat_all = lat_all.reshape(-1, width)
    kv = kv.reshape(width, 2 * cols)
    hid = hid.reshape(-1, hid.shape[-1])
    gp = gp.reshape(-1, gp.shape[-1])
    mid_all = mid_all.reshape(-1, width)
    branch_all = branch_all.reshape(-1, width)
    att_all = att_all.reshape(-1, cols)
    gq_all = gq_all.reshape(-1, cols)
    args = (hid, gp, mid_all, cot_all, branch_all, lat_all, att_all, gq_all, kv, gm)
    if hid.shape[0] <= 1024:
        (
            grad_down,
            grad_up,
            grad_out,
            grad_qkv,
            grad_media,
            output,
            grad_latents,
            gain_one,
            gain_two,
            gain_three,
        ) = post(*args, output, grad_latents, gains)
    else:
        grad_media = gm.astype(F32)
        grad_out = dot("rc,rd->cd", att_all, branch_all)
        grad_wq = dot("rd,re->de", lat_all, gq_all)
        grad_down = dot("rf,rd->fd", hid, cot_all)
        grad_up = dot("rd,rf->df", mid_all, gp)
        grad_kv = jnp.stack([kv[:, :cols], kv[:, cols:]]).astype(F32)
        grad_qkv = jnp.concatenate([grad_wq[None], grad_kv], axis=0)
        gain_one, gain_two, gain_three = gains[0], gains[1], gains[2]
    square_sums = gains[3, :3]
    roots = jnp.sqrt(square_sums / entry_total)
    return (
        output,
        grad_media,
        grad_latents,
        gain_one,
        gain_two,
        gain_three,
        grad_qkv,
        grad_out,
        grad_up,
        grad_down,
        roots[0],
        roots[1],
        roots[2],
    )


def solution(mesh):
    placed = (
        P(("sa", "ha"), None),
        P(("sa", "ha"), None),
        P("sa"),
        P(),
        P(),
        P(),
        P(None, None, "ha"),
        P("ha", None),
        P(None, "ha"),
        P("ha", None),
        P(("sa", "ha"), None),
    )
    return jax.shard_map(
        shards,
        mesh=mesh,
        in_specs=placed,
        out_specs=(
            P(("sa", "ha"), None),
            P(("sa", "ha"), None),
            P(("sa", "ha"), None),
            P(),
            P(),
            P(),
            P(None, None, "ha"),
            P("ha", None),
            P(None, "ha"),
            P("ha", None),
            P(),
            P(),
            P(),
        ),
        check_vma=False,
    )
```

```python
import functools

import jax
import jax.numpy as jnp
from jax import lax
from jax.experimental import pallas as pl
from jax.experimental.pallas import tpu as pltpu
from jax.sharding import PartitionSpec as P

HEAD = 96
PATCH = 256
EPS = 1e-05
NEG = -1000000000.0
F32 = jnp.float32
BF16 = jnp.bfloat16


def normalize(values):
    centered = values - jnp.mean(values, axis=-1, keepdims=True)
    inverse = lax.rsqrt(jnp.mean(centered * centered, axis=-1, keepdims=True) + EPS)
    return centered * inverse, inverse


def norm_grad(grad, normed, inverse):
    first = jnp.mean(grad, axis=-1, keepdims=True)
    second = jnp.mean(grad * normed, axis=-1, keepdims=True)
    return inverse * (grad - first - normed * second)


def dot(spec, a, b):
    return jnp.einsum(spec, a, b, preferred_element_type=F32)


MESH = pl.DeviceIdType.MESH
NZ = 4
CHUNKS = 12


def dg(a, b, ca, cb):
    return lax.dot_general(a, b, (((ca,), (cb,)), ((), ())), preferred_element_type=F32)


class Where:
    def __init__(self, nx, ny):
        self.nx, self.ny = nx, ny
        sa, ha = lax.axis_index("sa"), lax.axis_index("ha")
        self.own = {"z": sa // nx, "x": sa % nx, "y": ha // 2, "c": ha % 2}
        self.size = {"z": NZ, "x": nx, "y": ny, "c": 2}

    def at(self, axis, k):
        return lax.rem(self.own[axis] + k, self.size[axis])

    def device(self, axis, k):
        p = dict(self.own)
        p[axis] = self.at(axis, k)
        return {"sa": p["z"] * self.nx + p["x"], "ha": p["y"] * 2 + p["c"]}


def greet(me):
    barrier = pltpu.get_barrier_semaphore()
    count = 0
    for axis in "cyxz":
        for k in range(1, me.size[axis]):
            pl.semaphore_signal(
                barrier, inc=1, device_id=me.device(axis, k), device_id_type=MESH
            )
            count += 1
    pl.semaphore_wait(barrier, count)


class Gather:
    def __init__(self, me, own, buf, order, send, recv, local, done=""):
        self.me, self.own, self.buf, self.order = me, own, buf, order
        self.send, self.recv, self.local = send, recv, local
        self.done = done

    def slot(self, done):
        me = self.me
        return tuple(
            pl.ds(0, me.size[a]) if a in done else me.own[a] for a in "zxyc"
        )

    def keep(self):
        return pltpu.make_async_copy(
            self.own, self.buf.at[self.slot(self.done)], self.local
        )

    def copies(self, phase):
        done = self.done + self.order[:phase]
        axis = self.order[phase]
        first = sum(self.me.size[a] - 1 for a in self.order[:phase])
        here = self.buf.at[self.slot(done)]
        src = self.own if phase == 0 and self.own is not None else here
        return [
            pltpu.make_async_remote_copy(
                src_ref=src,
                dst_ref=here,
                send_sem=self.send.at[first + k - 1],
                recv_sem=self.recv.at[first + k - 1],
                device_id=self.me.device(axis, k),
                device_id_type=MESH,
            )
            for k in range(1, self.me.size[axis])
        ]

    def start(self, phase):
        if phase == 0 and self.own is not None:
            self.keep().start()
        for c in self.copies(phase):
            c.start()

    def finish(self, phase):
        if phase == 0 and self.own is not None:
            self.keep().wait()
        for c in self.copies(phase):
            c.wait_recv()

    def next(self, phase):
        self.finish(phase)
        self.start(phase + 1)

    def drain(self):
        for phase in range(len(self.order)):
            for c in self.copies(phase):
                c.wait_send()


class ColumnGather:
    def __init__(self, me, own, land, buf, order, send, recv, local):
        self.me, self.own, self.land, self.buf = me, own, land, buf
        self.send, self.recv, self.local = send, recv, local
        n = NZ + me.size["x"] - 2
        first = me.size["y"]
        self.rest = Gather(
            me, None, buf, order, send.at[pl.ds(first, n)], recv.at[pl.ds(first, n)], None, "yc"
        )

    @staticmethod
    def slots(nx, ny):
        return ny + NZ + nx - 2

    def over_y(self):
        me = self.me
        return [
            pltpu.make_async_remote_copy(
                src_ref=self.own.at[pl.ds(2 * me.at("y", k), 2)],
                dst_ref=self.land.at[me.own["y"]],
                send_sem=self.send.at[k - 1],
                recv_sem=self.recv.at[k - 1],
                device_id=me.device("y", k),
                device_id_type=MESH,
            )
            for k in range(1, me.size["y"])
        ]

    def keep_own(self):
        y = self.me.own["y"]
        return pltpu.make_async_copy(
            self.own.at[pl.ds(2 * y, 2)], self.land.at[y], self.local.at[0]
        )

    def over_c(self):
        me = self.me
        c, full = me.own["c"], pl.ds(0, me.size["y"])
        at = (me.own["z"], me.own["x"], full, c)
        i = me.size["y"] - 1
        return pltpu.make_async_remote_copy(
            src_ref=self.land.at[full, 1 - c],
            dst_ref=self.buf.at[at],
            send_sem=self.send.at[i],
            recv_sem=self.recv.at[i],
            device_id=me.device("c", 1),
            device_id_type=MESH,
        )

    def keep_c(self):
        me = self.me
        c, full = me.own["c"], pl.ds(0, me.size["y"])
        at = (me.own["z"], me.own["x"], full, c)
        return pltpu.make_async_copy(self.land.at[full, c], self.buf.at[at], self.local.at[1])

    def start(self):
        self.keep_own().start()
        for copy in self.over_y():
            copy.start()

    def to_c(self):
        self.keep_own().wait()
        for copy in self.over_y():
            copy.wait_recv()
        self.keep_c().start()
        self.over_c().start()

    def finish_c(self):
        self.keep_c().wait()
        self.over_c().wait_recv()

    def to_rest(self):
        self.finish_c()
        self.rest.start(0)

    def to_last(self):
        self.rest.next(0)

    def finish(self):
        self.rest.finish(1)

    def drain_c(self):
        for copy in self.over_y():
            copy.wait_send()
        self.over_c().wait_send()

    def drain(self):
        self.drain_c()
        self.rest.drain()


def tail_kernel(
    nx,
    ny,
    hat_h,
    gkv_h,
    wkv_h,
    up_h,
    down_h,
    media_h,
    cot_all,
    wq_h,
    gain_r,
    gain_l,
    lat_r,
    gres_r,
    gq_r,
    part_r,
    branch_r,
    unused_mid,
    unused_att,
    kv_o,
    gm_o,
    hid_o,
    gp_o,
    mid_all,
    att_all,
    branch_all,
    gq_all,
    gains_o,
    glat_o,
    hat,
    gkv,
    wkv,
    up,
    down,
    send_c,
    recv_c,
    acc,
    send_y,
    recv_y,
    send_x,
    recv_x,
    send_n,
    recv_n,
    send_f,
    recv_f,
    red,
    gq_y,
    ql_out,
    ql_in,
    media_t,
    gm_t,
    mid_t,
    cot_t,
    hid_t,
    gp_t,
    wqb,
    gbuf,
    grecv,
    load_sem,
    tile_sem,
    out_sem,
    c_send,
    c_recv,
    y_send,
    y_recv,
    x_send,
    x_recv,
    z_send,
    z_recv,
    xa_send,
    xa_recv,
    keep_sem,
    g_send,
    g_recv,
    mid_send,
    mid_recv,
    br_send,
    br_recv,
    aq_send,
    aq_recv,
    ql_send,
    ql_recv,
    at_send,
    at_recv,
    own_sem,
):
    me = Where(nx, ny)
    z, x, y, c = (me.own[a] for a in "zxyc")
    T = CHUNKS
    TG = send_c.shape[0]
    per_g = T // TG
    pieces = 2 * ny
    big = send_c.shape[1]
    chunk = acc.shape[1]
    quarter = send_x.shape[2]
    sub = red.shape[1]
    feat = hat.shape[1]

    def load(i, src, dst):
        return pltpu.make_async_copy(src, dst, load_sem.at[i])

    hat_copy = load(0, hat_h, hat)
    wkv_copy = load(2, wkv_h, wkv)
    up_copy = load(3, up_h, up)
    down_copy = load(4, down_h, down)

    def gkv_load(k, parity):
        a = 2 * me.at("y", k) + parity
        return pltpu.make_async_copy(gkv_h.at[a], gkv.at[a], load_sem.at[6 + 2 * k + parity])

    hat_copy.start()
    for k in list(range(1, ny)) + [0]:
        gkv_load(k, 1 - c).start()
        gkv_load(k, c).start()
    greet(me)

    mid = Gather(me, None, mid_all, "xc", mid_send, mid_recv, None, "yz")
    att = Gather(me, None, att_all, "xz", at_send, at_recv, None, "yc")
    branch = Gather(me, branch_r, branch_all, "zxyc", br_send, br_recv, own_sem.at[1])

    gq = ColumnGather(me, gq_r, gq_y, gq_all, "zx", aq_send, aq_recv, own_sem.at[pl.ds(2, 2)])

    def ql_copy(k):
        return pltpu.make_async_remote_copy(
            src_ref=ql_out.at[me.at("y", k)],
            dst_ref=ql_in.at[k - 1],
            send_sem=ql_send.at[k - 1],
            recv_sem=ql_recv.at[k - 1],
            device_id=me.device("y", k),
            device_id_type=MESH,
        )

    att.start(0)
    mid.start(0)
    branch.start(0)
    gq.start()
    wq_load = load(5, wq_h, wqb)

    def grad_rows(k, t, parity):
        piece = 2 * me.at("y", k) + parity
        left = hat[:, pl.ds(pl.multiple_of(t * big, 128), big)]
        return dg(left, gkv[piece], 0, 0)

    def core_copy(t):
        return pltpu.make_async_remote_copy(
            src_ref=send_c.at[t],
            dst_ref=recv_c.at[t],
            send_sem=c_send.at[t],
            recv_sem=c_recv.at[t],
            device_id=me.device("c", 1),
            device_id_type=MESH,
        )

    def y_copy(k, t):
        return pltpu.make_async_remote_copy(
            src_ref=send_y.at[k - 1, t],
            dst_ref=recv_y.at[k - 1, t],
            send_sem=y_send.at[k - 1, t],
            recv_sem=y_recv.at[k - 1, t],
            device_id=me.device("y", k),
            device_id_type=MESH,
        )

    def x_copy(k, t):
        return pltpu.make_async_remote_copy(
            src_ref=send_x.at[k - 1, t],
            dst_ref=recv_x.at[k - 1, t],
            send_sem=x_send.at[k - 1, t],
            recv_sem=x_recv.at[k - 1, t],
            device_id=me.device("x", k),
            device_id_type=MESH,
        )

    odd, half = lax.rem(z, 2), z // 2
    near = me.device("z", 1 - 2 * odd + NZ)
    far = me.device("z", 2)
    mine_at = x * NZ + odd * 2 + half

    def z_hop(i, src, dst, where, t):
        return pltpu.make_async_remote_copy(
            src_ref=src,
            dst_ref=dst,
            send_sem=z_send.at[i, t],
            recv_sem=z_recv.at[i, t],
            device_id=where,
            device_id_type=MESH,
        )

    def near_copy(t):
        return z_hop(0, send_n.at[t], recv_n.at[t], near, t)

    def far_copy(t):
        return z_hop(1, send_f.at[t], recv_f.at[t], far, t)

    def far_back(t):
        return z_hop(2, red.at[t], kv_o.at[t, mine_at], far, t)

    def near_back(t):
        rows = kv_o.at[t, pl.ds(x * NZ + odd * 2, 2)]
        return z_hop(3, rows, rows, near, t)

    def xa_copy(k, t):
        rows = kv_o.at[t, pl.ds(x * NZ, NZ)]
        return pltpu.make_async_remote_copy(
            src_ref=rows,
            dst_ref=rows,
            send_sem=xa_send.at[k - 1, t],
            recv_sem=xa_recv.at[k - 1, t],
            device_id=me.device("x", k),
            device_id_type=MESH,
        )

    def keep_copy(t):
        return pltpu.make_async_copy(red.at[t], kv_o.at[t, mine_at], keep_sem.at[t])

    def latent_queries():
        wq_load.wait()
        for src in range(ny):
            total = dg(gq_y[src, 0], wqb[0], 1, 1) + dg(gq_y[src, 1], wqb[1], 1, 1)
            ql_out[src] = total.astype(BF16)
        for k in range(1, ny):
            ql_copy(k).start()

    def step_y(t):
        for k in range(1, ny):
            y_copy(k, t).wait_recv()
        whole = acc[t]
        for k in range(1, ny):
            whole = whole + recv_y[k - 1, t].astype(F32)
        acc[t] = whole
        for k in range(1, nx):
            there = pl.ds(pl.multiple_of(me.at("x", k) * quarter, 8), quarter)
            send_x[k - 1, t] = acc[t, there].astype(BF16)
            x_copy(k, t).start()

    def step_x(t):
        for k in range(1, nx):
            x_copy(k, t).wait_recv()
        here = pl.ds(pl.multiple_of(x * quarter, 8), quarter)
        whole = acc[t, here]
        for k in range(1, nx):
            whole = whole + recv_x[k - 1, t].astype(F32)
        acc[t, here] = whole
        away = pl.ds(pl.multiple_of(x * quarter + (1 - odd) * 2 * sub, 8), 2 * sub)
        send_n[t] = acc[t, away].astype(BF16)
        near_copy(t).start()

    def step_near(t):
        near_copy(t).wait_recv()
        here = pl.ds(pl.multiple_of(x * quarter + odd * 2 * sub, 8), 2 * sub)
        acc[t, here] = acc[t, here] + recv_n[t].astype(F32)
        away = x * quarter + odd * 2 * sub + (1 - half) * sub
        send_f[t] = acc[t, pl.ds(pl.multiple_of(away, 8), sub)].astype(BF16)
        far_copy(t).start()

    def step_far(t):
        far_copy(t).wait_recv()
        here = x * quarter + odd * 2 * sub + half * sub
        whole = acc[t, pl.ds(pl.multiple_of(here, 8), sub)] + recv_f[t].astype(F32)
        red[t] = whole.astype(BF16)
        keep_copy(t).start()
        far_back(t).start()

    def step_far_back(t):
        keep_copy(t).wait()
        far_back(t).wait_recv()
        near_back(t).start()

    def step_near_back(t):
        near_back(t).wait_recv()
        for k in range(1, nx):
            xa_copy(k, t).start()

    def step_xa(t):
        for k in range(1, nx):
            xa_copy(k, t).wait_recv()

    hat_copy.wait()
    lag = 2
    steps = ny * TG

    @pl.loop(0, steps + lag)
    def _(j):
        @pl.when(j < steps)
        def _():
            k, t = lax.rem(1 + j, ny), j // ny
            slot = lax.rem(j, TG)

            @pl.when(j < ny)
            def _():
                gkv_load(k, 1 - c).wait()
                gkv_load(k, c).wait()

            @pl.when(j == 3)
            def _():
                for copy in (wkv_copy, up_copy, down_copy, wq_load):
                    copy.start()

            @pl.when(j >= TG)
            def _():
                core_copy(slot).wait_send()

            send_c[slot] = grad_rows(k, t, 1 - c).astype(BF16)
            core_copy(slot).start()

        @pl.when(j >= lag)
        def _():
            i = j - lag
            k, t = lax.rem(1 + i, ny), i // ny
            slot = lax.rem(i, TG)
            mine = grad_rows(k, t, c)
            core_copy(slot).wait_recv()
            mine = mine + recv_c[slot].astype(F32)

            @pl.when(k == 0)
            def _():
                for h in range(per_g):
                    acc[per_g * t + h] = mine[h * chunk : (h + 1) * chunk]

            @pl.when(k > 0)
            def _():
                for step in range(1, ny):

                    @pl.when(k == step)
                    def _():
                        for h in range(per_g):
                            low = mine[h * chunk : (h + 1) * chunk].astype(BF16)
                            send_y[step - 1, per_g * t + h] = low
                            y_copy(step, per_g * t + h).start()

        @pl.when(j == 3)
        def _():
            att.next(0)
            gq.to_c()

        @pl.when(j == 5)
        def _():
            latent_queries()

        for at, action, t in ((6, step_y, 0), (9, step_y, 1), (10, step_x, 0)):

            @pl.when(j == at)
            def _():
                action(t)

        @pl.when(j == 11)
        def _():
            branch.next(0)

        @pl.when(j == 9)
        def _():
            mid.next(0)
            gq.finish_c()

    for t in range(TG):
        core_copy(t).wait_send()
    wkv_copy.wait()
    up_copy.wait()
    down_copy.wait()

    gbuf[...] = part_r[...]
    media_rows = media_h.shape[0]
    tile = media_t.shape[1]
    n_media = media_rows // tile

    def media_load(u):
        return pltpu.make_async_copy(
            media_h.at[pl.ds(pl.multiple_of(u * tile, tile), tile)],
            media_t.at[lax.rem(u, 2)],
            tile_sem.at[lax.rem(u, 2)],
        )

    def gm_store(u):
        return pltpu.make_async_copy(
            gm_t, gm_o.at[pl.ds(pl.multiple_of(u * tile, tile), tile)], out_sem.at[0]
        )

    def media_tile(u):
        @pl.when(u + 1 < n_media)
        def _():
            media_load(u + 1).start()

        rows = pl.ds(pl.multiple_of(u * tile, tile), tile)
        total = dg(gkv[0, rows], wkv[0], 1, 1)
        for a in range(1, pieces):
            total = total + dg(gkv[a, rows], wkv[a], 1, 1)
        media_load(u).wait()
        values = media_t[lax.rem(u, 2)].astype(F32)
        normed, inverse = normalize(values)
        gbuf[0:1] = gbuf[0:1] + jnp.sum(total * normed, axis=0, keepdims=True)
        result = norm_grad(total * gain_r[...].reshape(1, -1), normed, inverse)

        @pl.when(u >= 1)
        def _():
            gm_store(u - 1).wait()

        gm_t[...] = result.astype(BF16)
        gm_store(u).start()

    xt = mid_t.shape[1]
    n_ffn = NZ * (nx // xt)

    def rows_load(u):
        zz, xx = u // (nx // xt), lax.rem(u, nx // xt) * xt
        b = lax.rem(u, 2)
        return [
            pltpu.make_async_copy(
                mid_all.at[zz, pl.ds(xx, xt)], mid_t.at[b], tile_sem.at[2 + b]
            ),
            pltpu.make_async_copy(
                cot_all.at[zz, pl.ds(xx, xt)], cot_t.at[b], tile_sem.at[4 + b]
            ),
        ]

    def ffn_store(u):
        return [
            pltpu.make_async_copy(hid_t, hid_o.at[u], out_sem.at[1]),
            pltpu.make_async_copy(gp_t, gp_o.at[u], out_sem.at[2]),
        ]

    def ffn_tile(u):
        @pl.when(u + 1 < n_ffn)
        def _():
            for copy in rows_load(u + 1):
                copy.start()

        for copy in rows_load(u):
            copy.wait()

        @pl.when(u >= 1)
        def _():
            for copy in ffn_store(u - 1):
                copy.wait()

        b = lax.rem(u, 2)
        mid_rows = mid_t[b].reshape(-1, feat)
        cot_rows = cot_t[b].reshape(-1, feat)
        width = up.shape[1] // 3
        for part in range(3):
            cols = pl.ds(part * width, width)
            pre = dg(mid_rows, up[:, cols], 1, 0)
            grad = dg(cot_rows, down[cols, :], 1, 1)
            cdf = 0.5 * (1.0 + lax.erf(pre * (0.5**0.5)))
            slope = cdf + pre * (jnp.exp(-0.5 * pre * pre) * 0.3989422804014327)
            hid_t[:, cols] = (pre * cdf).astype(BF16)
            gp_t[:, cols] = (grad * slope).astype(BF16)
        for copy in ffn_store(u):
            copy.start()

    def latent_rows():
        rows = pl.ds(media_rows, lat_r.shape[0])
        total = dg(gkv[0, rows], wkv[0], 1, 1)
        for a in range(1, pieces):
            total = total + dg(gkv[a, rows], wkv[a], 1, 1)
        total = total + ql_out[y].astype(F32)
        for k in range(1, ny):
            ql_copy(k).wait_recv()
            total = total + ql_in[k - 1].astype(F32)
        normed, inverse = normalize(lat_r[...])
        gbuf[1:2] = jnp.sum(total * normed, axis=0, keepdims=True)
        glat_o[...] = gres_r[...] + norm_grad(total * gain_l[...].reshape(1, -1), normed, inverse)

    def comm(s):
        for lead, action in (
            (2, step_y),
            (1, step_x),
            (0, step_near),
            (-1, step_far),
            (-2, step_far_back),
            (-3, step_near_back),
        ):

            @pl.when(jnp.logical_and(s + lead >= max(lead, 0), s + lead < T))
            def _():
                action(s + lead)

    def gain_copies(axis, base):
        return [
            pltpu.make_async_remote_copy(
                src_ref=gbuf,
                dst_ref=grecv.at[base + k - 1],
                send_sem=g_send.at[base + k - 1],
                recv_sem=g_recv.at[base + k - 1],
                device_id=me.device(axis, k),
                device_id_type=MESH,
            )
            for k in range(1, me.size[axis])
        ]

    def gain_base(axis):
        return sum(me.size[a] - 1 for a in "cyxz"[: "cyxz".index(axis)])

    def gain_start(axis):
        for copy in gain_copies(axis, gain_base(axis)):
            copy.start()

    def gain_finish(axis):
        base = gain_base(axis)
        for copy in gain_copies(axis, base):
            copy.wait_send()
            copy.wait_recv()
        total = gbuf[...]
        for k in range(1, me.size[axis]):
            total = total + grecv[base + k - 1]
        gbuf[...] = total

    media_load(0).start()
    per = n_ffn // 4

    @pl.loop(0, T + 4)
    def _(s):
        comm(s)

        for i, copy in enumerate(gq.rest.copies(0)):

            @pl.when(s == i)
            def _():
                copy.start()

        @pl.when(s < n_media)
        def _():
            media_tile(s)

        @pl.when(s == n_media)
        def _():
            gm_store(n_media - 1).wait()
            latent_rows()
            gain_start("c")
            mid.finish(1)
            for copy in rows_load(0):
                copy.start()

        @pl.when(s == n_media + 1)
        def _():
            gain_finish("c")
            gain_start("x")

        @pl.when(jnp.logical_and(s > n_media, s < n_media + 5))
        def _():
            @pl.loop(0, per)
            def _(u):
                ffn_tile((s - n_media - 1) * per + u)

        @pl.when(s == 9)
        def _():
            gq.to_last()

        @pl.when(s == n_media + 4)
        def _():
            gain_finish("x")
            gain_start("z")

        @pl.when(s == n_media + 5)
        def _():
            for copy in ffn_store(n_ffn - 1):
                copy.wait()
            branch.next(1)

        @pl.when(s == n_media + 7)
        def _():
            gain_finish("z")
            gain_start("y")

        @pl.when(s == n_media + 10)
        def _():
            branch.next(2)

    @pl.loop(0, T)
    def _(t):
        step_xa(t)

    gain_finish("y")
    gains_o[...] = gbuf[...]
    branch.finish(3)
    gq.finish()
    att.finish(1)
    att.drain()
    mid.drain()
    branch.drain()
    gq.drain()
    for k in range(1, ny):
        ql_copy(k).wait_send()

    @pl.loop(0, T)
    def _(t):
        for k in range(1, ny):
            y_copy(k, t).wait_send()
        for k in range(1, nx):
            x_copy(k, t).wait_send()
            xa_copy(k, t).wait_send()
        for copy in (near_copy(t), far_copy(t), far_back(t), near_back(t)):
            copy.wait_send()


def tail(
    nx, ny, hat, gkv, wkv, up, down, media, cot_all, wq, gain_m, gain_l, lats, gres, gq, parts, branch, mid_all, att_all
):
    T = CHUNKS
    TG = 6
    rows, feat = hat.shape
    pieces, _, two = gkv.shape
    lat = branch.shape[0]
    ff = up.shape[1]
    blocks = nx * NZ
    chunk = feat // T
    sub = chunk // blocks
    xt = 256 // (lat * pieces)
    tile_rows = xt * pieces * lat
    tiles = NZ * nx // xt
    any_ = pl.BlockSpec(memory_space=pl.ANY)
    vm = pl.BlockSpec(memory_space=pltpu.VMEM)
    S = jax.ShapeDtypeStruct
    every = (NZ, nx, ny, 2, lat)
    V = pltpu.VMEM
    D = pltpu.SemaphoreType.DMA
    spread4 = NZ + nx + ny + 2 - 4
    media_rows = media.shape[0]
    outs = (
        S((T, blocks, sub, two), BF16),
        S((media_rows, feat), BF16),
        S((tiles, tile_rows, ff), BF16),
        S((tiles, tile_rows, ff), BF16),
        S(every + (feat,), BF16),
        S(every + (two // 2,), BF16),
        S(every + (feat,), BF16),
        S(every + (two // 2,), BF16),
        S((8, feat), F32),
        S(gres.shape, F32),
    )
    return pl.pallas_call(
        functools.partial(tail_kernel, nx, ny),
        out_shape=outs,
        in_specs=[any_] * 8 + [vm] * 7 + [any_] * 2,
        out_specs=(any_,) * 8 + (vm,) * 2,
        input_output_aliases={15: 4, 16: 5},
        scratch_shapes=[
            V(hat.shape, BF16),
            V(gkv.shape, BF16),
            V(wkv.shape, BF16),
            V(up.shape, BF16),
            V(down.shape, BF16),
            V((TG, feat // TG, two), BF16),
            V((TG, feat // TG, two), BF16),
            V((T, chunk, two), F32),
            V((ny - 1, T, chunk, two), BF16),
            V((ny - 1, T, chunk, two), BF16),
            V((nx - 1, T, NZ * sub, two), BF16),
            V((nx - 1, T, NZ * sub, two), BF16),
            V((T, 2 * sub, two), BF16),
            V((T, 2 * sub, two), BF16),
            V((T, sub, two), BF16),
            V((T, sub, two), BF16),
            V((T, sub, two), BF16),
            V((ny, 2, lat, two // 2), BF16),
            V((ny, lat, feat), BF16),
            V((ny - 1, lat, feat), BF16),
            V((2, 256, feat), BF16),
            V((256, feat), BF16),
            V((2, xt, ny, 2, lat, feat), BF16),
            V((2, xt, ny, 2, lat, feat), BF16),
            V((tile_rows, ff), BF16),
            V((tile_rows, ff), BF16),
            V(wq.shape, BF16),
            V((8, feat), F32),
            V((spread4, 8, feat), F32),
            D((6 + pieces,)),
            D((6,)),
            D((3,)),
            D((TG,)),
            D((TG,)),
            D((ny - 1, T)),
            D((ny - 1, T)),
            D((nx - 1, T)),
            D((nx - 1, T)),
            D((4, T)),
            D((4, T)),
            D((nx - 1, T)),
            D((nx - 1, T)),
            D((T,)),
            D((spread4,)),
            D((spread4,)),
            D((spread4,)),
            D((spread4,)),
            D((spread4,)),
            D((spread4,)),
            D((ColumnGather.slots(nx, ny),)),
            D((ColumnGather.slots(nx, ny),)),
            D((ny - 1,)),
            D((ny - 1,)),
            D((spread4,)),
            D((spread4,)),
            D((4,)),
        ],
        compiler_params=pltpu.CompilerParams(
            collective_id=3, has_side_effects=True, vmem_limit_bytes=67043328
        ),
        name="tail",
    )(
        hat, gkv, wkv, up, down, media, cot_all, wq, gain_m, gain_l, lats, gres, gq, parts, branch, mid_all, att_all
    )


def post_kernel(
    hid_h,
    gp_h,
    mid_h,
    cot_h,
    branch_h,
    lat_h,
    att_h,
    gq_h,
    kv_h,
    gm_h,
    res_r,
    lat_r,
    gains_r,
    down_o,
    up_o,
    out_o,
    qkv_o,
    media_o,
    res_o,
    lat_o,
    one_o,
    two_o,
    three_o,
    left,
    right,
    small,
    tiles,
    media_in,
    media_out,
    in_sem,
    tile_sem,
    min_sem,
    mout_sem,
):
    rows = left.shape[1]
    n_k = hid_h.shape[0] // rows
    cols = att_h.shape[1]
    width = tiles.shape[1]
    n_media = gm_h.shape[0] // media_in.shape[1]
    counts = {"tile": 0, "media": 0}
    depth = media_out.shape[0]

    def media_load(i):
        size = media_in.shape[1]
        return pltpu.make_async_copy(
            gm_h.at[pl.ds(i * size, size)], media_in.at[i], min_sem.at[i]
        )

    def media_store(i):
        size = media_in.shape[1]
        return pltpu.make_async_copy(
            media_out.at[i % depth], media_o.at[pl.ds(i * size, size)], mout_sem.at[i % depth]
        )

    def media_step():
        i = counts["media"]
        if i >= n_media:
            return
        counts["media"] = i + 1
        media_load(i).wait()
        if i >= depth:
            media_store(i - depth).wait()
        media_out[i % depth] = media_in[i].astype(F32)
        media_store(i).start()

    pending = [None] * tiles.shape[0]

    def emit(value, target):
        i = counts["tile"] % len(pending)
        counts["tile"] += 1
        if pending[i] is not None:
            pending[i].wait()
        a, b = value.shape
        tiles[i, 0:a, 0:b] = value
        pending[i] = pltpu.make_async_copy(
            tiles.at[i, pl.ds(0, a), pl.ds(0, b)], target, tile_sem.at[i]
        )
        pending[i].start()

    def load(slot, a, b, k):
        part = pl.ds(k * rows, rows)
        return [
            pltpu.make_async_copy(a.at[part], left.at[slot, :, pl.ds(0, a.shape[1])], in_sem.at[2 * slot]),
            pltpu.make_async_copy(b.at[part], right.at[slot, :, pl.ds(0, b.shape[1])], in_sem.at[2 * slot + 1]),
        ]

    jobs = [
        (att_h, branch_h, out_o),
        (hid_h, cot_h, down_o),
        (mid_h, gp_h, up_o),
        (lat_h, gq_h, qkv_o.at[0]),
    ]
    loads = [load(i, a, b, 0) for i, (a, b, unused) in enumerate(jobs)]
    kv_loads = [
        pltpu.make_async_copy(kv_h.at[:, pl.ds(i * cols, cols)], small.at[i], in_sem.at[8 + i])
        for i in range(2)
    ]
    for copy in loads[0] + loads[1]:
        copy.start()
    for i in range(n_media):
        media_load(i).start()
    for copy in loads[2] + loads[3] + kv_loads:
        copy.start()
    res_o[...] = res_r[...]
    lat_o[...] = lat_r[...]
    for i, ref in enumerate((one_o, two_o, three_o)):
        ref[...] = gains_r[i]
    for i, (a, b, target) in enumerate(jobs):
        for copy in loads[i]:
            copy.wait()
        slot = i
        m, n = a.shape[1], b.shape[1]
        for at in range(0, m, width):
            step = min(width, m - at)
            value = dg(left[slot, :, at : at + step], right[slot, :, 0:n], 0, 0)
            emit(value, target.at[pl.ds(at, step), pl.ds(0, n)])
            media_step()
    while counts["media"] < n_media:
        media_step()
    for i in range(2):
        kv_loads[i].wait()
        for at in range(0, kv_h.shape[0], width):
            value = small[i, at : at + width].astype(F32)
            emit(value, qkv_o.at[1 + i, pl.ds(at, width)])
    for copy in pending:
        copy.wait()
    for i in range(max(n_media - depth, 0), n_media):
        media_store(i).wait()


def post(hid, gp, mid, cot, branch, lat, att, gq, kv, gm, res, glat, gains):
    S = jax.ShapeDtypeStruct
    V = pltpu.VMEM
    D = pltpu.SemaphoreType.DMA
    any_ = pl.BlockSpec(memory_space=pl.ANY)
    rows, ff = hid.shape
    feat = mid.shape[1]
    cols = att.shape[1]
    wide = max(feat, ff)
    args = (hid, gp, mid, cot, branch, lat, att, gq, kv, gm)
    vm = pl.BlockSpec(memory_space=pltpu.VMEM)
    return pl.pallas_call(
        post_kernel,
        out_shape=(
            S((ff, feat), F32),
            S((feat, ff), F32),
            S((cols, feat), F32),
            S((3, feat, cols), F32),
            S(gm.shape, F32),
            S(res.shape, F32),
            S(glat.shape, F32),
            S((feat,), F32),
            S((feat,), F32),
            S((feat,), F32),
        ),
        in_specs=[any_] * len(args) + [vm] * 3,
        out_specs=(any_,) * 5 + (vm,) * 5,
        scratch_shapes=[
            V((4, rows, wide), BF16),
            V((4, rows, wide), BF16),
            V((2, feat, cols), BF16),
            V((4, 256, wide), F32),
            V((gm.shape[0] // 64, 64, feat), BF16),
            V((4, 64, feat), F32),
            D((10,)),
            D((4,)),
            D((gm.shape[0] // 64,)),
            D((4,)),
        ],
        compiler_params=pltpu.CompilerParams(vmem_limit_bytes=67043328),
        name="weights",
    )(*args, res, glat, gains)


def full_sum(x):
    return jnp.sum(jnp.sum(x, axis=1, keepdims=True), axis=0, keepdims=True)


class Relay:
    def __init__(self, me, own, buf, order, send, recv):
        self.me, self.own, self.buf, self.order = me, own, buf, order
        self.send, self.recv = send, recv
        ny, nx = me.size["y"] - 1, me.size["x"] - 1
        sizes = {"o": 1, "y": ny, "x": ny * nx, "z": ny, "c": ny}
        self.base, total = {}, 0
        for a in "oyxzc":
            self.base[a] = total
            total += sizes[a]

    @staticmethod
    def slots(nx, ny):
        return 1 + 3 * (ny - 1) + (ny - 1) * (nx - 1)

    def part(self, done):
        me = self.me
        index = []
        if "x" in self.order:
            index.append(pl.ds(0, me.size["x"]) if "x" in done else me.own["x"])
        if "z" in self.order:
            index.append(pl.ds(0, 2) if "z" in done else lax.rem(me.own["z"], 2))
        return tuple(index)

    def copies(self, phase):
        me, buf = self.me, self.buf
        y, c = me.own["y"], me.own["c"]
        out = []

        def add(src, dst, where):
            i = self.base[phase] + len(out)
            out.append(
                pltpu.make_async_remote_copy(
                    src_ref=src,
                    dst_ref=dst,
                    send_sem=self.send.at[i],
                    recv_sem=self.recv.at[i],
                    device_id=where,
                    device_id_type=MESH,
                )
            )

        if phase == "o":
            add(self.own, buf.at[y, c], me.device("c", 1))
            return out
        done = self.order[1 : self.order.index(phase)] if phase in "xz" else ""
        for k in range(1, me.size["y"]):
            if phase == "y":
                at = self.part("")
                src = self.own.at[at] if at else self.own
                add(src, buf.at[(y, c) + at], me.device("y", k))
                continue
            yk = me.at("y", me.size["y"] - k)
            if phase == "c":
                add(buf.at[yk, c], buf.at[yk, c], me.device("c", 1))
                continue
            ref = buf.at[(yk, c) + self.part(done)]
            if phase == "z":
                add(ref, ref, me.device("z", 1 - 2 * lax.rem(me.own["z"], 2) + NZ))
            else:
                for j in range(1, me.size["x"]):
                    add(ref, ref, me.device("x", j))
        return out

    def start(self, phase):
        for copy in self.copies(phase):
            copy.start()

    def wait(self, phase):
        for copy in self.copies(phase):
            copy.wait_recv()

    def next(self, phase):
        self.wait(phase)
        at = self.order.index(phase) + 1
        self.start(self.order[at] if at < len(self.order) else "c")

    def drain(self):
        for phase in "o" + self.order + "c":
            for copy in self.copies(phase):
                copy.wait_send()


def front_kernel(
    nx,
    ny,
    aligned,
    count_s,
    lat_r,
    cot_r,
    gain_m,
    gain_l,
    gain_f,
    media_h,
    kvw_h,
    wq_h,
    out_h,
    up_h,
    down_h,
    hat_o,
    gkv_o,
    wkv_all,
    wq_o,
    o_all,
    cot_all,
    lat_all,
    att_all,
    mid_all,
    branch_o,
    gq_o,
    gres_o,
    output_o,
    part_o,
    hat,
    kv,
    wkv_own,
    wbuf,
    wq_v,
    o_v,
    up,
    down,
    media_t,
    lat_y,
    q_y,
    q64,
    pexp,
    probs,
    stat,
    stat_in,
    o64,
    o_in,
    att64,
    att_low,
    att_y,
    g64,
    mid_ha,
    cot_ha,
    hid,
    gpre,
    ghid,
    sums,
    sums_in,
    load_sem,
    tile_sem,
    wload_sem,
    store_sem,
    w_send,
    w_recv,
    u_send,
    u_recv,
    qy_send,
    qy_recv,
    pair_send,
    pair_recv,
    st_send,
    st_recv,
    ha_send,
    ha_recv,
    ct_send,
    ct_recv,
    lt_send,
    lt_recv,
    at_send,
    at_recv,
    md_send,
    md_recv,
    own_sem,
):
    me = Where(nx, ny)
    y, c = me.own["y"], me.own["c"]
    group = 2 * ny
    place = lax.axis_index("ha")
    lat = lat_r.shape[0]
    media_rows = media_h.shape[0]
    rows = hat.shape[0]
    feat = hat.shape[1]
    cols = q64.shape[-1]
    heads = cols // HEAD
    scale = HEAD ** (-0.5)
    partner = me.device("c", 1)
    n_w = wkv_own.shape[0]
    n_o = o_v.shape[1]

    def load(i, src, dst):
        return pltpu.make_async_copy(src, dst, load_sem.at[i])

    wkv_loads = (
        [
            load(0, kvw_h.at[1], wkv_own.at[..., pl.ds(0, cols)]),
            load(1, kvw_h.at[2], wkv_own.at[..., pl.ds(cols, cols)]),
        ]
        if aligned
        else [load(0, kvw_h, wkv_own)]
    )
    up_load, down_load = load(2, up_h, up), load(3, down_h, down)
    wq_load = load(4, wq_h.at[0], wq_v.at[c])
    o_load = load(5, out_h, o_v.at[place])
    for copy in wkv_loads:
        copy.start()
    tile = media_t.shape[1]
    tiles = media_rows // tile

    def media_load(u):
        return pltpu.make_async_copy(
            media_h.at[pl.ds(pl.multiple_of(u * tile, tile), tile)],
            media_t.at[lax.rem(u, 2)],
            tile_sem.at[lax.rem(u, 2)],
        )

    media_load(0).start()
    wq_load.start()
    down_load.start()
    up_load.start()
    o_load.start()

    barrier = pltpu.get_barrier_semaphore()
    greeted = [me.device(a, k) for a in "cyxz" for k in range(1, me.size[a])]
    for k in range(1, ny):
        greeted.append({"sa": lax.axis_index("sa"), "ha": me.at("y", k) * 2 + 1 - c})
    for where in greeted:
        pl.semaphore_signal(barrier, inc=1, device_id=where, device_id_type=MESH)
    pl.semaphore_wait(barrier, len(greeted))

    both = (pl.ds(0, ny), pl.ds(0, 2))
    relays = [
        Relay(
            me,
            wkv_own.at[i],
            wkv_all.at[both + (i,)],
            ("yxz", "yzx")[i % 2],
            w_send.at[i],
            w_recv.at[i],
        )
        for i in range(n_w)
    ]
    o_relays = [
        Relay(
            me,
            out_h.at[i],
            o_all.at[both + (i,)],
            "yx" if i == 0 else "yz",
            u_send.at[i],
            u_recv.at[i],
        )
        for i in range(n_o)
    ]
    gather_cot = Gather(me, cot_r, cot_all, "zyxc", ct_send, ct_recv, own_sem.at[0])
    own_lat = hat.at[pl.ds(media_rows, lat)]
    gather_lat = Gather(me, own_lat, lat_all, "yzxc", lt_send, lt_recv, own_sem.at[1])
    gather_att = ColumnGather(
        me, att_low, att_y, att_all, "xz", at_send, at_recv, own_sem.at[pl.ds(2, 2)]
    )

    def remote(src, dst, send, recv, where):
        return pltpu.make_async_remote_copy(
            src_ref=src,
            dst_ref=dst,
            send_sem=send,
            recv_sem=recv,
            device_id=where,
            device_id_type=MESH,
        )

    def pair_copy(i, src, dst):
        return remote(src, dst, pair_send.at[i], pair_recv.at[i], partner)

    def ha_copies(base, source, target):
        out = []
        for k in range(1, group):
            there = lax.rem(place + k, group)
            out.append(
                remote(
                    source(there),
                    target(k),
                    ha_send.at[base, k - 1],
                    ha_recv.at[base, k - 1],
                    {"sa": lax.axis_index("sa"), "ha": there},
                )
            )
        return out

    cot_copies = ha_copies(0, lambda there: cot_r, lambda k: cot_ha.at[place])
    mid_copies = ha_copies(1, lambda there: mid_ha.at[y, c], lambda k: mid_ha.at[y, c])
    gmid_copies = ha_copies(2, lambda there: sums.at[0, there], lambda k: sums_in.at[0, k - 1])
    ffn_copies = ha_copies(3, lambda there: sums.at[1, there], lambda k: sums_in.at[1, k - 1])
    lat_copies = [
        remote(own_lat, lat_y.at[y], qy_send.at[0, k - 1], qy_recv.at[0, k - 1], me.device("y", k))
        for k in range(1, ny)
    ]
    back_copies = [
        remote(
            q_y.at[me.at("y", k)],
            q64.at[pl.ds(2 * y, 2), c],
            qy_send.at[1, k - 1],
            qy_recv.at[1, k - 1],
            me.device("y", k),
        )
        for k in range(1, ny)
    ]
    wq_copy = pair_copy(5, wq_h.at[0], wq_v.at[c])

    gather_cot.start(0)
    normed, unused = normalize(lat_r[...])
    low = (normed * gain_l[...].reshape(1, -1)).astype(BF16)
    hat[pl.ds(media_rows, lat)] = low
    lat_y[y] = low
    for copy in lat_copies:
        copy.start()
    for copy in wkv_loads:
        copy.wait()
    for relay in relays:
        relay.start("o")
        relay.start("y")
    wq_copy.start()
    for relay in o_relays:
        relay.start("o")
    cot_ha[place] = cot_r[...]
    own_store = pltpu.make_async_copy(wkv_own, wkv_all.at[y, c], store_sem.at[0])
    own_store.start()

    @pl.loop(0, tiles)
    def _(u):
        @pl.when(u + 1 < tiles)
        def _():
            media_load(u + 1).start()

        media_load(u).wait()
        normed, unused = normalize(media_t[lax.rem(u, 2)].astype(F32))
        hat[pl.ds(pl.multiple_of(u * tile, tile), tile)] = (normed * gain_m[...].reshape(1, -1)).astype(BF16)

    hat_store = pltpu.make_async_copy(hat, hat_o, store_sem.at[1])
    hat_store.start()
    step = rows // 4

    def project(weights, piece):
        @pl.loop(0, 4)
        def _(u):
            part = pl.ds(pl.multiple_of(u * step, 8), step)
            w = weights[...].reshape(feat, 2 * cols)
            kv[piece, part] = dg(hat[part], w, 1, 0).astype(BF16)

    def weight_load(slot, ya, ca):
        return pltpu.make_async_copy(wkv_all.at[ya, ca], wbuf.at[slot], wload_sem.at[slot])

    project(wkv_own, place)
    for relay in relays:
        relay.wait("o")
    weight_load(0, y, 1 - c).start()
    relays[0].next("y")
    weight_load(0, y, 1 - c).wait()
    project(wbuf.at[0], 2 * y + 1 - c)
    relays[1].next("y")
    relays[0].next("x")
    wq_load.wait()
    wq_copy.wait_recv()
    for copy in lat_copies:
        copy.wait_recv()
    wq_store = pltpu.make_async_copy(wq_v, wq_o, store_sem.at[2])
    wq_store.start()
    all_lat = lat_y[...].reshape(ny * lat, feat)
    for ca in range(2):
        w = wq_v[ca].reshape(feat, cols)
        q_y[pl.ds(0, ny), ca] = dg(all_lat, w, 1, 0).astype(BF16).reshape(ny, lat, cols)
    q64[2 * y, c] = q_y[y, 0]
    q64[2 * y + 1, c] = q_y[y, 1]
    for copy in back_copies:
        copy.start()
    relays[2].next("y")
    for relay in o_relays:
        relay.start("y")
    for copy in cot_copies:
        copy.start()
    gather_lat.start(0)
    gather_cot.next(0)
    relays[1].next("z")
    relays[3].next("y")
    for copy in back_copies:
        copy.wait_recv()
    q_copy = pair_copy(0, q64.at[pl.ds(0, group), c], q64.at[pl.ds(0, group), c])
    q_copy.start()
    relays[2].next("x")

    lane = lax.broadcasted_iota(jnp.int32, (2 * lat, cols), 1)

    def inside(h):
        return jnp.logical_and(lane >= h * HEAD, lane < (h + 1) * HEAD)

    def spread(x):
        return jnp.concatenate(
            [jnp.where(inside(h), x, jnp.zeros_like(x)) for h in range(heads)], axis=0
        )

    def merge(x):
        total = jnp.where(inside(0), x[: 2 * lat], 0.0)
        for h in range(1, heads):
            total = total + jnp.where(inside(h), x[2 * lat * h : 2 * lat * (h + 1)], 0.0)
        return total

    tall = heads * 2 * lat
    limit = count_s[y] * PATCH - c * media_rows
    key = lax.broadcasted_iota(jnp.int32, (tall, rows), 1)
    half = lax.broadcasted_iota(jnp.int32, (tall, 128), 1) < 64

    def stat_copy(a):
        return remote(stat.at[a], stat_in.at[a], st_send.at[a], st_recv.at[a], partner)

    def attend(ya):
        @pl.loop(0, 2)
        def _(ca):
            a = 2 * ya + ca
            q_blk = spread(q64[a].reshape(2 * lat, cols))
            scores = dg(q_blk, kv[a, :, pl.ds(0, cols)], 1, 1) * scale
            usable = jnp.logical_or(key < limit, key >= media_rows)
            scores = jnp.where(usable, scores, NEG)
            top = jnp.max(scores, axis=-1, keepdims=True)
            value = jnp.exp(scores - top)
            pexp[a] = value
            total = jnp.sum(value, axis=-1, keepdims=True)
            stat[a] = jnp.where(half, top, total)
            stat_copy(a).start()

    def settle(ya):
        @pl.loop(0, 2)
        def _(ca):
            a = 2 * ya + ca
            stat_copy(a).wait_recv()
            top, total = stat[a, :, 0:1], stat[a, :, 64:65]
            top_in, total_in = stat_in[a, :, 0:1], stat_in[a, :, 64:65]
            top_all = jnp.maximum(top, top_in)
            mine = jnp.exp(top - top_all)
            denom = total * mine + total_in * jnp.exp(top_in - top_all)
            low = (pexp[a] * (mine / denom)).astype(BF16)
            probs[a] = low
            o64[a] = merge(dg(low, kv[a, :, pl.ds(cols, cols)], 1, 0)).reshape(2, lat, cols)

    q_copy.wait_recv()
    attend(y)
    relays[0].next("z")
    relays[3].next("z")
    settle(y)
    relays[1].next("x")
    relays[2].next("z")
    relays[3].next("x")
    for k in range(1, ny):
        yk = me.at("y", ny - k)
        weight_load(1, yk, c).start()
        if k == 1:
            for relay in o_relays:
                relay.next("y")
        weight_load(1, yk, c).wait()
        project(wbuf.at[1], 2 * yk + c)
        if k == 1:
            for relay in relays:
                relay.wait("c")
        weight_load(0, yk, 1 - c).start()
        if k == 1:
            for relay in o_relays:
                relay.next(relay.order[1])
            gather_lat.next(0)
            gather_cot.next(1)
        weight_load(0, yk, 1 - c).wait()
        project(wbuf.at[0], 2 * yk + 1 - c)
        attend(yk)
    down_load.wait()
    for copy in cot_copies:
        copy.wait_recv()
    ghid[...] = dg(cot_ha[...].reshape(group * lat, feat), down[...], 1, 1)
    for k in range(1, ny):
        settle(me.at("y", ny - k))

    o_copy = pair_copy(1, o64.at[pl.ds(0, group), 1 - c], o_in)
    o_copy.start()
    o_loads = []
    for relay in o_relays:
        relay.wait("o")
        relay.wait("c")
    others = [(y, 1 - c)]
    for k in range(1, ny):
        others += [(me.at("y", ny - k), c), (me.at("y", ny - k), 1 - c)]
    for i, (ya, ca) in enumerate(others):
        o_loads.append(load(6 + i, o_all.at[ya, ca], o_v.at[2 * ya + ca]))
        o_loads[-1].start()
    o_load.wait()
    for copy in o_loads:
        copy.wait()
    o_copy.wait_recv()
    branch = jnp.zeros((lat, feat), F32)
    for a in range(group):
        mine = o64[a, c] + o_in[a]
        att64[a, c] = mine
        low = mine.astype(BF16)
        att_low[a] = low
        branch = branch + dg(low, o_v[a].reshape(cols, feat), 1, 0)
    att_copy = pair_copy(2, att64.at[pl.ds(0, group), c], att64.at[pl.ds(0, group), c])
    residual = lat_r[...] + branch
    mid_norm, mid_inv = normalize(residual)
    mid_low = (mid_norm * gain_f[...].reshape(1, -1)).astype(BF16)
    mid_ha[y, c] = mid_low
    for copy in mid_copies:
        copy.start()
    att_copy.start()
    gather_att.start()
    part_o[...] = jnp.zeros_like(part_o)
    spot = lax.broadcasted_iota(jnp.int32, (1, feat), 1)
    squares = jnp.where(spot == 0, full_sum(residual * residual), 0.0)
    squares = squares + jnp.where(spot == 1, full_sum(branch * branch), 0.0)
    up_load.wait()
    for copy in mid_copies:
        copy.wait_recv()
    mid_keep = pltpu.make_async_copy(
        mid_ha.at[pl.ds(0, ny), c],
        mid_all.at[me.own["z"], me.own["x"], pl.ds(0, ny), c],
        own_sem.at[4],
    )
    gather_mid = Gather(me, None, mid_all, "z", md_send, md_recv, None, "y")
    mid_keep.start()
    pre = dg(mid_ha[...].reshape(group * lat, feat), up[...], 1, 0)
    cdf = 0.5 * (1.0 + lax.erf(pre * (0.5**0.5)))
    slope = cdf + pre * (jnp.exp(-0.5 * pre * pre) * 0.3989422804014327)
    gpre[...] = (ghid[...] * slope).astype(BF16)
    hid[...] = (pre * cdf).astype(BF16)
    sums[0] = dg(gpre[...], up[...], 1, 1).reshape(group, lat, feat).astype(BF16)
    for copy in gmid_copies:
        copy.start()
    grad_mid = sums[0, place].astype(F32)
    sums[1] = dg(hid[...], down[...], 1, 0).reshape(group, lat, feat).astype(BF16)
    gather_att.to_c()
    mid_keep.wait()
    gather_mid.start(0)
    gather_lat.next(1)
    gather_cot.next(2)
    for k, copy in enumerate(gmid_copies):
        copy.wait_recv()
        grad_mid = grad_mid + sums_in[0, k].astype(F32)
    for copy in ffn_copies:
        copy.start()
    grad_res = cot_r[...].astype(F32) + norm_grad(grad_mid * gain_f[...].reshape(1, -1), mid_norm, mid_inv)
    gres_o[...] = grad_res
    grad_low = grad_res.astype(BF16)
    branch_o[...] = grad_low
    for a in range(group):
        g64[a, c] = dg(grad_low, o_v[a].reshape(cols, feat), 1, 1).astype(BF16)
    g_copy = pair_copy(3, g64.at[pl.ds(0, group), c], g64.at[pl.ds(0, group), c])
    g_copy.start()
    part_o[2:3] = jnp.sum(grad_mid * mid_norm, axis=0, keepdims=True)
    att_copy.wait_recv()
    o_copy.wait_send()
    for a in range(group):
        stat_copy(a).wait_send()
    g_copy.wait_recv()

    def gkv_store(a):
        return pltpu.make_async_copy(kv.at[a], gkv_o.at[a], st_send.at[a])

    @pl.loop(0, group)
    def _(a):
        q_blk = spread(q64[a].reshape(2 * lat, cols))
        g_blk = spread(g64[a].reshape(2 * lat, cols))
        att = att64[a].reshape(2 * lat, cols)
        inner = jnp.sum(
            g_blk.astype(F32) * jnp.concatenate([att] * heads, axis=0), axis=-1, keepdims=True
        )
        keys = kv[a, :, pl.ds(0, cols)]
        low = probs[a]
        grad = dg(g_blk, kv[a, :, pl.ds(cols, cols)], 1, 1)
        grad = (low.astype(F32) * (grad - inner)).astype(BF16)
        o64[a] = (merge(dg(grad, keys, 1, 0)) * scale).reshape(2, lat, cols)
        kv[a, :, pl.ds(0, cols)] = (dg(grad, q_blk, 0, 0) * scale).astype(BF16)
        kv[a, :, pl.ds(cols, cols)] = dg(low, g_blk, 0, 0).astype(BF16)
        gkv_store(a).start()

    gq_copy = pair_copy(4, o64.at[pl.ds(0, group), 1 - c], o_in)
    gq_copy.start()
    for copy in ffn_copies:
        copy.wait_recv()
    ffn = sums[1, place].astype(F32)
    for k in range(1, group):
        ffn = ffn + sums_in[1, k - 1].astype(F32)
    output_o[...] = residual + ffn
    squares = squares + jnp.where(spot == 2, full_sum(ffn * ffn), 0.0)
    part_o[3:4] = squares
    gq_copy.wait_recv()
    for a in range(group):
        gq_o[a] = (o64[a, c] + o_in[a]).astype(BF16)
    gather_lat.next(2)
    gather_cot.finish(3)
    gather_lat.finish(3)
    gather_att.finish_c()
    gather_mid.finish(0)
    for gather in (gather_cot, gather_lat, gather_mid):
        gather.drain()
    gather_att.drain_c()
    own_store.wait()
    wq_store.wait()
    hat_store.wait()
    for a in range(group):
        gkv_store(a).wait()
    for relay in relays + o_relays:
        relay.drain()
    for copy in (q_copy, att_copy, g_copy, gq_copy, wq_copy):
        copy.wait_send()
    for copies in (cot_copies, mid_copies, gmid_copies, ffn_copies, lat_copies, back_copies):
        for copy in copies:
            copy.wait_send()


def front(nx, ny, counts, latents, cot, gain_m, gain_l, gain_f, media, qkv, out_w, up, down):
    group = 2 * ny
    media_rows, feat = media.shape
    lat = latents.shape[0]
    rows = media_rows + lat
    cols = qkv.shape[-1]
    ff = up.shape[1]
    aligned = cols % 128 == 0
    tall = cols // HEAD * 2 * lat
    any_ = pl.BlockSpec(memory_space=pl.ANY)
    vm = pl.BlockSpec(memory_space=pltpu.VMEM)
    S = jax.ShapeDtypeStruct
    V = pltpu.VMEM
    D = pltpu.SemaphoreType.DMA
    every = (NZ, nx, ny, 2, lat)
    n_w = 4
    n_o = 2 if nx == 2 else 1
    half = (n_w, nx, 2, feat // (2 * nx * n_w))
    o_part = (n_o, nx, cols // (nx * n_o), feat)
    if aligned:
        wkv = qkv.reshape((3,) + half + (cols,))
    else:
        wkv = jnp.concatenate([qkv[1], qkv[2]], axis=-1).reshape(half + (2 * cols,))
    spread4 = NZ + nx + ny + 2 - 4
    slots = Relay.slots(nx, ny)
    outs = (
        S((rows, feat), BF16),
        S((group, rows, 2 * cols), BF16),
        S((ny, 2) + half + (2 * cols,), BF16),
        S((2, feat, cols), BF16),
        S((ny, 2) + o_part, BF16),
        S(every + (feat,), BF16),
        S(every + (feat,), BF16),
        S(every + (cols,), BF16),
        S(every + (feat,), BF16),
        S((lat, feat), BF16),
        S((group, lat, cols), BF16),
        S((lat, feat), F32),
        S((lat, feat), F32),
        S((8, feat), F32),
    )
    return pl.pallas_call(
        functools.partial(front_kernel, nx, ny, aligned),
        out_shape=outs,
        in_specs=[pl.BlockSpec(memory_space=pltpu.SMEM)] + [vm] * 5 + [any_] * 6,
        out_specs=(any_,) * 9 + (vm,) * 5,
        scratch_shapes=[
            V((rows, feat), BF16),
            V((group, rows, 2 * cols), BF16),
            V(half + (2 * cols,), BF16),
            V((2,) + half + (2 * cols,), BF16),
            V((2, feat, cols), BF16),
            V((group,) + o_part, BF16),
            V(up.shape, BF16),
            V(down.shape, BF16),
            V((2, 256, feat), BF16),
            V((ny, lat, feat), BF16),
            V((ny, 2, lat, cols), BF16),
            V((group, 2, lat, cols), BF16),
            V((group, tall, rows), F32),
            V((group, tall, rows), BF16),
            V((group, tall, 128), F32),
            V((group, tall, 128), F32),
            V((group, 2, lat, cols), F32),
            V((group, lat, cols), F32),
            V((group, 2, lat, cols), F32),
            V((group, lat, cols), BF16),
            V((ny, 2, lat, cols), BF16),
            V((group, 2, lat, cols), BF16),
            V((ny, 2, lat, feat), BF16),
            V((group, lat, feat), BF16),
            V((group * lat, ff), BF16),
            V((group * lat, ff), BF16),
            V((group * lat, ff), F32),
            V((2, group, lat, feat), BF16),
            V((2, group - 1, lat, feat), BF16),
            D((6 + group,)),
            D((2,)),
            D((2,)),
            D((3,)),
            D((n_w, slots)),
            D((n_w, slots)),
            D((n_o, slots)),
            D((n_o, slots)),
            D((2, ny - 1)),
            D((2, ny - 1)),
            D((6,)),
            D((6,)),
            D((group,)),
            D((group,)),
            D((4, group - 1)),
            D((4, group - 1)),
            D((spread4,)),
            D((spread4,)),
            D((spread4,)),
            D((spread4,)),
            D((ColumnGather.slots(nx, ny),)),
            D((ColumnGather.slots(nx, ny),)),
            D((NZ - 1,)),
            D((NZ - 1,)),
            D((5,)),
        ],
        compiler_params=pltpu.CompilerParams(
            collective_id=2, has_side_effects=True, vmem_limit_bytes=67043328
        ),
        name="front",
    )(
        counts,
        latents,
        cot,
        gain_m,
        gain_l,
        gain_f,
        media,
        wkv,
        qkv.reshape(3, feat, cols),
        out_w.reshape(o_part),
        up,
        down,
    )


def shards(
    media_tokens,
    latents,
    frame_counts,
    gain_media,
    gain_latent,
    gain_ffn,
    qkv_weight,
    out_weight,
    up_weight,
    down_weight,
    cotangent,
):
    group = lax.axis_size("ha")
    width = media_tokens.shape[1]
    lat = latents.shape[0]
    cols = qkv_weight.shape[2]
    entry_total = float(lat * width * lax.axis_size("sa") * group)
    nx, ny = lax.axis_size("sa") // NZ, group // 2
    gains_in = (gain_media, gain_latent, gain_ffn)
    (
        hat,
        gkv,
        wkv_all,
        wq_pair,
        unused,
        cot_all,
        lat_all,
        att_all,
        mid_all,
        grad_branch,
        grad_q,
        grad_residual,
        output,
        parts,
    ) = front(
        nx,
        ny,
        frame_counts,
        latents,
        cotangent,
        *gains_in,
        media_tokens,
        qkv_weight,
        out_weight,
        up_weight,
        down_weight,
    )
    kv, gm, hid, gp, mid_all, att_all, branch_all, gq_all, gains, grad_latents = tail(
        nx,
        ny,
        hat,
        gkv,
        wkv_all.reshape(group, width, 2 * cols),
        up_weight,
        down_weight,
        media_tokens,
        cot_all,
        wq_pair,
        gains_in[0],
        gains_in[1],
        latents,
        grad_residual,
        grad_q,
        parts,
        grad_branch,
        mid_all,
        att_all,
    )
    cot_all = cot_all.reshape(-1, width)
    lat_all = lat_all.reshape(-1, width)
    kv = kv.reshape(width, 2 * cols)
    hid = hid.reshape(-1, hid.shape[-1])
    gp = gp.reshape(-1, gp.shape[-1])
    mid_all = mid_all.reshape(-1, width)
    branch_all = branch_all.reshape(-1, width)
    att_all = att_all.reshape(-1, cols)
    gq_all = gq_all.reshape(-1, cols)
    args = (hid, gp, mid_all, cot_all, branch_all, lat_all, att_all, gq_all, kv, gm)
    if hid.shape[0] <= 1024:
        (
            grad_down,
            grad_up,
            grad_out,
            grad_qkv,
            grad_media,
            output,
            grad_latents,
            gain_one,
            gain_two,
            gain_three,
        ) = post(*args, output, grad_latents, gains)
    else:
        grad_media = gm.astype(F32)
        grad_out = dot("rc,rd->cd", att_all, branch_all)
        grad_wq = dot("rd,re->de", lat_all, gq_all)
        grad_down = dot("rf,rd->fd", hid, cot_all)
        grad_up = dot("rd,rf->df", mid_all, gp)
        grad_kv = jnp.stack([kv[:, :cols], kv[:, cols:]]).astype(F32)
        grad_qkv = jnp.concatenate([grad_wq[None], grad_kv], axis=0)
        gain_one, gain_two, gain_three = gains[0], gains[1], gains[2]
    square_sums = gains[3, :3]
    roots = jnp.sqrt(square_sums / entry_total)
    return (
        output,
        grad_media,
        grad_latents,
        gain_one,
        gain_two,
        gain_three,
        grad_qkv,
        grad_out,
        grad_up,
        grad_down,
        roots[0],
        roots[1],
        roots[2],
    )


def solution(mesh):
    placed = (
        P(("sa", "ha"), None),
        P(("sa", "ha"), None),
        P("sa"),
        P(),
        P(),
        P(),
        P(None, None, "ha"),
        P("ha", None),
        P(None, "ha"),
        P("ha", None),
        P(("sa", "ha"), None),
    )
    return jax.shard_map(
        shards,
        mesh=mesh,
        in_specs=placed,
        out_specs=(
            P(("sa", "ha"), None),
            P(("sa", "ha"), None),
            P(("sa", "ha"), None),
            P(),
            P(),
            P(),
            P(None, None, "ha"),
            P("ha", None),
            P(None, "ha"),
            P("ha", None),
            P(),
            P(),
            P(),
        ),
        check_vma=False,
    )
```
